32 devices in a mesh: dp: 4 (over y, x), ctx: 2 (over core), mp: 4 (over z).
Axes of the slice: x: 2, y: 2, z: 4, core: 2. Of those that a mesh axis runs over, the one named last changes fastest.
Arguments:
- inputs: bfloat16 [12, 1024, 1536], P('dp', ('ctx', 'mp')), may hold values from -6 to 6
- w_query: bfloat16 [1536, 1536], P(('dp', 'ctx'), 'mp'), may hold values from -0.21875 to 0.21875
- w_key: bfloat16 [1536, 1536], P(('dp', 'ctx'), 'mp'), may hold values from -0.21875 to 0.21875
- w_value: bfloat16 [1536, 1536], P(('dp', 'ctx'), 'mp'), may hold values from -0.15625 to 0.15625
- w_out: bfloat16 [1536, 1536], P('mp', ('dp', 'ctx')), may hold values from -0.875 to 0.875
- w_up: bfloat16 [1536, 8, 768], P(('dp', 'ctx'), None, 'mp'), may hold values from -0.15625 to 0.15625
- w_down: bfloat16 [8, 768, 1536], P(None, 'mp', ('dp', 'ctx')), may hold values from -0.15625 to 0.15625
- gain_attn: bfloat16 [1536], P(('dp', 'ctx')), may hold values from 0.099609375 to 1.8984375
- gain_ffn: bfloat16 [1536], P(('dp', 'ctx')), may hold values from 0.099609375 to 1.8984375
- cotangent: bfloat16 [12, 1024, 1536], P('dp', ('ctx', 'mp')), may hold values from -6 to 6
Outputs:
- outputs: bfloat16 [12, 1024, 1536], P('dp', ('ctx', 'mp'))
- input_grads: float32 [12, 1024, 1536], P('dp', ('ctx', 'mp'))
- grad_query: float32 [1536, 1536], P(('dp', 'ctx'), 'mp')
- grad_key: float32 [1536, 1536], P(('dp', 'ctx'), 'mp')
- grad_value: float32 [1536, 1536], P(('dp', 'ctx'), 'mp')
- grad_out: float32 [1536, 1536], P('mp', ('dp', 'ctx'))
- grad_up: float32 [1536, 8, 768], P(('dp', 'ctx'), None, 'mp')
- grad_down: float32 [8, 768, 1536], P(None, 'mp', ('dp', 'ctx'))
- grad_gain_attn: float32 [1536], P(('dp', 'ctx'))
- grad_gain_ffn: float32 [1536], P(('dp', 'ctx'))
The draws below stay inside these ranges and needn't reach their ends.
All inputs are finite; a program needn't handle non-finite values.
Results may differ from the reference program's by a relative error of at most 0.015.
Values may be sent and summed in bfloat16 or wider, within the bound.
No kernel may reach another device: no remote copies, remote signals or barrier semaphores. Data moves between devices by JAX's collectives and lax.ppermute only.
A program may use at most 256 MiB of HBM per device.

```python
import jax
import jax.numpy as jnp
from jax import lax

D = 1536
HEADS = 12
HEAD = 128
BLOCK_W = 768
LEN = 1024
INST_DEV = 3
INST = 12
N_DP = 4


def levels(stream_key, shape, shards, low, high):
    gain, own = 1.0, jax.random.fold_in(stream_key, 6)
    for dim, shards_of in shards:
        draws = jnp.exp(jax.random.uniform(jax.random.fold_in(own, dim), (shards_of,), jnp.float32, low / len(shards), high / len(shards)))
        gain = gain * jnp.repeat(draws, shape[dim] // shards_of).reshape([-1 if axis == dim else 1 for axis in range(len(shape))])
    return gain


def scatter_about(key, dims, scale, reach, split=(), held_as=jnp.bfloat16):
    array = jax.random.normal(key, dims, jnp.float32) * scale
    if len(split) > 0:
        array = levels(key, dims, split, -0.22, 0.18) * array
    return jnp.clip(array, min=-reach, max=reach).astype(held_as)


def setup_inputs(seed: int = 0) -> dict:
    keys = jax.random.split(jax.random.key(seed), 11)
    inputs = scatter_about(keys[0], (INST, LEN, D), 1.0, 6.0, ((0, 4), (1, 8)))
    w_query = scatter_about(keys[1], (D, D), (D // 2) ** -0.5, 0.21875, ((0, 8), (1, 4)))
    w_key = scatter_about(keys[2], (D, D), (D // 2) ** -0.5, 0.21875, ((0, 8), (1, 4)))
    w_value = scatter_about(keys[3], (D, D), D ** -0.5, 0.15625, ((0, 8), (1, 4)))
    w_out = scatter_about(keys[4], (D, D), (D // 32) ** -0.5, 0.875, ((0, 4), (1, 8)))
    w_up = scatter_about(keys[5], (D, 8, BLOCK_W), D ** -0.5, 0.15625, ((0, 8), (2, 4)))
    w_down = scatter_about(keys[6], (8, BLOCK_W, D), (2 * BLOCK_W) ** -0.5, 0.15625, ((1, 4), (2, 8)))
    gain_attn = jnp.clip(1.0 + 0.18 * jax.random.normal(keys[7], (D,), jnp.float32), 0.099609375, 1.8984375).astype(jnp.bfloat16)
    gain_ffn = jnp.clip(1.0 + 0.18 * jax.random.normal(keys[8], (D,), jnp.float32), 0.099609375, 1.8984375).astype(jnp.bfloat16)
    cotangent = scatter_about(keys[9], (INST, LEN, D), 1.0, 6.0, ((0, 4), (1, 8)))
    return dict(inputs=inputs, w_query=w_query, w_key=w_key, w_value=w_value, w_out=w_out, w_up=w_up, w_down=w_down, gain_attn=gain_attn, gain_ffn=gain_ffn, cotangent=cotangent)


@jax.custom_vjp
def low(v):
    return lax.optimization_barrier(v.astype(jnp.bfloat16)).astype(jnp.float32)

@jax.custom_vjp
def low_back(v):
    return v

def low_keep(v):
    return (low(v), None)

def low_pass(kept, grad):
    return (grad,)

def back_keep(v):
    return (v, None)

def back_low(kept, grad):
    return (low(grad),)
low.defvjp(low_keep, low_pass)
low_back.defvjp(back_keep, back_low)
EPSILON = 1e-06
NEGATIVE = -1e+30

def normalize(values, gain_vec):
    inv_rms = lax.rsqrt(lax.optimization_barrier(jnp.mean(values * values, axis=-1, keepdims=True)) + EPSILON)
    return values * inv_rms * gain_vec

def rotation(positions, head_size):
    half_size = head_size // 2
    frequency = 10000.0 ** (-jnp.arange(half_size, dtype=jnp.float32) / half_size)
    angles = positions.astype(jnp.float32)[:, None] * frequency[None, :]
    return (jnp.cos(angles)[:, None, :], jnp.sin(angles)[:, None, :])

def rotate(values, cosine, sine_part):
    half_size = values.shape[-1] // 2
    leading = values[..., :half_size]
    trailing = values[..., half_size:]
    return jnp.concatenate([leading * cosine - trailing * sine_part, trailing * cosine + leading * sine_part], axis=-1)

def matmul(left, right):
    return jnp.dot(left, right, precision=lax.Precision.HIGHEST, preferred_element_type=jnp.float32)

def layer(inputs, w_query, w_key, w_value, w_out, w_up, w_down, gain_attn, gain_ffn, blocks):
    length = inputs.shape[0]
    positions = jnp.arange(length, dtype=jnp.int32)
    cosine, sine_part = rotation(positions, HEAD)
    normed_first = low(normalize(inputs, gain_attn))
    query_rows = low(rotate(low_back(matmul(normed_first, w_query)).reshape(length, HEADS, HEAD), cosine, sine_part))
    key_rows = low(rotate(low_back(matmul(normed_first, w_key)).reshape(length, HEADS, HEAD), cosine, sine_part))
    value_rows = low(low_back(matmul(normed_first, w_value))).reshape(length, HEADS, HEAD)
    factor = HEAD ** (-0.5)
    scores = low_back(jnp.einsum('qhd,khd->hqk', query_rows, key_rows, precision=lax.Precision.HIGHEST) * factor)
    causal = positions[:, None] >= positions[None, :]
    masked = jnp.where(causal[None], scores, NEGATIVE)
    softened = jax.nn.softmax(masked, axis=-1)
    mixed = jnp.einsum('hqk,khd->qhd', low(softened), value_rows, precision=lax.Precision.HIGHEST)
    mixed = low(low_back(mixed)).reshape(length, HEADS * HEAD)
    hidden_state = inputs + low_back(matmul(mixed, w_out))
    normed_second = low(normalize(hidden_state, gain_ffn))
    width_used = blocks * BLOCK_W
    upped = low_back(matmul(normed_second, w_up[:, :blocks].reshape(D, width_used)))
    activated = low(jax.nn.gelu(upped, approximate=True))
    return hidden_state + matmul(activated, w_down[:blocks].reshape(width_used, D))

def reference(inputs, w_query, w_key, w_value, w_out, w_up, w_down, gain_attn, gain_ffn, cotangent):
    weights = tuple((weight_arg.astype(jnp.float32) for weight_arg in (w_query, w_key, w_value, w_out, w_up, w_down, gain_attn, gain_ffn)))
    groups = N_DP // 4
    shaped_in = inputs.reshape(groups, 4, INST_DEV, LEN, D)
    shaped_ct = cotangent.reshape(groups, 4, INST_DEV, LEN, D)
    running = tuple((jnp.zeros(weight_arg.shape, jnp.float32) for weight_arg in weights))
    level_outputs = []
    level_grads = []
    for grain_level in range(4):

        def instance_step(totals, bundle, blocks=2 ** grain_level):
            sample, sample_ct = bundle

            def forward(sample_in, *params):
                return layer(sample_in, *params, blocks)
            result, pullback = jax.vjp(forward, sample.astype(jnp.float32), *weights)
            gradients = pullback(sample_ct.astype(jnp.float32))
            totals = tuple((earlier_sum + new_term for earlier_sum, new_term in zip(totals, gradients[1:])))
            return (totals, (result.astype(jnp.bfloat16), gradients[0]))
        level_in = shaped_in[:, grain_level].reshape(groups * INST_DEV, LEN, D)
        level_ct = shaped_ct[:, grain_level].reshape(groups * INST_DEV, LEN, D)
        running, (level_out, level_grad) = lax.scan(instance_step, running, (level_in, level_ct))
        level_outputs.append(level_out.reshape(groups, INST_DEV, LEN, D))
        level_grads.append(level_grad.reshape(groups, INST_DEV, LEN, D))
    outputs = jnp.stack(level_outputs, 1).reshape(INST, LEN, D)
    input_grads = jnp.stack(level_grads, 1).reshape(INST, LEN, D)
    return (outputs, input_grads, running[0], running[1], running[2], running[3], running[4], running[5], running[6], running[7])
```

```python
import jax
import jax.numpy as jnp
from jax import lax
from jax.sharding import PartitionSpec as P

HEAD = 128
LEVELS = 4
EPSILON = 1e-06
NEGATIVE = -1e30
BF = jnp.bfloat16
F32 = jnp.float32


def flip(shard, axis, bit):
    devices = lax.axis_size(axis)
    return lax.ppermute(shard, axis, [(i, i ^ bit) for i in range(devices)])


def turn(shard, axis, by):
    devices = lax.axis_size(axis)
    return lax.ppermute(shard, axis, [(i, (i + by) % devices) for i in range(devices)])


def put(buffer, part, index, dim):
    starts = [0] * buffer.ndim
    starts[dim] = index
    return lax.dynamic_update_slice(buffer, part, tuple(starts))


def take(buffer, index, dim):
    return lax.dynamic_index_in_dim(buffer, index, dim, keepdims=False)


def level_gather(part, mine):
    half = part.shape[0] // 2
    from_x = flip(part, "dp", 1)
    from_y = flip(part, "dp", 2)
    low_half = flip(from_x[:half], "dp", 2)
    high_half = flip(from_y[half:], "dp", 1)
    whole = jnp.zeros((LEVELS,) + part.shape, part.dtype)
    whole = put(whole, part[None], mine, 0)
    whole = put(whole, from_x[None], mine ^ 1, 0)
    whole = put(whole, from_y[None], mine ^ 2, 0)
    rest = jnp.concatenate([low_half, high_half], 0)
    return put(whole, rest[None], mine ^ 3, 0)


def level_scatter(parts, mine):
    half = parts.shape[1] // 2
    own, by_x, by_y, by_xy = (take(parts, mine ^ k, 0) for k in range(LEVELS))
    got_x = flip(jnp.stack([by_x[:half], by_xy[:half]]), "dp", 1)
    got_y = flip(jnp.stack([by_y[half:], by_xy[half:]]), "dp", 2)
    send_y = (by_y[:half].astype(F32) + got_x[1].astype(F32)).astype(parts.dtype)
    send_x = (by_x[half:].astype(F32) + got_y[1].astype(F32)).astype(parts.dtype)
    last_y = flip(send_y, "dp", 2)
    last_x = flip(send_x, "dp", 1)
    first = own[:half].astype(F32) + got_x[0].astype(F32) + last_y.astype(F32)
    second = own[half:].astype(F32) + got_y[0].astype(F32) + last_x.astype(F32)
    return jnp.concatenate([first, second], 0)


def level_swap(parts, mine):
    whole = jnp.zeros(parts.shape, parts.dtype)
    whole = put(whole, take(parts, mine, 0)[None], mine, 0)
    for k in range(1, LEVELS):
        whole = put(whole, flip(take(parts, mine ^ k, 0), "dp", k)[None], mine ^ k, 0)
    return whole


def rank_swap(parts, mine, axis):
    devices = lax.axis_size(axis)
    found = [(mine, take(parts, mine, 0))]
    for k in range(1, devices):
        sent = turn(take(parts, (mine + k) % devices, 0), axis, k)
        found.append(((mine + devices - k) % devices, sent))
    return found


def teams(devices):
    return [list(range(level, devices, LEVELS)) for level in range(LEVELS)]


def team_gather(part):
    devices = lax.axis_size("dp")
    if devices == LEVELS:
        return part[None]
    return lax.all_gather(part, "dp", axis=0, axis_index_groups=teams(devices))


def team_scatter(parts):
    devices = lax.axis_size("dp")
    if devices == LEVELS:
        return parts[0]
    return lax.psum_scatter(
        parts, "dp", scatter_dimension=0, axis_index_groups=teams(devices), tiled=False
    )


def pair_gather(part, mine, dim):
    other = flip(part, "ctx", 1)
    shape = part.shape[:dim] + (2,) + part.shape[dim:]
    whole = jnp.zeros(shape, part.dtype)
    whole = put(whole, jnp.expand_dims(part, dim), mine, dim)
    return put(whole, jnp.expand_dims(other, dim), 1 - mine, dim)


def pair_scatter(parts, mine, dim):
    other = flip(take(parts, 1 - mine, dim), "ctx", 1)
    return take(parts, mine, dim).astype(F32) + other.astype(F32)


def model_gather(part, level, ctx):
    rows, width = part.shape
    whole = team_gather(level_gather(part, level))
    whole = pair_gather(whole.reshape(-1, rows, width), ctx, 1)
    return whole.reshape(-1, width)


def model_scatter(grad, level, ctx, rows):
    width = grad.shape[1]
    parts = grad.reshape(-1, 2, rows, width)
    parts = pair_scatter(parts, ctx, 1).astype(grad.dtype)
    parts = parts.reshape(-1, LEVELS, rows, width)
    parts = team_scatter(parts)
    return level_scatter(parts, level)


def inverse_rms(values):
    return lax.rsqrt(jnp.mean(values * values, axis=-1, keepdims=True) + EPSILON)


def norm_back(values, inv_rms, weighted):
    return inv_rms * weighted - values * (inv_rms * inv_rms * inv_rms) * jnp.mean(
        weighted * values, axis=-1, keepdims=True
    )


def rotation(positions, head_size):
    half_size = head_size // 2
    frequency = 10000.0 ** (-jnp.arange(half_size, dtype=jnp.float32) / half_size)
    angles = positions.astype(jnp.float32)[:, None] * frequency[None, :]
    return (jnp.cos(angles)[:, None, :], jnp.sin(angles)[:, None, :])


def rotate(values, cosine, sine_part):
    half_size = values.shape[-1] // 2
    leading = values[..., :half_size]
    trailing = values[..., half_size:]
    return jnp.concatenate(
        [leading * cosine - trailing * sine_part, trailing * cosine + leading * sine_part], axis=-1
    )


def gelu_tanh(values):
    return jax.nn.gelu(values, approximate=True)


def product(equation, left, right):
    return jnp.einsum(equation, left, right, preferred_element_type=F32)


def local(inputs, w_query, w_key, w_value, w_out, w_up, w_down, gain_attn, gain_ffn, cotangent):
    count, shard_len, width = inputs.shape
    own_rows = count * shard_len
    ranks = lax.axis_size("mp")
    length_half = shard_len * ranks
    total_rows = count * length_half
    level = lax.axis_index("dp") % LEVELS
    ctx = lax.axis_index("ctx")
    rank = lax.axis_index("mp")
    part_rows, head_cols = w_query.shape
    head_count = head_cols // HEAD
    factor = HEAD ** (-0.5)
    gain_a = gain_attn.astype(F32)[:, None]
    gain_f = gain_ffn.astype(F32)[:, None]

    inputs_f = inputs.astype(F32)
    inv_first = inverse_rms(inputs_f)
    unit_first = (inputs_f * inv_first).astype(BF)
    rows_first = lax.all_gather(unit_first, "mp", axis=1, tiled=True).reshape(total_rows, width)

    scaled = jnp.concatenate(
        [(gain_a * w.astype(F32)).astype(BF) for w in (w_query, w_key, w_value)], axis=1
    )
    qkv_full = model_gather(scaled, level, ctx)
    out_cols = jnp.zeros((part_rows, ranks * head_cols), BF)
    out_turned = w_out.T
    out_cols = put(out_cols, out_turned, rank * head_cols, 1)
    for k in range(1, ranks):
        out_cols = put(
            out_cols, turn(out_turned, "mp", k), (rank + ranks - k) % ranks * head_cols, 1
        )
    out_full = model_gather(out_cols, level, ctx)

    cot_rows = level_gather(cotangent.reshape(own_rows, width), level)

    blocks = w_up.shape[1]
    unit_cols = w_up.shape[2]
    sub = unit_cols // LEVELS
    half_blocks = blocks // 2
    up_turned = (gain_f[:, :, None] * w_up.astype(F32)).astype(BF).transpose(1, 2, 0)
    both = jnp.stack([up_turned, w_down])
    both = both.reshape(2, 2, half_blocks, unit_cols, part_rows)
    sent_ctx = flip(take(both, 1 - ctx, 1), "ctx", 1)
    kept = take(both, ctx, 1)
    pair = jnp.zeros((2, half_blocks, unit_cols, 2, part_rows), BF)
    pair = put(pair, kept[:, :, :, None], ctx, 3)
    pair = put(pair, sent_ctx[:, :, :, None], 1 - ctx, 3)
    pair = pair.reshape(2, half_blocks, LEVELS, sub, 2 * part_rows).transpose(2, 0, 1, 3, 4)
    swapped = team_gather(level_swap(pair, level))
    swapped = swapped.transpose(2, 3, 4, 0, 1, 5).reshape(2, half_blocks, sub, width)
    ranked = lax.all_gather(swapped, "mp", axis=2)
    ranked = ranked.reshape(2, half_blocks, ranks * sub, width)
    whole = pair_gather(ranked, ctx, 1).reshape(2, blocks * unit_cols, width)
    up_mine, down_mine = whole[0], whole[1]

    positions = ctx * length_half + jnp.arange(length_half, dtype=jnp.int32)
    cosine, sine_part = rotation(positions, HEAD)
    projected = product("rd,dc->rc", rows_first, qkv_full).reshape(
        count, length_half, 3, head_count, HEAD
    )
    query_rows = rotate(projected[:, :, 0], cosine, sine_part).astype(BF)
    key_rows = rotate(projected[:, :, 1], cosine, sine_part).astype(BF)
    value_rows = projected[:, :, 2].astype(BF)
    early = [(0, 1)]
    early_keys, early_values = lax.ppermute((key_rows, value_rows), "ctx", early)
    row_ids = jnp.arange(length_half)[:, None]
    col_ids = jnp.arange(2 * length_half)[None, :]
    visible = jnp.where(col_ids < length_half, ctx >= 1, col_ids - length_half <= row_ids)

    def scores_of(query_one, keys_all):
        raw_scores = product("qhd,khd->hqk", query_one, keys_all) * factor
        return jnp.where(visible[None], raw_scores, NEGATIVE)

    def attend(package):
        query_one, key_one, value_one, key_early, value_early = package
        keys_all = jnp.concatenate([key_early, key_one], 0)
        values_all = jnp.concatenate([value_early, value_one], 0)
        scores = scores_of(query_one, keys_all)
        largest = jnp.max(scores, axis=-1, keepdims=True)
        exponent = jnp.exp(scores - largest)
        totals = jnp.sum(exponent, axis=-1, keepdims=True)
        softened = exponent / totals
        mixed_one = product("hqk,khd->qhd", softened.astype(BF), values_all)
        return (mixed_one.astype(BF), (largest + jnp.log(totals))[..., 0])

    mixed_rows, log_totals = lax.map(
        attend, (query_rows, key_rows, value_rows, early_keys, early_values)
    )
    mixed_parts = mixed_rows.reshape(count, ranks, shard_len, head_cols).transpose(1, 0, 2, 3)
    mixed_own = jnp.zeros((own_rows, ranks * head_cols), BF)
    for source, found in rank_swap(mixed_parts, rank, "mp"):
        mixed_own = put(mixed_own, found.reshape(own_rows, head_cols), source * head_cols, 1)
    attended = product("rc,dc->rd", mixed_own, out_full)
    hidden = inputs_f.reshape(own_rows, width) + attended
    inv_second = inverse_rms(hidden)
    unit_second = (hidden * inv_second).astype(BF)

    rows_second = level_gather(unit_second, level)
    results, grads_in, activated_all, grad_up_all = [], [], [], []
    for one in range(LEVELS):
        used = 2**one * unit_cols
        upped = product("rd,hd->rh", rows_second[one], up_mine[:used])
        activated, gelu_pull = jax.vjp(gelu_tanh, upped)
        activated = activated.astype(BF)
        grad_act = product("rd,hd->rh", cot_rows[one], down_mine[:used])
        grad_upped = gelu_pull(grad_act)[0].astype(BF)
        grads_in.append(product("rh,hd->rd", grad_upped, up_mine[:used]).astype(BF))
        results.append(product("rh,hd->rd", activated, down_mine[:used]).astype(BF))
        activated_all.append(activated)
        grad_up_all.append(grad_upped)

    grad_second = level_scatter(jnp.stack(grads_in), level)
    result = level_scatter(jnp.stack(results), level)
    outputs = (hidden + result).astype(BF).reshape(inputs.shape)
    grad_hidden = cotangent.astype(F32).reshape(own_rows, width) + norm_back(
        hidden, inv_second, grad_second
    )

    def block_grads(left_all, right):
        pieces = []
        for one in range(LEVELS):
            first = 0 if one == 0 else 2 ** (one - 1) * unit_cols
            last = 2**one * unit_cols
            left = jnp.concatenate([left_all[k][:, first:last] for k in range(one, LEVELS)], 0)
            pieces.append(product("rh,rd->hd", left, right[one:].reshape(-1, width)).astype(BF))
        return jnp.concatenate(pieces, 0)

    grad_ffn = jnp.stack(
        [block_grads(grad_up_all, rows_second), block_grads(activated_all, cot_rows)]
    )
    grad_ffn = pair_scatter(grad_ffn.reshape(2, 2, half_blocks * unit_cols, width), ctx, 1)
    grad_ffn = grad_ffn.astype(BF).reshape(2, half_blocks, ranks, sub, width)
    grad_ffn = lax.psum_scatter(grad_ffn, "mp", scatter_dimension=2, tiled=True)
    grad_ffn = grad_ffn.reshape(2, half_blocks, sub, -1, LEVELS, 2 * part_rows)
    grad_ffn = team_scatter(grad_ffn.transpose(3, 4, 0, 1, 2, 5))
    grad_ffn = level_swap(grad_ffn, level).transpose(1, 2, 0, 3, 4)
    grad_ffn = grad_ffn.reshape(2, half_blocks, unit_cols, 2, part_rows)
    sent_ctx = flip(take(grad_ffn, 1 - ctx, 3), "ctx", 1)
    own_ffn = jnp.zeros((2, 2, half_blocks, unit_cols, part_rows), BF)
    own_ffn = put(own_ffn, take(grad_ffn, ctx, 3)[:, None], ctx, 1)
    own_ffn = put(own_ffn, sent_ctx[:, None], 1 - ctx, 1)
    own_ffn = own_ffn.reshape(2, blocks, unit_cols, part_rows).astype(F32)
    grad_up_unit = own_ffn[0].transpose(2, 0, 1)
    grad_up_out = gain_f[:, :, None] * grad_up_unit
    grad_down_out = own_ffn[1]
    gain_ffn_part = jnp.sum(grad_up_unit * w_up.astype(F32), axis=(1, 2))

    grad_low = grad_hidden.astype(BF)
    grad_mixed_own = product("rd,dc->rc", grad_low, out_full).astype(BF)
    grad_parts = grad_mixed_own.reshape(count, shard_len, ranks, head_cols).transpose(2, 0, 1, 3)
    grad_mixed = jnp.zeros((count, ranks, shard_len, head_cols), BF)
    for source, found in rank_swap(grad_parts, rank, "mp"):
        grad_mixed = put(grad_mixed, found[:, None], source, 1)
    grad_mixed = grad_mixed.reshape(count, length_half, head_count, HEAD)
    grad_out_w = product("rd,rc->dc", grad_low, mixed_own).astype(BF)
    grad_out_w = model_scatter(grad_out_w, level, ctx, part_rows).astype(BF)
    grad_out_parts = grad_out_w.reshape(part_rows, ranks, head_cols).transpose(1, 0, 2)
    grad_out_out = 0.0
    for _, found in rank_swap(grad_out_parts, rank, "mp"):
        grad_out_out = grad_out_out + found.astype(F32)
    grad_out_out = grad_out_out.T

    def attend_back(package):
        query_one, key_one, value_one, key_early, value_early, log_one, grad_one = package
        keys_all = jnp.concatenate([key_early, key_one], 0)
        values_all = jnp.concatenate([value_early, value_one], 0)
        scores = scores_of(query_one, keys_all)
        softened = jnp.exp(scores - log_one[..., None])
        grad_soft = product("qhd,khd->hqk", grad_one, values_all)
        grad_values = product("hqk,qhd->khd", softened.astype(BF), grad_one)
        inner = jnp.sum(grad_soft * softened, axis=-1, keepdims=True)
        grad_scores = (softened * (grad_soft - inner)).astype(BF)
        grad_queries = product("hqk,khd->qhd", grad_scores, keys_all) * factor
        grad_keys = product("hqk,qhd->khd", grad_scores, query_one) * factor
        return (
            grad_queries,
            grad_keys[length_half:],
            grad_keys[:length_half].astype(BF),
            grad_values[length_half:],
            grad_values[:length_half].astype(BF),
        )

    grad_queries, grad_key_own, grad_key_early, grad_value_own, grad_value_early = lax.map(
        attend_back,
        (query_rows, key_rows, value_rows, early_keys, early_values, log_totals, grad_mixed),
    )
    key_back, value_back = lax.ppermute((grad_key_early, grad_value_early), "ctx", [(1, 0)])
    grad_query_low = rotate(grad_queries, cosine, -sine_part).astype(BF)
    grad_key_low = rotate(grad_key_own + key_back.astype(F32), cosine, -sine_part).astype(BF)
    grad_value_low = (grad_value_own + value_back.astype(F32)).astype(BF)
    grad_qkv = jnp.concatenate(
        [g.reshape(total_rows, head_cols) for g in (grad_query_low, grad_key_low, grad_value_low)],
        axis=1,
    )
    grad_first = product("rc,dc->rd", grad_qkv, qkv_full).astype(BF)
    grad_first = lax.psum_scatter(
        grad_first.reshape(count, length_half, width), "mp", scatter_dimension=1, tiled=True
    )
    input_grads = grad_hidden.reshape(inputs.shape) + norm_back(
        inputs_f, inv_first, grad_first.astype(F32)
    )
    grad_qkv_w = product("rd,rc->dc", rows_first, grad_qkv).astype(BF)
    grad_qkv_w = model_scatter(grad_qkv_w, level, ctx, part_rows)
    originals = jnp.concatenate([w.astype(F32) for w in (w_query, w_key, w_value)], axis=1)
    gain_attn_part = jnp.sum(grad_qkv_w * originals, axis=1)
    grad_qkv_out = gain_a * grad_qkv_w
    gains = lax.psum(jnp.stack([gain_attn_part, gain_ffn_part]), "mp")
    return (
        outputs,
        input_grads,
        grad_qkv_out[:, :head_cols],
        grad_qkv_out[:, head_cols : 2 * head_cols],
        grad_qkv_out[:, 2 * head_cols :],
        grad_out_out,
        grad_up_out,
        grad_down_out,
        gains[0],
        gains[1],
    )


def solution(mesh):
    in_specs = (
        P("dp", ("ctx", "mp"), None),
        P(("dp", "ctx"), "mp"),
        P(("dp", "ctx"), "mp"),
        P(("dp", "ctx"), "mp"),
        P("mp", ("dp", "ctx")),
        P(("dp", "ctx"), None, "mp"),
        P(None, "mp", ("dp", "ctx")),
        P(("dp", "ctx")),
        P(("dp", "ctx")),
        P("dp", ("ctx", "mp"), None),
    )
    out_specs = (
        P("dp", ("ctx", "mp"), None),
        P("dp", ("ctx", "mp"), None),
        P(("dp", "ctx"), "mp"),
        P(("dp", "ctx"), "mp"),
        P(("dp", "ctx"), "mp"),
        P("mp", ("dp", "ctx")),
        P(("dp", "ctx"), None, "mp"),
        P(None, "mp", ("dp", "ctx")),
        P(("dp", "ctx")),
        P(("dp", "ctx")),
    )
    return jax.shard_map(local, mesh=mesh, in_specs=in_specs, out_specs=out_specs, check_vma=False)
```

```python
import functools

import jax
import jax.numpy as jnp
from jax import lax
from jax.experimental import pallas as pl
from jax.experimental.pallas import tpu as pltpu
from jax.sharding import PartitionSpec as P

HEAD = 128
LEVELS = 4
EPSILON = 1e-06
NEGATIVE = -1e30
BF = jnp.bfloat16
F32 = jnp.float32
MIB = 1 << 20


def flip(shard, axis, bit):
    devices = lax.axis_size(axis)
    return lax.ppermute(shard, axis, [(i, i ^ bit) for i in range(devices)])


def turn(shard, axis, by):
    devices = lax.axis_size(axis)
    return lax.ppermute(shard, axis, [(i, (i + by) % devices) for i in range(devices)])


def after(values, *others):
    return lax.optimization_barrier((values,) + others)[0]


def put(buffer, part, index, dim=0):
    starts = [0] * buffer.ndim
    starts[dim] = index
    return lax.dynamic_update_slice(buffer, jnp.expand_dims(part, dim), tuple(starts))


def take(buffer, index, dim=0):
    return lax.dynamic_index_in_dim(buffer, index, dim, keepdims=False)


def side_by_side(parts):
    return jnp.concatenate([parts[k] for k in range(parts.shape[0])], axis=-1)


def pack(part, width):
    rows, cols = part.shape
    return side_by_side(part.reshape(width // cols, -1, cols))


def unpack(packed, cols):
    strips = packed.shape[1] // cols
    return jnp.concatenate([packed[:, k * cols : (k + 1) * cols] for k in range(strips)], 0)


def line_gather(part):
    ranks, rank = lax.axis_size("mp"), lax.axis_index("mp")
    upward, downward = [], []
    up = down = part
    for k in range(1, ranks):
        up = lax.ppermute(up, "mp", [(i, i + 1) for i in range(k - 1, ranks - 1)])
        down = lax.ppermute(down, "mp", [(i, i - 1) for i in range(1, ranks - k + 1)])
        upward.append(up)
        downward.append(down)
    whole = jnp.zeros((ranks,) + part.shape, part.dtype)
    for k in range(ranks - 1, 0, -1):
        whole = put(whole, upward[k - 1], jnp.maximum(rank - k, 0))
        whole = put(whole, downward[k - 1], jnp.minimum(rank + k, ranks - 1))
    return put(whole, part, rank)


def line_scatter(parts):
    ranks, rank = lax.axis_size("mp"), lax.axis_index("mp")
    up = down = None
    for k in range(1, ranks):
        send_up = take(parts, jnp.minimum(rank + ranks - k, ranks - 1))
        send_down = take(parts, jnp.maximum(rank + k - ranks, 0))
        if up is not None:
            send_up = (send_up.astype(F32) + up.astype(F32)).astype(parts.dtype)
            send_down = (send_down.astype(F32) + down.astype(F32)).astype(parts.dtype)
        up = lax.ppermute(send_up, "mp", [(i, i + 1) for i in range(k)])
        down = lax.ppermute(send_down, "mp", [(i, i - 1) for i in range(ranks - k, ranks)])
    return take(parts, rank).astype(F32) + up.astype(F32) + down.astype(F32)


def rank_swap(parts):
    ranks, rank = lax.axis_size("mp"), lax.axis_index("mp")
    found = [turn(take(parts, (rank + k) % ranks), "mp", k) for k in range(1, ranks)]
    whole = put(jnp.zeros(parts.shape, parts.dtype), take(parts, rank), rank)
    for k in range(1, ranks):
        whole = put(whole, found[k - 1], (rank + ranks - k) % ranks)
    return whole


def level_gather(part, mine):
    half = part.shape[0] // 2
    from_x = flip(part, "dp", 1)
    from_y = flip(part, "dp", 2)
    low_half = flip(from_x[:half], "dp", 2)
    high_half = flip(from_y[half:], "dp", 1)
    whole = put(jnp.zeros((LEVELS,) + part.shape, part.dtype), part, mine)
    whole = put(whole, from_x, mine ^ 1)
    whole = put(whole, from_y, mine ^ 2)
    return put(whole, jnp.concatenate([low_half, high_half], 0), mine ^ 3)


def level_gather_small(part, mine):
    whole = put(jnp.zeros((LEVELS,) + part.shape, part.dtype), part, mine)
    for k in range(1, LEVELS):
        whole = put(whole, flip(part, "dp", k), mine ^ k)
    return whole


def level_scatter_open(parts, mine):
    half = parts.shape[1] // 2
    own, by_x, by_y, by_xy = (take(parts, mine ^ k) for k in range(LEVELS))
    got_x = flip(jnp.stack([by_x[:half], by_xy[:half]]), "dp", 1)
    got_y = flip(jnp.stack([by_y[half:], by_xy[half:]]), "dp", 2)
    return own, by_x[half:], by_y[:half], got_x, got_y


def level_scatter_close(own, by_x, by_y, got_x, got_y):
    half = by_y.shape[0]
    send_y = (by_y.astype(F32) + got_x[1].astype(F32)).astype(own.dtype)
    send_x = (by_x.astype(F32) + got_y[1].astype(F32)).astype(own.dtype)
    last_y = flip(send_y, "dp", 2)
    last_x = flip(send_x, "dp", 1)
    first = own[:half].astype(F32) + got_x[0].astype(F32) + last_y.astype(F32)
    second = own[half:].astype(F32) + got_y[0].astype(F32) + last_x.astype(F32)
    return jnp.concatenate([first, second], 0)


def level_scatter(parts, mine):
    return level_scatter_close(*level_scatter_open(parts, mine))


def level_swap(parts, mine):
    whole = put(jnp.zeros(parts.shape, parts.dtype), take(parts, mine), mine)
    for k in range(1, LEVELS):
        whole = put(whole, flip(take(parts, mine ^ k), "dp", k), mine ^ k)
    return whole


def teams(devices):
    return [list(range(level, devices, LEVELS)) for level in range(LEVELS)]


def team_gather(part):
    devices = lax.axis_size("dp")
    if devices == LEVELS:
        return part[None]
    return lax.all_gather(part, "dp", axis=0, axis_index_groups=teams(devices))


def team_scatter(parts):
    devices = lax.axis_size("dp")
    if devices == LEVELS:
        return parts[0]
    return lax.psum_scatter(
        parts, "dp", scatter_dimension=0, axis_index_groups=teams(devices), tiled=False
    )


def pair_gather(part, mine, dim=0):
    other = flip(part, "ctx", 1)
    shape = part.shape[:dim] + (2,) + part.shape[dim:]
    return put(put(jnp.zeros(shape, part.dtype), part, mine, dim), other, 1 - mine, dim)


def pair_split(first, second, mine):
    own = jnp.where(mine == 0, first, second)
    return own, flip(jnp.where(mine == 0, second, first), "ctx", 1)


def pair_scatter(parts, mine, dim):
    other = flip(take(parts, 1 - mine, dim), "ctx", 1)
    return take(parts, mine, dim).astype(F32) + other.astype(F32)


def model_gather(part, level, ctx):
    rows, width = part.shape
    whole = team_gather(level_gather(part, level))
    whole = pair_gather(whole.reshape(-1, rows, width), ctx, 1)
    return whole.reshape(-1, width)


def model_scatter(grad, level, ctx, rows):
    width = grad.shape[1]
    parts = grad.reshape(-1, 2, rows, width)
    parts = pair_scatter(parts, ctx, 1).astype(grad.dtype)
    parts = team_scatter(parts.reshape(-1, LEVELS, rows, width))
    return level_scatter(parts, level)


def contract(left, right, left_dim, right_dim):
    return lax.dot_general(
        left, right, (((left_dim,), (right_dim,)), ((), ())), preferred_element_type=F32
    )


def turned(values, cosine, sine):
    return values * cosine + pltpu.roll(values, HEAD // 2, 1) * sine


def project_kernel(rows_ref, gain_ref, weight_ref, cos_ref, sin_ref, out_ref, normed_ref):
    @pl.when(pl.program_id(0) == 0)
    def _():
        values = rows_ref[...].reshape(normed_ref.shape).astype(F32)
        inv = lax.rsqrt(jnp.mean(values * values, axis=-1, keepdims=True) + EPSILON)
        normed_ref[...] = (values * inv * gain_ref[...]).astype(BF)

    values = contract(normed_ref[...], weight_ref[...], 1, 0)
    cosine, sine = cos_ref[0], sin_ref[0]
    for head in range(values.shape[1] // HEAD):
        cols = slice(head * HEAD, (head + 1) * HEAD)
        out_ref[0, :, cols] = turned(values[:, cols], cosine, sine).astype(BF)


def project(which, shard_len, rows, gain, weight, cosine, sine):
    ranks, _, width = rows.shape
    length = ranks * shard_len
    cols = weight.shape[1] // 3
    table = pl.BlockSpec((1, length, HEAD), lambda j: (j // 2, 0, 0))
    return pl.pallas_call(
        project_kernel,
        grid=(3,),
        in_specs=[
            pl.BlockSpec((ranks, shard_len, width), lambda j: (0, which, 0)),
            pl.BlockSpec((1, width), lambda j: (0, 0)),
            pl.BlockSpec((width, cols), lambda j: (0, j)),
            table,
            table,
        ],
        out_specs=[
            pl.BlockSpec((1, length, cols), lambda j: (j, 0, 0)),
            pl.BlockSpec((length, width), lambda j: (0, 0)),
        ],
        out_shape=[
            jax.ShapeDtypeStruct((3, length, cols), BF),
            jax.ShapeDtypeStruct((length, width), BF),
        ],
        compiler_params=pltpu.CompilerParams(vmem_limit_bytes=24 * MIB),
        cost_estimate=pl.CostEstimate(
            flops=6 * length * width * cols,
            bytes_accessed=4 * length * width + 6 * width * cols + 6 * length * cols,
            transcendentals=0,
        ),
        name="project",
    )(rows, gain, weight, cosine, sine)


def softmax_parts(query, key_own, key_early, first, late):
    factor = HEAD ** (-0.5)
    own = contract(query, key_own, 1, 1) * factor
    row_ids = first + lax.broadcasted_iota(jnp.int32, own.shape, 0)
    col_ids = lax.broadcasted_iota(jnp.int32, own.shape, 1)
    own = jnp.where(col_ids <= row_ids, own, NEGATIVE)
    early = contract(query, key_early, 1, 1) * factor if late else None
    return own, early


def attend_kernel(strip, ctx_ref, query_ref, key_ref, value_ref, early_ref, mixed_ref, log_ref):
    length = query_ref.shape[1]

    def run(late):
        for first in range(0, length, strip):
            end = first + strip
            own, early = softmax_parts(
                query_ref[0, first:end], key_ref[0, :end], early_ref[0], first, late
            )
            largest = jnp.max(own, axis=-1, keepdims=True)
            if late:
                largest = jnp.maximum(largest, jnp.max(early, axis=-1, keepdims=True))
            own = jnp.exp(own - largest)
            total = jnp.sum(own, axis=-1, keepdims=True)
            if late:
                early = jnp.exp(early - largest)
                total = total + jnp.sum(early, axis=-1, keepdims=True)
            inverse = 1.0 / total
            mixed = contract((own * inverse).astype(BF), value_ref[0, :end], 1, 0)
            if late:
                mixed = mixed + contract((early * inverse).astype(BF), early_ref[1], 1, 0)
            mixed_ref[first:end] = mixed.astype(BF)
            log_ref[0, first:end] = largest + jnp.log(total)

    @pl.when(ctx_ref[0] == 0)
    def _():
        run(False)

    @pl.when(ctx_ref[0] != 0)
    def _():
        run(True)


def attend(ctx_flag, qkv, early):
    _, length, cols = qkv.shape
    heads = cols // HEAD
    one = lambda which: pl.BlockSpec((1, length, HEAD), lambda h, c: (which, 0, h))
    return pl.pallas_call(
        functools.partial(attend_kernel, length // 2),
        grid_spec=pltpu.PrefetchScalarGridSpec(
            num_scalar_prefetch=1,
            grid=(heads,),
            in_specs=[
                one(0),
                one(1),
                one(2),
                pl.BlockSpec((2, length, HEAD), lambda h, c: (0, 0, h)),
            ],
            out_specs=[
                pl.BlockSpec((length, HEAD), lambda h, c: (0, h)),
                pl.BlockSpec((1, length, 1), lambda h, c: (h, 0, 0)),
            ],
        ),
        out_shape=[
            jax.ShapeDtypeStruct((length, cols), BF),
            jax.ShapeDtypeStruct((heads, length, 1), F32),
        ],
        compiler_params=pltpu.CompilerParams(vmem_limit_bytes=24 * MIB),
        cost_estimate=pl.CostEstimate(
            flops=8 * length * length * cols,
            bytes_accessed=14 * length * cols,
            transcendentals=2 * length * length * heads,
        ),
        name="attend",
    )(ctx_flag, qkv, qkv, qkv, early)


def attend_back_kernel(
    strip,
    ctx_ref,
    query_ref,
    key_ref,
    value_ref,
    early_ref,
    log_ref,
    grad_ref,
    cos_ref,
    sin_ref,
    query_out,
    own_out,
    early_out,
):
    length = query_ref.shape[1]
    factor = HEAD ** (-0.5)

    def run(late):
        early_key_sum = early_value_sum = 0.0
        for first in range(length - strip, -1, -strip):
            end = first + strip
            query = query_ref[0, first:end]
            grad = grad_ref[first:end]
            log = log_ref[0, first:end]
            own, early = softmax_parts(query, key_ref[0, :end], early_ref[0], first, late)
            own = jnp.exp(own - log)
            own_grad = contract(grad, value_ref[0, :end], 1, 1)
            inner = jnp.sum(own_grad * own, axis=-1, keepdims=True)
            if late:
                early = jnp.exp(early - log)
                early_grad = contract(grad, early_ref[1], 1, 1)
                inner = inner + jnp.sum(early_grad * early, axis=-1, keepdims=True)
            own_low = (own * (own_grad - inner)).astype(BF)
            grad_query = contract(own_low, key_ref[0, :end], 1, 0)
            grad_key = contract(own_low, query, 0, 0) * factor
            grad_value = contract(own.astype(BF), grad, 0, 0)
            if first == length - strip:
                own_out[0] = grad_key
                own_out[1] = grad_value
            else:
                own_out[0, :end] += grad_key
                own_out[1, :end] += grad_value
            if late:
                early_low = (early * (early_grad - inner)).astype(BF)
                grad_query = grad_query + contract(early_low, early_ref[0], 1, 0)
                early_key_sum = early_key_sum + contract(early_low, query, 0, 0)
                early_value_sum = early_value_sum + contract(early.astype(BF), grad, 0, 0)
            grad_query = grad_query * factor
            query_out[first:end] = turned(
                grad_query, cos_ref[0, first:end], -sin_ref[0, first:end]
            ).astype(BF)
        if late:
            early_out[0] = (early_key_sum * factor).astype(BF)
            early_out[1] = early_value_sum.astype(BF)
        else:
            early_out[...] = jnp.zeros(early_out.shape, BF)

    @pl.when(ctx_ref[0] == 0)
    def _():
        run(False)

    @pl.when(ctx_ref[0] != 0)
    def _():
        run(True)


def attend_back(ctx_flag, qkv, early, logs, grad, cosine, sine):
    _, length, cols = qkv.shape
    heads = cols // HEAD
    one = lambda which: pl.BlockSpec((1, length, HEAD), lambda h, c: (which, 0, h))
    pair = pl.BlockSpec((2, length, HEAD), lambda h, c: (0, 0, h))
    flat = pl.BlockSpec((length, HEAD), lambda h, c: (0, h))
    table = pl.BlockSpec((1, length, HEAD), lambda h, c: (0, 0, 0))
    return pl.pallas_call(
        functools.partial(attend_back_kernel, length // 2),
        grid_spec=pltpu.PrefetchScalarGridSpec(
            num_scalar_prefetch=1,
            grid=(heads,),
            in_specs=[
                one(0),
                one(1),
                one(2),
                pair,
                pl.BlockSpec((1, length, 1), lambda h, c: (h, 0, 0)),
                flat,
                table,
                table,
            ],
            out_specs=[flat, pair, pair],
        ),
        out_shape=[
            jax.ShapeDtypeStruct((length, cols), BF),
            jax.ShapeDtypeStruct((2, length, cols), F32),
            jax.ShapeDtypeStruct((2, length, cols), BF),
        ],
        compiler_params=pltpu.CompilerParams(vmem_limit_bytes=32 * MIB),
        cost_estimate=pl.CostEstimate(
            flops=20 * length * length * cols,
            bytes_accessed=28 * length * cols,
            transcendentals=2 * length * length * heads,
        ),
        name="attend_back",
    )(ctx_flag, qkv, qkv, qkv, early, logs, grad, cosine, sine)


def project_back_kernel(
    query_ref, own_ref, back_ref, cos_ref, sin_ref, weight_ref, low_ref, out_ref
):
    cols = query_ref.shape[1]

    @pl.when(pl.program_id(0) == 0)
    def _():
        low_ref[:, :cols] = query_ref[...]
        keys = own_ref[0] + back_ref[0].astype(F32)
        cosine, sine = cos_ref[0], -sin_ref[0]
        for head in range(cols // HEAD):
            part = slice(head * HEAD, (head + 1) * HEAD)
            into = slice(cols + head * HEAD, cols + (head + 1) * HEAD)
            low_ref[:, into] = turned(keys[:, part], cosine, sine).astype(BF)
        low_ref[:, 2 * cols :] = (own_ref[1] + back_ref[1].astype(F32)).astype(BF)

    out_ref[...] = contract(low_ref[...], weight_ref[...], 1, 1).astype(BF)


def project_back(grad_query, grad_own, back, cosine, sine, weight):
    length, cols = grad_query.shape
    width = weight.shape[0]
    step = width // 3
    whole = lambda shape: pl.BlockSpec(shape, lambda j: (0,) * len(shape))
    return pl.pallas_call(
        project_back_kernel,
        grid=(3,),
        in_specs=[
            whole((length, cols)),
            whole((2, length, cols)),
            whole((2, length, cols)),
            whole((1, length, HEAD)),
            whole((1, length, HEAD)),
            pl.BlockSpec((step, 3 * cols), lambda j: (j, 0)),
        ],
        out_specs=[
            whole((length, 3 * cols)),
            pl.BlockSpec((length, step), lambda j: (0, j)),
        ],
        out_shape=[
            jax.ShapeDtypeStruct((length, 3 * cols), BF),
            jax.ShapeDtypeStruct((length, width), BF),
        ],
        compiler_params=pltpu.CompilerParams(vmem_limit_bytes=24 * MIB),
        cost_estimate=pl.CostEstimate(
            flops=6 * length * width * cols,
            bytes_accessed=6 * width * cols + 18 * length * cols + 2 * length * width,
            transcendentals=0,
        ),
        name="project_back",
    )(grad_query, grad_own, back, cosine, sine, weight)


def gelu_both(values):
    scale = (2.0 / jnp.pi) ** 0.5
    square = values * values
    tanh = jnp.tanh(scale * values * (1.0 + 0.044715 * square))
    half = 0.5 * (1.0 + tanh)
    slope = half + 0.5 * values * (1.0 - tanh * tanh) * scale * (1.0 + 3 * 0.044715 * square)
    return values * half, slope


def feed_kernel(rows_ref, cot_ref, up_ref, down_ref, grad_ref, act_ref, pre_ref, sum_ref):
    step = pl.program_id(0)
    half = up_ref.shape[0]

    def run(used):
        upped = contract(rows_ref[0], up_ref[:used], 1, 1)
        activated, slope = gelu_both(upped)
        grad_act = contract(cot_ref[0], down_ref[:used], 1, 1)
        grad_upped = (grad_act * slope).astype(BF)
        act_ref[0, :, :used] = activated.astype(BF)
        pre_ref[0, :, :used] = grad_upped
        return contract(grad_upped, up_ref[:used], 1, 0)

    for one in range(LEVELS - 1):

        @pl.when(step == one)
        def _(one=one):
            grad_ref[0] = run(half // 2 ** (LEVELS - 2 - one)).astype(BF)

    @pl.when(step == LEVELS - 1)
    def _():
        sum_ref[...] = run(half)

    @pl.when(step == LEVELS)
    def _():
        grad_ref[0] = (sum_ref[...] + run(half)).astype(BF)


def feed(rows, cot, up, down):
    _, length, width = rows.shape
    half = up.shape[0] // 2
    by_level = pl.BlockSpec((1, length, width), lambda s: (jnp.minimum(s, LEVELS - 1), 0, 0))
    by_half = pl.BlockSpec((half, width), lambda s: (s // LEVELS, 0))
    by_step = pl.BlockSpec((1, length, half), lambda s: (s, 0, 0))
    return pl.pallas_call(
        feed_kernel,
        grid=(LEVELS + 1,),
        in_specs=[by_level, by_level, by_half, by_half],
        out_specs=[by_level, by_step, by_step],
        out_shape=[
            jax.ShapeDtypeStruct(rows.shape, BF),
            jax.ShapeDtypeStruct((LEVELS + 1, length, half), BF),
            jax.ShapeDtypeStruct((LEVELS + 1, length, half), BF),
        ],
        scratch_shapes=[pltpu.VMEM((length, width), F32)],
        compiler_params=pltpu.CompilerParams(vmem_limit_bytes=44 * MIB),
        cost_estimate=pl.CostEstimate(
            flops=24 * length * width * half,
            bytes_accessed=24 * length * width + 8 * half * width + 20 * length * half,
            transcendentals=5 * length * half,
        ),
        name="feed",
    )(rows, cot, up, down)


def feed_weights_kernel(
    rows_ref, cot_ref, act_ref, pre_ref, down_ref, grad_ref, out_ref, up_sum, down_sum, out_sum
):
    step = pl.program_id(0)
    half = down_ref.shape[0]
    _, ranks, _, blocks, sub, _ = grad_ref.shape

    def add(used, fresh):
        up_part = contract(pre_ref[0, :, :used], rows_ref[0], 0, 0)
        down_part = contract(act_ref[0, :, :used], cot_ref[0], 0, 0)
        if fresh == used:
            up_sum[:used] = up_part
            down_sum[:used] = down_part
        else:
            up_sum[:fresh] += up_part[:fresh]
            down_sum[:fresh] += down_part[:fresh]
            if fresh < used:
                up_sum[fresh:used] = up_part[fresh:]
                down_sum[fresh:used] = down_part[fresh:]
        return contract(act_ref[0, :, :used], down_ref[:used], 1, 0)

    def store():
        for block in range(blocks):
            for rank in range(ranks):
                first = (block * ranks + rank) * sub
                grad_ref[0, rank, 0, block] = up_sum[first : first + sub].astype(BF)
                grad_ref[0, rank, 1, block] = down_sum[first : first + sub].astype(BF)

    for one in range(LEVELS - 1):

        @pl.when(step == one)
        def _(one=one):
            used = half // 2 ** (LEVELS - 2 - one)
            out_ref[0] = add(used, used if one == 0 else used // 2).astype(BF)

    @pl.when(step == LEVELS - 1)
    def _():
        up_sum[...] += contract(pre_ref[0], rows_ref[0], 0, 0)
        down_sum[...] += contract(act_ref[0], cot_ref[0], 0, 0)
        out_sum[...] = contract(act_ref[0], down_ref[...], 1, 0)
        store()

    @pl.when(step == LEVELS)
    def _():
        out_ref[0] = (out_sum[...] + add(half, half)).astype(BF)
        store()


def feed_weights(rows, cot, activated, before, down, ranks, blocks):
    _, length, width = rows.shape
    half = down.shape[0] // 2
    sub = half // (ranks * blocks)
    by_level = pl.BlockSpec((1, length, width), lambda s: (jnp.minimum(s, LEVELS - 1), 0, 0))
    by_half = pl.BlockSpec((half, width), lambda s: (s // LEVELS, 0))
    by_step = pl.BlockSpec((1, length, half), lambda s: (s, 0, 0))
    shape = (2, ranks, 2, blocks, sub, width)
    return pl.pallas_call(
        feed_weights_kernel,
        grid=(LEVELS + 1,),
        in_specs=[by_level, by_level, by_step, by_step, by_half],
        out_specs=[
            pl.BlockSpec((1,) + shape[1:], lambda s: (s // LEVELS, 0, 0, 0, 0, 0)),
            by_level,
        ],
        out_shape=[jax.ShapeDtypeStruct(shape, BF), jax.ShapeDtypeStruct(rows.shape, BF)],
        scratch_shapes=[
            pltpu.VMEM((half, width), F32),
            pltpu.VMEM((half, width), F32),
            pltpu.VMEM((length, width), F32),
        ],
        compiler_params=pltpu.CompilerParams(vmem_limit_bytes=56 * MIB),
        cost_estimate=pl.CostEstimate(
            flops=24 * length * width * half,
            bytes_accessed=24 * length * width + 12 * half * width + 20 * length * half,
            transcendentals=0,
        ),
        name="feed_weights",
    )(rows, cot, activated, before, down)


def outer_kernel(count, *refs):
    lefts, rights, out_ref = refs[:count], refs[count : 2 * count], refs[-1]
    total = contract(lefts[0][...], rights[0][...], 0, 0)
    for left, right in zip(lefts[1:], rights[1:]):
        total = total + contract(left[...], right[...], 0, 0)
    out_ref[...] = total.astype(BF)


def outer(lefts, rights):
    rows, m = lefts[0].shape
    n = rights[0].shape[1]
    count = len(lefts)
    step = m // 4
    return pl.pallas_call(
        functools.partial(outer_kernel, count),
        grid=(4,),
        in_specs=[pl.BlockSpec((rows, step), lambda j: (0, j))] * count
        + [pl.BlockSpec((rows, n), lambda j: (0, 0))] * count,
        out_specs=pl.BlockSpec((step, n), lambda j: (j, 0)),
        out_shape=jax.ShapeDtypeStruct((m, n), BF),
        compiler_params=pltpu.CompilerParams(vmem_limit_bytes=32 * MIB),
        cost_estimate=pl.CostEstimate(
            flops=2 * count * rows * m * n,
            bytes_accessed=2 * (count * rows * (m + n) + m * n),
            transcendentals=0,
        ),
        name="outer",
    )(*lefts, *rights)


def inverse_rms(values):
    return lax.rsqrt(jnp.mean(values * values, axis=-1, keepdims=True) + EPSILON)


def norm_back(values, inv_rms, weighted):
    return inv_rms * weighted - values * (inv_rms * inv_rms * inv_rms) * jnp.mean(
        weighted * values, axis=-1, keepdims=True
    )


def rotation(positions, head_size):
    half_size = head_size // 2
    frequency = 10000.0 ** (-jnp.arange(half_size, dtype=jnp.float32) / half_size)
    angles = positions.astype(jnp.float32)[:, None] * frequency[None, :]
    cosine, sine = jnp.cos(angles), jnp.sin(angles)
    cosine = jnp.concatenate([cosine, cosine], -1)
    sine = jnp.concatenate([-sine, sine], -1)
    return (
        jnp.stack([cosine, jnp.ones_like(cosine)]),
        jnp.stack([sine, jnp.zeros_like(sine)]),
    )


def product(equation, left, right):
    return jnp.einsum(equation, left, right, preferred_element_type=F32)


def local(inputs, w_query, w_key, w_value, w_out, w_up, w_down, gain_attn, gain_ffn, cotangent):
    count, shard_len, width = inputs.shape
    own_rows = count * shard_len
    ranks = lax.axis_size("mp")
    length_half = shard_len * ranks
    level = lax.axis_index("dp") % LEVELS
    ctx = lax.axis_index("ctx")
    rank = lax.axis_index("mp")
    part_rows, head_cols = w_query.shape
    each = range(count)
    ctx_flag = ctx.astype(jnp.int32)[None]

    out_rows = w_out.size // width
    rows_all = jnp.concatenate([inputs.reshape(own_rows, width), pack(w_out.T, width)], 0)
    rows_all = lax.all_gather(rows_all, "mp", axis=0)

    gains = team_gather(level_gather_small(jnp.stack([gain_attn, gain_ffn]), level))
    gains = pair_gather(gains.reshape(-1, 2, part_rows), ctx, 1)
    gains = gains.transpose(2, 0, 1, 3).reshape(2, 1, width).astype(F32)
    gain_first, gain_second = gains[0], gains[1]

    qkv_full = model_gather(jnp.concatenate([w_query, w_key, w_value], axis=1), level, ctx)
    out_parts = [unpack(rows_all[k, own_rows:], head_cols) for k in range(ranks)]
    out_full = model_gather(jnp.concatenate(out_parts, 1), level, ctx)

    blocks, unit_cols = w_up.shape[1:]
    sub = unit_cols // LEVELS
    half_blocks = blocks // 2
    up_turned = w_up.transpose(1, 2, 0)
    halves = [
        jnp.stack([up_turned[b : b + half_blocks], w_down[b : b + half_blocks]])
        for b in (0, half_blocks)
    ]
    own_part, sent_part = pair_split(halves[0], halves[1], ctx)
    pair = jnp.concatenate(
        [jnp.where(ctx == 0, own_part, sent_part), jnp.where(ctx == 0, sent_part, own_part)], -1
    )
    pair = pair.reshape(2, half_blocks, LEVELS, sub, 2 * part_rows).transpose(2, 0, 1, 3, 4)
    swapped = team_gather(level_swap(pair, level))
    swapped = side_by_side(swapped.reshape(-1, 2, half_blocks, sub, 2 * part_rows))
    cot_rows = level_gather(
        after(cotangent, swapped, qkv_full).reshape(own_rows, width), level
    )
    ranked = lax.all_gather(swapped, "mp", axis=0)
    positions = ctx * length_half + jnp.arange(length_half, dtype=jnp.int32)
    cosine, sine = rotation(positions, HEAD)
    qkv, early, logs, normed_all, mixed_own, hidden, inv_second, rows_second = (
        [] for _ in range(8)
    )
    for i in each:
        qkv_one, normed_one = project(i, shard_len, rows_all, gain_first, qkv_full, cosine, sine)
        early_one = lax.ppermute(qkv_one[1:], "ctx", [(0, 1)])
        mixed_one, log_one = attend(ctx_flag, qkv_one, early_one)
        mixed_one = side_by_side(rank_swap(mixed_one.reshape(ranks, shard_len, head_cols)))
        attended = product("rc,dc->rd", mixed_one, out_full)
        hidden_one = inputs[i].astype(F32) + attended
        inv_one = inverse_rms(hidden_one)
        normed_two = (hidden_one * inv_one * gain_second).astype(BF)
        rows_second.append(level_gather(normed_two, level))
        qkv.append(qkv_one)
        early.append(early_one)
        logs.append(log_one)
        normed_all.append(normed_one)
        mixed_own.append(mixed_one)
        hidden.append(hidden_one)
        inv_second.append(inv_one)

    ranked = after(ranked, hidden[-1])
    ranked = ranked.transpose(1, 2, 0, 3, 4).reshape(2, half_blocks, unit_cols, width)
    up_mine = pair_gather(ranked[0], ctx).reshape(blocks * unit_cols, width)
    down_mine = pair_gather(ranked[1], ctx).reshape(blocks * unit_cols, width)
    rows_second = jnp.concatenate(rows_second, 1)
    grads_in, activated, before = feed(rows_second, cot_rows, up_mine, down_mine)
    grads_in = grads_in.reshape(LEVELS, count, shard_len, width)
    opened = [list(level_scatter_open(grads_in[:, i], level)) for i in each]

    activated = after(activated, *opened[0][3:])
    grad_ffn, results = feed_weights(
        rows_second, cot_rows, activated, before, down_mine, ranks, half_blocks
    )
    grad_ffn = pair_scatter(grad_ffn.reshape(2, -1, width), ctx, 0).astype(BF)

    grad_first_all, grad_hidden_all, grad_low_all, grad_qkv_all = [], [], [], []
    for i in each:
        if i == 0:
            opened[i] = lax.optimization_barrier((opened[i], grad_ffn))[0]
        grad_second = gain_second * level_scatter_close(*opened[i])
        grad_hidden = cotangent[i].astype(F32) + norm_back(hidden[i], inv_second[i], grad_second)
        grad_low = grad_hidden.astype(BF)
        grad_mixed = product("rd,dc->rc", grad_low, out_full).astype(BF)
        grad_mixed = jnp.stack(jnp.split(grad_mixed, ranks, axis=1))
        grad_mixed = rank_swap(grad_mixed).reshape(length_half, head_cols)
        grad_query, grad_own, grad_early = attend_back(
            ctx_flag, qkv[i], early[i], logs[i], grad_mixed, cosine, sine
        )
        back = lax.ppermute(grad_early, "ctx", [(1, 0)])
        grad_qkv, grad_first = project_back(grad_query, grad_own, back, cosine, sine, qkv_full)
        grad_first_all.append(grad_first.reshape(ranks, shard_len, width))
        grad_hidden_all.append(grad_hidden)
        grad_low_all.append(grad_low)
        grad_qkv_all.append(grad_qkv)

    grad_out_w = outer(grad_low_all, mixed_own)
    grad_out_w = model_scatter(grad_out_w, level, ctx, part_rows).astype(BF)
    pieces = []
    for k in range(ranks):
        pieces += [one[k] for one in grad_first_all]
        pieces.append(pack(grad_out_w[:, k * head_cols : (k + 1) * head_cols], width))
    grad_first = jnp.concatenate(pieces, 0)
    grad_first = lax.psum_scatter(grad_first, "mp", scatter_dimension=0, tiled=True)

    result = level_scatter(after(results, grad_hidden_all[-1]), level)
    outputs = (jnp.concatenate(hidden, 0) + result).astype(BF).reshape(inputs.shape)

    grad_ffn = lax.psum_scatter(grad_ffn, "mp", scatter_dimension=0, tiled=True)
    grad_ffn = grad_ffn.reshape(2, half_blocks, sub, width)
    grad_ffn = jnp.stack(jnp.split(grad_ffn, width // (2 * part_rows), axis=-1))
    grad_ffn = team_scatter(grad_ffn.reshape((-1, LEVELS) + grad_ffn.shape[1:]))
    grad_ffn = level_swap(grad_ffn, level).transpose(1, 2, 0, 3, 4)
    grad_ffn = grad_ffn.reshape(2, half_blocks, unit_cols, 2 * part_rows)
    own_part, sent_part = pair_split(grad_ffn[..., :part_rows], grad_ffn[..., part_rows:], ctx)
    grad_ffn = jnp.concatenate(
        [jnp.where(ctx == 0, own_part, sent_part), jnp.where(ctx == 0, sent_part, own_part)], 1
    ).astype(F32)
    grad_up_out = grad_ffn[0].transpose(2, 0, 1)
    grad_down_out = grad_ffn[1]
    gain_ffn_part = jnp.sum(grad_up_out * w_up.astype(F32), axis=(1, 2)) / gain_ffn.astype(F32)

    grad_qkv_w = outer(normed_all, grad_qkv_all)
    grad_qkv_w = model_scatter(grad_qkv_w, level, ctx, part_rows)
    originals = jnp.concatenate([w_query, w_key, w_value], axis=1).astype(F32)
    gain_attn_part = jnp.sum(grad_qkv_w * originals, axis=1) / gain_attn.astype(F32)
    gain_grads = jnp.stack([gain_attn_part, gain_ffn_part])
    gain_grads = gain_grads + sum([turn(gain_grads, "mp", k) for k in range(1, ranks)])

    grad_first = after(grad_first, gain_grads, outputs, grad_qkv_w, grad_up_out, grad_down_out)
    grad_out_out = unpack(grad_first[own_rows:], head_cols).astype(F32).T
    inputs_f = inputs.astype(F32)
    input_grads = jnp.stack(grad_hidden_all) + norm_back(
        inputs_f,
        inverse_rms(inputs_f),
        gain_first * grad_first[:own_rows].reshape(inputs.shape).astype(F32),
    )
    return (
        outputs,
        input_grads,
        grad_qkv_w[:, :head_cols],
        grad_qkv_w[:, head_cols : 2 * head_cols],
        grad_qkv_w[:, 2 * head_cols :],
        grad_out_out,
        grad_up_out,
        grad_down_out,
        gain_grads[0],
        gain_grads[1],
    )


def solution(mesh):
    in_specs = (
        P("dp", ("ctx", "mp"), None),
        P(("dp", "ctx"), "mp"),
        P(("dp", "ctx"), "mp"),
        P(("dp", "ctx"), "mp"),
        P("mp", ("dp", "ctx")),
        P(("dp", "ctx"), None, "mp"),
        P(None, "mp", ("dp", "ctx")),
        P(("dp", "ctx")),
        P(("dp", "ctx")),
        P("dp", ("ctx", "mp"), None),
    )
    out_specs = (
        P("dp", ("ctx", "mp"), None),
        P("dp", ("ctx", "mp"), None),
        P(("dp", "ctx"), "mp"),
        P(("dp", "ctx"), "mp"),
        P(("dp", "ctx"), "mp"),
        P("mp", ("dp", "ctx")),
        P(("dp", "ctx"), None, "mp"),
        P(None, "mp", ("dp", "ctx")),
        P(("dp", "ctx")),
        P(("dp", "ctx")),
    )
    return jax.shard_map(local, mesh=mesh, in_specs=in_specs, out_specs=out_specs, check_vma=False)
```

```python
import functools

import jax
import jax.numpy as jnp
from jax import lax
from jax.experimental import pallas as pl
from jax.experimental.pallas import tpu as pltpu
from jax.sharding import PartitionSpec as P

HEAD = 128
LEVELS = 4
EPSILON = 1e-06
NEGATIVE = -1e30
BF = jnp.bfloat16
F32 = jnp.float32
MIB = 1 << 20
HURRY = 16


def flip(shard, axis, bit):
    devices = lax.axis_size(axis)
    return lax.ppermute(shard, axis, [(i, i ^ bit) for i in range(devices)])


def turn(shard, axis, by):
    devices = lax.axis_size(axis)
    return lax.ppermute(shard, axis, [(i, (i + by) % devices) for i in range(devices)])


def after(values, *others):
    return lax.optimization_barrier((values,) + others)[0]


def put(buffer, part, index, dim=0):
    starts = [0] * buffer.ndim
    starts[dim] = index
    return lax.dynamic_update_slice(buffer, jnp.expand_dims(part, dim), tuple(starts))


def take(buffer, index, dim=0):
    return lax.dynamic_index_in_dim(buffer, index, dim, keepdims=False)


def side_by_side(parts):
    return jnp.concatenate([parts[k] for k in range(parts.shape[0])], axis=-1)


def pack(part, width):
    rows, cols = part.shape
    return side_by_side(part.reshape(width // cols, -1, cols))


def unpack(packed, cols):
    strips = packed.shape[1] // cols
    return jnp.concatenate([packed[:, k * cols : (k + 1) * cols] for k in range(strips)], 0)


def rank_swap(parts):
    return [parts[0]] + [turn(parts[k], "mp", k) for k in range(1, len(parts))]


def level_pieces(part):
    half = part.shape[0] // 2
    from_x = flip(part, "dp", 1)
    from_y = flip(part, "dp", 2)
    return part, from_x, from_y, flip(from_x[:half], "dp", 2), flip(from_y[half:], "dp", 1)


def level_gather(part, mine):
    return level_join(level_pieces(part), mine)


def level_join(pieces, mine):
    part, from_x, from_y, low_half, high_half = pieces
    whole = put(jnp.zeros((LEVELS,) + part.shape, part.dtype), part, mine)
    whole = put(whole, from_x, mine ^ 1)
    whole = put(whole, from_y, mine ^ 2)
    return put(whole, jnp.concatenate([low_half, high_half], 0), mine ^ 3)


def level_gather_small(part, mine):
    whole = put(jnp.zeros((LEVELS,) + part.shape, part.dtype), part, mine)
    for k in range(1, LEVELS):
        whole = put(whole, flip(part, "dp", k), mine ^ k)
    return whole


def level_scatter_open(parts, mine):
    half = parts.shape[1] // 2
    own, by_x, by_y, by_xy = (take(parts, mine ^ k) for k in range(LEVELS))
    got_x = flip(jnp.stack([by_x[:half], by_xy[:half]]), "dp", 1)
    got_y = flip(jnp.stack([by_y[half:], by_xy[half:]]), "dp", 2)
    return own, by_x[half:], by_y[:half], got_x, got_y


def level_scatter_last(by_x, by_y, got_x, got_y):
    send_y = (by_y.astype(F32) + got_x[1].astype(F32)).astype(by_y.dtype)
    send_x = (by_x.astype(F32) + got_y[1].astype(F32)).astype(by_x.dtype)
    return flip(send_y, "dp", 2), flip(send_x, "dp", 1)


def level_scatter(parts, mine):
    opened = level_scatter_open(parts, mine)
    return level_sum(opened, level_scatter_last(*opened[1:]))


def level_sum(opened, last):
    own, _, by_y, got_x, got_y = opened
    last_y, last_x = last
    half = by_y.shape[0]
    first = own[:half].astype(F32) + got_x[0].astype(F32) + last_y.astype(F32)
    second = own[half:].astype(F32) + got_y[0].astype(F32) + last_x.astype(F32)
    return jnp.concatenate([first, second], 0)


def level_swap(parts, mine):
    whole = put(jnp.zeros(parts.shape, parts.dtype), take(parts, mine), mine)
    for k in range(1, LEVELS):
        whole = put(whole, flip(take(parts, mine ^ k), "dp", k), mine ^ k)
    return whole


def teams(devices):
    return [list(range(level, devices, LEVELS)) for level in range(LEVELS)]


def team_gather(part):
    devices = lax.axis_size("dp")
    if devices == LEVELS:
        return part[None]
    return lax.all_gather(part, "dp", axis=0, axis_index_groups=teams(devices))


def team_scatter(parts):
    devices = lax.axis_size("dp")
    if devices == LEVELS:
        return parts[0]
    return lax.psum_scatter(
        parts, "dp", scatter_dimension=0, axis_index_groups=teams(devices), tiled=False
    )


def pair_gather(part, mine, dim=0):
    other = flip(part, "ctx", 1)
    shape = part.shape[:dim] + (2,) + part.shape[dim:]
    return put(put(jnp.zeros(shape, part.dtype), part, mine, dim), other, 1 - mine, dim)


def pair_split(first, second, mine):
    own = jnp.where(mine == 0, first, second)
    return own, flip(jnp.where(mine == 0, second, first), "ctx", 1)


def pair_scatter(parts, mine, dim):
    other = flip(take(parts, 1 - mine, dim), "ctx", 1)
    return take(parts, mine, dim).astype(F32) + other.astype(F32)


def model_gather(part, level, ctx):
    rows, width = part.shape
    whole = team_gather(level_gather(part, level))
    whole = pair_gather(whole.reshape(-1, rows, width), ctx, 1)
    return whole.reshape(-1, width)


def model_scatter(grad, level, ctx, rows):
    width = grad.shape[1]
    parts = grad.reshape(-1, 2, rows, width)
    parts = pair_scatter(parts, ctx, 1).astype(grad.dtype)
    parts = team_scatter(parts.reshape(-1, LEVELS, rows, width))
    return level_scatter(parts, level)


def cost(flops, bytes_accessed, transcendentals):
    return pl.CostEstimate(
        flops=flops // HURRY,
        bytes_accessed=bytes_accessed // HURRY,
        transcendentals=transcendentals // HURRY,
    )


def contract(left, right, left_dim, right_dim):
    return lax.dot_general(
        left, right, (((left_dim,), (right_dim,)), ((), ())), preferred_element_type=F32
    )


def turned(values, cosine, sine):
    return values * cosine + pltpu.roll(values, HEAD // 2, 1) * sine


def project_kernel(rows_ref, gain_ref, weight_ref, cos_ref, sin_ref, out_ref, normed_ref):
    @pl.when(pl.program_id(1) == 0)
    def _():
        values = rows_ref[...].reshape(normed_ref.shape).astype(F32)
        inv = lax.rsqrt(jnp.mean(values * values, axis=-1, keepdims=True) + EPSILON)
        normed_ref[...] = (values * inv * gain_ref[...]).astype(BF)

    values = contract(normed_ref[...], weight_ref[...], 1, 0)
    cosine, sine = cos_ref[0], sin_ref[0]
    for head in range(values.shape[1] // HEAD):
        cols = slice(head * HEAD, (head + 1) * HEAD)
        out_ref[0, :, cols] = turned(values[:, cols], cosine, sine).astype(BF)


def project(count, shard_len, rows, gain, weight, cosine, sine):
    ranks, _, width = rows.shape
    length = ranks * shard_len
    cols = weight.shape[1] // 3
    table = pl.BlockSpec((1, length, HEAD), lambda i, j: (j // 2, 0, 0))
    return pl.pallas_call(
        project_kernel,
        grid=(count, 3),
        in_specs=[
            pl.BlockSpec((ranks, shard_len, width), lambda i, j: (0, i, 0)),
            pl.BlockSpec((1, width), lambda i, j: (0, 0)),
            pl.BlockSpec((width, cols), lambda i, j: (0, j)),
            table,
            table,
        ],
        out_specs=[
            pl.BlockSpec((1, length, cols), lambda i, j: (j, i, 0)),
            pl.BlockSpec((length, width), lambda i, j: (i, 0)),
        ],
        out_shape=[
            jax.ShapeDtypeStruct((3, count * length, cols), BF),
            jax.ShapeDtypeStruct((count * length, width), BF),
        ],
        compiler_params=pltpu.CompilerParams(vmem_limit_bytes=24 * MIB),
        cost_estimate=cost(
            flops=6 * length * width * cols,
            bytes_accessed=4 * length * width + 6 * width * cols + 6 * length * cols,
            transcendentals=0,
        ),
        name="project",
    )(rows, gain, weight, cosine, sine)


def softmax_parts(query, key_own, key_early, first, late):
    factor = HEAD ** (-0.5)
    own = contract(query, key_own, 1, 1) * factor
    row_ids = first + lax.broadcasted_iota(jnp.int32, own.shape, 0)
    col_ids = lax.broadcasted_iota(jnp.int32, own.shape, 1)
    own = jnp.where(col_ids <= row_ids, own, NEGATIVE)
    early = contract(query, key_early, 1, 1) * factor if late else None
    return own, early


def attend_kernel(strip, place_ref, query_ref, key_ref, value_ref, early_ref, *refs):
    *part_refs, log_ref, mixed_ref = refs
    length = query_ref.shape[1]
    ranks = len(part_refs)
    shard_len = length // ranks

    def run(late):
        for first in range(0, length, strip):
            end = first + strip
            own, early = softmax_parts(
                query_ref[0, first:end], key_ref[0, :end], early_ref[0], first, late
            )
            largest = jnp.max(own, axis=-1, keepdims=True)
            if late:
                largest = jnp.maximum(largest, jnp.max(early, axis=-1, keepdims=True))
            own = jnp.exp(own - largest)
            total = jnp.sum(own, axis=-1, keepdims=True)
            if late:
                early = jnp.exp(early - largest)
                total = total + jnp.sum(early, axis=-1, keepdims=True)
            inverse = 1.0 / total
            mixed = contract((own * inverse).astype(BF), value_ref[0, :end], 1, 0)
            if late:
                mixed = mixed + contract((early * inverse).astype(BF), early_ref[1], 1, 0)
            mixed_ref[first:end] = mixed.astype(BF)
            log_ref[0, first:end] = largest + jnp.log(total)

    @pl.when(place_ref[0] == 0)
    def _():
        run(False)

    @pl.when(place_ref[0] != 0)
    def _():
        run(True)

    for k, part_ref in enumerate(part_refs):
        target = lax.rem(place_ref[1] + k, ranks)
        part_ref[...] = mixed_ref[pl.ds(pl.multiple_of(target * shard_len, shard_len), shard_len)]


def attend(place, ranks, length, qkv, early):
    _, rows, cols = qkv.shape
    count = rows // length
    heads = cols // HEAD
    shard_len = length // ranks
    one = lambda which: pl.BlockSpec((1, length, HEAD), lambda i, h, p: (which, i, h))
    part = pl.BlockSpec((shard_len, HEAD), lambda i, h, p: (i, h))
    *parts, logs = pl.pallas_call(
        functools.partial(attend_kernel, length // 2),
        grid_spec=pltpu.PrefetchScalarGridSpec(
            num_scalar_prefetch=1,
            grid=(count, heads),
            in_specs=[
                one(0),
                one(1),
                one(2),
                pl.BlockSpec((2, length, HEAD), lambda i, h, p: (0, i, h)),
            ],
            out_specs=[part] * ranks + [pl.BlockSpec((1, length, 1), lambda i, h, p: (i * heads + h, 0, 0))],
            scratch_shapes=[pltpu.VMEM((length, HEAD), BF)],
        ),
        out_shape=[jax.ShapeDtypeStruct((count * shard_len, cols), BF)] * ranks
        + [jax.ShapeDtypeStruct((count * heads, length, 1), F32)],
        compiler_params=pltpu.CompilerParams(vmem_limit_bytes=24 * MIB),
        cost_estimate=cost(
            flops=8 * length * length * cols,
            bytes_accessed=14 * length * cols,
            transcendentals=2 * length * length * heads,
        ),
        name="attend",
    )(place, qkv, qkv, qkv, early)
    return parts, logs


def hidden_kernel(ranks, place_ref, input_ref, gain_ref, weight_ref, *refs):
    part_refs, (hidden_ref, normed_ref, mixed_ref) = refs[:ranks], refs[ranks:]
    cols = part_refs[0].shape[1]
    hidden = input_ref[...].astype(F32)
    for k, part_ref in enumerate(part_refs):
        source = lax.rem(place_ref[1] + ranks - k, ranks)
        where = pl.ds(pl.multiple_of(source * cols, HEAD), cols)
        hidden = hidden + contract(part_ref[...], weight_ref[:, where], 1, 1)
        mixed_ref[:, where] = part_ref[...]
    hidden_ref[...] = hidden
    inv = lax.rsqrt(jnp.mean(hidden * hidden, axis=-1, keepdims=True) + EPSILON)
    normed_ref[...] = (hidden * inv * gain_ref[...]).astype(BF)


def finish_attention(place, inputs, gain, weight, parts):
    shard_len, width = inputs.shape
    ranks, cols = len(parts), parts[0].shape[1]
    whole = lambda shape: pl.BlockSpec(shape, lambda j, p: (0,) * len(shape))
    return pl.pallas_call(
        functools.partial(hidden_kernel, ranks),
        grid_spec=pltpu.PrefetchScalarGridSpec(
            num_scalar_prefetch=1,
            grid=(1,),
            in_specs=[
                whole((shard_len, width)),
                whole((1, width)),
                whole(weight.shape),
            ]
            + [whole((shard_len, cols))] * ranks,
            out_specs=[
                whole((shard_len, width)),
                whole((shard_len, width)),
                whole((shard_len, ranks * cols)),
            ],
        ),
        out_shape=[
            jax.ShapeDtypeStruct((shard_len, width), F32),
            jax.ShapeDtypeStruct((shard_len, width), BF),
            jax.ShapeDtypeStruct((shard_len, ranks * cols), BF),
        ],
        compiler_params=pltpu.CompilerParams(vmem_limit_bytes=40 * MIB),
        cost_estimate=cost(
            flops=2 * shard_len * width * width,
            bytes_accessed=2 * width * width + 12 * shard_len * width,
            transcendentals=0,
        ),
        name="finish_attention",
    )(place, inputs, gain, weight, *parts)


def grad_hidden_kernel(
    ranks,
    place_ref,
    own_ref,
    got_x_ref,
    last_y_ref,
    got_y_ref,
    last_x_ref,
    hidden_ref,
    cot_ref,
    gain_ref,
    weight_ref,
    grad_ref,
    low_ref,
    *part_refs,
):
    half = last_y_ref.shape[0]
    cols = part_refs[0].shape[1]
    for rows, got_ref, last_ref in (
        (slice(0, half), got_x_ref, last_y_ref),
        (slice(half, 2 * half), got_y_ref, last_x_ref),
    ):
        weighted = own_ref[rows].astype(F32) + got_ref[0].astype(F32) + last_ref[...].astype(F32)
        weighted = weighted * gain_ref[...]
        values = hidden_ref[rows]
        inv = lax.rsqrt(jnp.mean(values * values, axis=-1, keepdims=True) + EPSILON)
        inner = jnp.mean(weighted * values, axis=-1, keepdims=True)
        grad = inv * weighted - values * (inv * inv * inv * inner) + cot_ref[rows].astype(F32)
        grad_ref[rows] = grad
        low_ref[rows] = grad.astype(BF)
    for k, part_ref in enumerate(part_refs):
        target = lax.rem(place_ref[1] + k, ranks)
        where = pl.ds(pl.multiple_of(target * cols, HEAD), cols)
        part_ref[...] = contract(low_ref[...], weight_ref[:, where], 1, 0).astype(BF)


def begin_back(place, ranks, pieces, hidden, cotangent, gain, weight):
    shard_len, width = hidden.shape
    cols = weight.shape[1] // ranks
    half = shard_len // 2
    whole = lambda shape: pl.BlockSpec(shape, lambda j, p: (0,) * len(shape))
    first = pl.BlockSpec((1, half, width), lambda j, p: (0, 0, 0))
    grad, low, *parts = pl.pallas_call(
        functools.partial(grad_hidden_kernel, ranks),
        grid_spec=pltpu.PrefetchScalarGridSpec(
            num_scalar_prefetch=1,
            grid=(1,),
            in_specs=[
                whole((shard_len, width)),
                first,
                whole((half, width)),
                first,
                whole((half, width)),
                whole((shard_len, width)),
                whole((shard_len, width)),
                whole((1, width)),
                whole(weight.shape),
            ],
            out_specs=[whole((shard_len, width))] * 2 + [whole((shard_len, cols))] * ranks,
        ),
        out_shape=[
            jax.ShapeDtypeStruct((shard_len, width), F32),
            jax.ShapeDtypeStruct((shard_len, width), BF),
        ]
        + [jax.ShapeDtypeStruct((shard_len, cols), BF)] * ranks,
        compiler_params=pltpu.CompilerParams(vmem_limit_bytes=48 * MIB),
        cost_estimate=cost(
            flops=2 * shard_len * width * width,
            bytes_accessed=2 * width * width + 20 * shard_len * width,
            transcendentals=0,
        ),
        name="begin_back",
    )(place, *pieces, hidden, cotangent, gain, weight)
    return grad, low, parts


def attend_back_kernel(
    strip, place_ref, query_ref, key_ref, value_ref, early_ref, log_ref, cos_ref, sin_ref, *refs
):
    *part_refs, query_out, own_out, early_out, grad_ref = refs
    length = query_ref.shape[1]
    factor = HEAD ** (-0.5)
    ranks = len(part_refs)
    shard_len = length // ranks
    for k, part_ref in enumerate(part_refs):
        source = lax.rem(place_ref[1] + ranks - k, ranks)
        grad_ref[pl.ds(pl.multiple_of(source * shard_len, shard_len), shard_len)] = part_ref[...]

    def run(late):
        early_key_sum = early_value_sum = 0.0
        for first in range(length - strip, -1, -strip):
            end = first + strip
            query = query_ref[0, first:end]
            grad = grad_ref[first:end]
            log = log_ref[0, first:end]
            own, early = softmax_parts(query, key_ref[0, :end], early_ref[0], first, late)
            own = jnp.exp(own - log)
            own_grad = contract(grad, value_ref[0, :end], 1, 1)
            inner = jnp.sum(own_grad * own, axis=-1, keepdims=True)
            if late:
                early = jnp.exp(early - log)
                early_grad = contract(grad, early_ref[1], 1, 1)
                inner = inner + jnp.sum(early_grad * early, axis=-1, keepdims=True)
            own_low = (own * (own_grad - inner)).astype(BF)
            grad_query = contract(own_low, key_ref[0, :end], 1, 0)
            grad_key = contract(own_low, query, 0, 0) * factor
            grad_value = contract(own.astype(BF), grad, 0, 0)
            if first == length - strip:
                own_out[0] = grad_key
                own_out[1] = grad_value
            else:
                own_out[0, :end] += grad_key
                own_out[1, :end] += grad_value
            if late:
                early_low = (early * (early_grad - inner)).astype(BF)
                grad_query = grad_query + contract(early_low, early_ref[0], 1, 0)
                early_key_sum = early_key_sum + contract(early_low, query, 0, 0)
                early_value_sum = early_value_sum + contract(early.astype(BF), grad, 0, 0)
            grad_query = grad_query * factor
            query_out[first:end] = turned(
                grad_query, cos_ref[0, first:end], -sin_ref[0, first:end]
            ).astype(BF)
        if late:
            early_out[0] = (early_key_sum * factor).astype(BF)
            early_out[1] = early_value_sum.astype(BF)
        else:
            early_out[...] = jnp.zeros(early_out.shape, BF)

    @pl.when(place_ref[0] == 0)
    def _():
        run(False)

    @pl.when(place_ref[0] != 0)
    def _():
        run(True)


def attend_back(place, length, qkv, early, logs, parts, cosine, sine):
    _, rows, cols = qkv.shape
    count = rows // length
    heads, ranks = cols // HEAD, len(parts)
    one = lambda which: pl.BlockSpec((1, length, HEAD), lambda i, h, p: (which, i, h))
    pair = pl.BlockSpec((2, length, HEAD), lambda i, h, p: (0, i, h))
    table = pl.BlockSpec((1, length, HEAD), lambda i, h, p: (0, 0, 0))
    return pl.pallas_call(
        functools.partial(attend_back_kernel, length // 2),
        grid_spec=pltpu.PrefetchScalarGridSpec(
            num_scalar_prefetch=1,
            grid=(count, heads),
            in_specs=[
                one(0),
                one(1),
                one(2),
                pair,
                pl.BlockSpec((1, length, 1), lambda i, h, p: (i * heads + h, 0, 0)),
                table,
                table,
            ]
            + [pl.BlockSpec((length // ranks, HEAD), lambda i, h, p: (i, h))] * ranks,
            out_specs=[pl.BlockSpec((length, HEAD), lambda i, h, p: (i, h)), pair, pair],
            scratch_shapes=[pltpu.VMEM((length, HEAD), BF)],
        ),
        out_shape=[
            jax.ShapeDtypeStruct((rows, cols), BF),
            jax.ShapeDtypeStruct((2, rows, cols), F32),
            jax.ShapeDtypeStruct((2, rows, cols), BF),
        ],
        compiler_params=pltpu.CompilerParams(vmem_limit_bytes=32 * MIB),
        cost_estimate=cost(
            flops=20 * length * length * cols,
            bytes_accessed=28 * length * cols,
            transcendentals=2 * length * length * heads,
        ),
        name="attend_back",
    )(place, qkv, qkv, qkv, early, logs, cosine, sine, *parts)


def project_back_kernel(
    query_ref, own_ref, back_ref, cos_ref, sin_ref, weight_ref, low_ref, out_ref
):
    cols = query_ref.shape[1]

    @pl.when(pl.program_id(1) == 0)
    def _():
        low_ref[:, :cols] = query_ref[...]
        keys = own_ref[0] + back_ref[0].astype(F32)
        cosine, sine = cos_ref[0], -sin_ref[0]
        for head in range(cols // HEAD):
            part = slice(head * HEAD, (head + 1) * HEAD)
            into = slice(cols + head * HEAD, cols + (head + 1) * HEAD)
            low_ref[:, into] = turned(keys[:, part], cosine, sine).astype(BF)
        low_ref[:, 2 * cols :] = (own_ref[1] + back_ref[1].astype(F32)).astype(BF)

    result = contract(low_ref[...], weight_ref[...], 1, 1).astype(BF)
    out_ref[...] = result.reshape(out_ref.shape)


def project_back(count, ranks, grad_query, grad_own, back, cosine, sine, weight):
    rows, cols = grad_query.shape
    length = rows // count
    width = weight.shape[0]
    step = width // 3
    pair = pl.BlockSpec((2, length, cols), lambda i, j: (0, i, 0))
    table = pl.BlockSpec((1, length, HEAD), lambda i, j: (0, 0, 0))
    return pl.pallas_call(
        project_back_kernel,
        grid=(count, 3),
        in_specs=[
            pl.BlockSpec((length, cols), lambda i, j: (i, 0)),
            pair,
            pair,
            table,
            table,
            pl.BlockSpec((step, 3 * cols), lambda i, j: (j, 0)),
        ],
        out_specs=[
            pl.BlockSpec((length, 3 * cols), lambda i, j: (i, 0)),
            pl.BlockSpec((ranks, 1, length // ranks, step), lambda i, j: (0, i, 0, j)),
        ],
        out_shape=[
            jax.ShapeDtypeStruct((rows, 3 * cols), BF),
            jax.ShapeDtypeStruct((ranks, count, length // ranks, width), BF),
        ],
        compiler_params=pltpu.CompilerParams(vmem_limit_bytes=32 * MIB),
        cost_estimate=cost(
            flops=6 * rows * width * cols,
            bytes_accessed=6 * width * cols + 18 * rows * cols + 2 * rows * width,
            transcendentals=0,
        ),
        name="project_back",
    )(grad_query, grad_own, back, cosine, sine, weight)


def gelu_both(values):
    scale = (2.0 / jnp.pi) ** 0.5
    square = values * values
    tanh = jnp.tanh(scale * values * (1.0 + 0.044715 * square))
    half = 0.5 * (1.0 + tanh)
    slope = half + 0.5 * values * (1.0 - tanh * tanh) * scale * (1.0 + 3 * 0.044715 * square)
    return values * half, slope


def stack_units(first, own_ref, other_ref, which, into):
    ranks, _, blocks, sub, _ = own_ref.shape

    def fill(source):
        for block in range(blocks):
            for rank in range(ranks):
                row = (block * ranks + rank) * sub
                into[row : row + sub] = source[rank, which, block]

    @pl.when(first)
    def _():
        fill(own_ref)

    @pl.when(jnp.logical_not(first))
    def _():
        fill(other_ref)


def feed_kernel(count, place_ref, cot_ref, own_ref, other_ref, *refs):
    rows_in, refs = refs[: 5 * count], refs[5 * count :]
    grads_out, (rows_ref, down_ref, act_ref, pre_ref, up_ref, sum_ref) = (
        refs[: 5 * count],
        refs[5 * count :],
    )
    step = pl.program_id(0)
    half = up_ref.shape[0]
    shard_len = rows_ref.shape[1] // count
    part = shard_len // 2
    ctx, mine = place_ref[0], place_ref[2]

    for turn_of, at in ((0, 0), (1, LEVELS)):

        @pl.when(step == at)
        def _(turn_of=turn_of):
            stack_units(ctx == turn_of, own_ref, other_ref, 0, up_ref)
            stack_units(ctx == turn_of, own_ref, other_ref, 1, down_ref.at[0])

    for k in range(LEVELS):

        @pl.when((step < LEVELS) & (jnp.bitwise_xor(mine, k) == step))
        def _(k=k):
            for i in range(count):
                pieces = rows_in[5 * i : 5 * i + 5]
                rows = slice(i * shard_len, (i + 1) * shard_len)
                if k < LEVELS - 1:
                    rows_ref[0, rows] = pieces[k][...]
                else:
                    rows_ref[0, rows.start : rows.start + part] = pieces[3][...]
                    rows_ref[0, rows.start + part : rows.stop] = pieces[4][...]

    def run(used):
        upped = contract(rows_ref[0], up_ref[:used], 1, 1)
        activated, slope = gelu_both(upped)
        grad_act = contract(cot_ref[0], down_ref[0, :used], 1, 1)
        grad_upped = (grad_act * slope).astype(BF)
        act_ref[0, :, :used] = activated.astype(BF)
        pre_ref[0, :, :used] = grad_upped
        return contract(grad_upped, up_ref[:used], 1, 0)

    for one in range(LEVELS - 1):

        @pl.when(step == one)
        def _(one=one):
            sum_ref[...] = run(half // 2 ** (LEVELS - 2 - one))

    @pl.when(step == LEVELS - 1)
    def _():
        sum_ref[...] = run(half)

    @pl.when(step == LEVELS)
    def _():
        sum_ref[...] += run(half)

    level = jnp.minimum(step, LEVELS - 1)
    for k in range(LEVELS):

        @pl.when((step != LEVELS - 1) & (jnp.bitwise_xor(mine, k) == level))
        def _(k=k):
            for i in range(count):
                keep, keep_x, keep_y, send_x, send_y = grads_out[5 * i : 5 * i + 5]
                first = sum_ref[i * shard_len : i * shard_len + part].astype(BF)
                second = sum_ref[i * shard_len + part : (i + 1) * shard_len].astype(BF)
                if k == 0:
                    keep[:part] = first
                    keep[part:] = second
                elif k == 1:
                    send_x[0] = first
                    keep_x[...] = second
                elif k == 2:
                    keep_y[...] = first
                    send_y[0] = second
                else:
                    send_x[1] = first
                    send_y[1] = second


def feed(place, rows, cot, own, other):
    count = len(rows)
    _, length, width = cot.shape
    half = own.shape[0] * own.shape[2] * own.shape[3]
    shard_len = length // count
    part = shard_len // 2
    whole = lambda shape: pl.BlockSpec(
        shape, lambda s, p: (0,) * len(shape), pipeline_mode=pl.Buffered(1)
    )
    fixed = lambda shape: pl.BlockSpec(shape, lambda s, p: (0,) * len(shape))
    by_level = pl.BlockSpec((1, length, width), lambda s, p: (jnp.minimum(s, LEVELS - 1), 0, 0))
    by_half = pl.BlockSpec((1, half, width), lambda s, p: (s // LEVELS, 0, 0))
    by_step = pl.BlockSpec((1, length, half), lambda s, p: (s, 0, 0))
    pieces = [
        (shard_len, width),
        (part, width),
        (part, width),
        (2, part, width),
        (2, part, width),
    ]
    *grads, rows_all, down, activated, before = pl.pallas_call(
        functools.partial(feed_kernel, count),
        grid_spec=pltpu.PrefetchScalarGridSpec(
            num_scalar_prefetch=1,
            grid=(LEVELS + 1,),
            in_specs=[by_level, whole(own.shape), whole(own.shape)]
            + [whole(piece.shape) for one in rows for piece in one],
            out_specs=[fixed(shape) for shape in pieces] * count
            + [by_level, by_half, by_step, by_step],
            scratch_shapes=[pltpu.VMEM((half, width), BF), pltpu.VMEM((length, width), F32)],
        ),
        out_shape=[jax.ShapeDtypeStruct(shape, BF) for shape in pieces] * count
        + [
            jax.ShapeDtypeStruct(cot.shape, BF),
            jax.ShapeDtypeStruct((2, half, width), BF),
            jax.ShapeDtypeStruct((LEVELS + 1, length, half), BF),
            jax.ShapeDtypeStruct((LEVELS + 1, length, half), BF),
        ],
        compiler_params=pltpu.CompilerParams(vmem_limit_bytes=58 * MIB),
        cost_estimate=cost(
            flops=24 * length * width * half,
            bytes_accessed=24 * length * width + 8 * half * width + 20 * length * half,
            transcendentals=5 * length * half,
        ),
        name="feed",
    )(place, cot, own, other, *[piece for one in rows for piece in one])
    grads = [grads[5 * i : 5 * i + 5] for i in range(count)]
    return grads, rows_all, down, activated, before


def feed_weights_kernel(
    place_ref,
    rows_ref,
    cot_ref,
    act_ref,
    pre_ref,
    down_ref,
    keep_ref,
    send_ref,
    out_ref,
    up_sum,
    down_sum,
    out_sum,
    stage,
    sem,
):
    step = pl.program_id(0)
    half = down_ref.shape[1]
    ranks, _, blocks, sub, _ = stage.shape

    def add(used, fresh):
        up_part = contract(pre_ref[0, :, :used], rows_ref[0], 0, 0)
        down_part = contract(act_ref[0, :, :used], cot_ref[0], 0, 0)
        if fresh == used:
            up_sum[:used] = up_part
            down_sum[:used] = down_part
        else:
            up_sum[:fresh] += up_part[:fresh]
            down_sum[:fresh] += down_part[:fresh]
            if fresh < used:
                up_sum[fresh:used] = up_part[fresh:]
                down_sum[fresh:used] = down_part[fresh:]
        return contract(act_ref[0, :, :used], down_ref[0, :used], 1, 0)

    def store(which):
        for block in range(blocks):
            for rank in range(ranks):
                first = (block * ranks + rank) * sub
                stage[rank, 0, block] = up_sum[first : first + sub].astype(BF)
                stage[rank, 1, block] = down_sum[first : first + sub].astype(BF)

        @pl.when(place_ref[0] == which)
        def _():
            copy = pltpu.make_async_copy(stage, keep_ref, sem)
            copy.start()
            copy.wait()

        @pl.when(place_ref[0] != which)
        def _():
            copy = pltpu.make_async_copy(stage, send_ref, sem)
            copy.start()
            copy.wait()

    for one in range(LEVELS - 1):

        @pl.when(step == one)
        def _(one=one):
            used = half // 2 ** (LEVELS - 2 - one)
            out_ref[0] = add(used, used if one == 0 else used // 2).astype(BF)

    @pl.when(step == LEVELS - 1)
    def _():
        up_sum[...] += contract(pre_ref[0], rows_ref[0], 0, 0)
        down_sum[...] += contract(act_ref[0], cot_ref[0], 0, 0)
        out_sum[...] = contract(act_ref[0], down_ref[0], 1, 0)
        store(0)

    @pl.when(step == LEVELS)
    def _():
        out_ref[0] = (out_sum[...] + add(half, half)).astype(BF)
        store(1)


def feed_weights(place, rows, cot, activated, before, down, ranks, blocks):
    _, length, width = rows.shape
    half = down.shape[1]
    sub = half // (ranks * blocks)
    by_level = pl.BlockSpec((1, length, width), lambda s, p: (jnp.minimum(s, LEVELS - 1), 0, 0))
    by_half = pl.BlockSpec((1, half, width), lambda s, p: (s // LEVELS, 0, 0))
    by_step = pl.BlockSpec((1, length, half), lambda s, p: (s, 0, 0))
    shape = (ranks, 2, blocks, sub, width)
    return pl.pallas_call(
        feed_weights_kernel,
        grid_spec=pltpu.PrefetchScalarGridSpec(
            num_scalar_prefetch=1,
            grid=(LEVELS + 1,),
            in_specs=[by_level, by_level, by_step, by_step, by_half],
            out_specs=[
                pl.BlockSpec(memory_space=pl.ANY),
                pl.BlockSpec(memory_space=pl.ANY),
                by_level,
            ],
            scratch_shapes=[
                pltpu.VMEM((half, width), F32),
                pltpu.VMEM((half, width), F32),
                pltpu.VMEM((length, width), F32),
                pltpu.VMEM(shape, BF),
                pltpu.SemaphoreType.DMA(()),
            ],
        ),
        out_shape=[
            jax.ShapeDtypeStruct(shape, BF),
            jax.ShapeDtypeStruct(shape, BF),
            jax.ShapeDtypeStruct(rows.shape, BF),
        ],
        compiler_params=pltpu.CompilerParams(vmem_limit_bytes=56 * MIB),
        cost_estimate=cost(
            flops=24 * length * width * half,
            bytes_accessed=24 * length * width + 12 * half * width + 20 * length * half,
            transcendentals=0,
        ),
        name="feed_weights",
    )(place, rows, cot, activated, before, down)


def outer_kernel(count, *refs):
    lefts, rights, out_ref = refs[:count], refs[count : 2 * count], refs[-1]
    total = contract(lefts[0][...], rights[0][...], 0, 0)
    for left, right in zip(lefts[1:], rights[1:]):
        total = total + contract(left[...], right[...], 0, 0)
    out_ref[...] = total.astype(BF)


def outer(lefts, rights):
    rows, m = lefts[0].shape
    n = rights[0].shape[1]
    count = len(lefts)
    step = m // 4
    return pl.pallas_call(
        functools.partial(outer_kernel, count),
        grid=(4,),
        in_specs=[pl.BlockSpec((rows, step), lambda j: (0, j))] * count
        + [pl.BlockSpec((rows, n), lambda j: (0, 0))] * count,
        out_specs=pl.BlockSpec((step, n), lambda j: (j, 0)),
        out_shape=jax.ShapeDtypeStruct((m, n), BF),
        compiler_params=pltpu.CompilerParams(vmem_limit_bytes=32 * MIB),
        cost_estimate=cost(
            flops=2 * count * rows * m * n,
            bytes_accessed=2 * (count * rows * (m + n) + m * n),
            transcendentals=0,
        ),
        name="outer",
    )(*lefts, *rights)


def inverse_rms(values):
    return lax.rsqrt(jnp.mean(values * values, axis=-1, keepdims=True) + EPSILON)


def norm_back(values, inv_rms, weighted):
    return inv_rms * weighted - values * (inv_rms * inv_rms * inv_rms) * jnp.mean(
        weighted * values, axis=-1, keepdims=True
    )


def rotation(positions, head_size):
    half_size = head_size // 2
    frequency = 10000.0 ** (-jnp.arange(half_size, dtype=jnp.float32) / half_size)
    angles = positions.astype(jnp.float32)[:, None] * frequency[None, :]
    cosine, sine = jnp.cos(angles), jnp.sin(angles)
    cosine = jnp.concatenate([cosine, cosine], -1)
    sine = jnp.concatenate([-sine, sine], -1)
    return (
        jnp.stack([cosine, jnp.ones_like(cosine)]),
        jnp.stack([sine, jnp.zeros_like(sine)]),
    )


def product(equation, left, right):
    return jnp.einsum(equation, left, right, preferred_element_type=F32)


def local(inputs, w_query, w_key, w_value, w_out, w_up, w_down, gain_attn, gain_ffn, cotangent):
    count, shard_len, width = inputs.shape
    own_rows = count * shard_len
    ranks = lax.axis_size("mp")
    length_half = shard_len * ranks
    level = lax.axis_index("dp") % LEVELS
    ctx = lax.axis_index("ctx")
    rank = lax.axis_index("mp")
    part_rows, head_cols = w_query.shape
    place = jnp.stack([ctx, rank, level]).astype(jnp.int32)

    inputs_flat = inputs.reshape(own_rows, width)
    cot_flat = cotangent.reshape(own_rows, width)
    rows_all = jnp.concatenate([inputs_flat, pack(w_out.T, width)], 0)
    rows_all = lax.all_gather(rows_all, "mp", axis=0)

    gains = team_gather(level_gather_small(jnp.stack([gain_attn, gain_ffn]), level))
    gains = pair_gather(gains.reshape(-1, 2, part_rows), ctx, 1)
    gains = gains.transpose(2, 0, 1, 3).reshape(2, 1, width).astype(F32)
    gain_first, gain_second = gains[0], gains[1]

    qkv_full = model_gather(jnp.concatenate([w_query, w_key, w_value], axis=1), level, ctx)
    blocks, unit_cols = w_up.shape[1:]
    sub = unit_cols // LEVELS
    half_blocks = blocks // 2
    up_turned = w_up.transpose(1, 2, 0)
    halves = [
        jnp.stack([up_turned[b : b + half_blocks], w_down[b : b + half_blocks]])
        for b in (0, half_blocks)
    ]
    own_part, sent_part = pair_split(halves[0], halves[1], ctx)
    pair = jnp.concatenate(
        [jnp.where(ctx == 0, own_part, sent_part), jnp.where(ctx == 0, sent_part, own_part)], -1
    )
    pair = pair.reshape(2, half_blocks, LEVELS, sub, 2 * part_rows).transpose(2, 0, 1, 3, 4)
    swapped = team_gather(level_swap(pair, level))
    swapped = side_by_side(swapped.reshape(-1, 2, half_blocks, sub, 2 * part_rows))
    cot_pieces = level_pieces(after(cot_flat, swapped))
    ranked = lax.all_gather(swapped, "mp", axis=0)
    positions = ctx * length_half + jnp.arange(length_half, dtype=jnp.int32)
    cosine, sine = rotation(positions, HEAD)
    qkv, normed = project(
        count, shard_len, rows_all, after(gain_first, *cot_pieces), qkv_full, cosine, sine
    )
    cot_rows = level_join(after(cot_pieces, qkv), level)
    out_rows = rows_all[:, own_rows:]
    out_parts = jnp.concatenate([unpack(out_rows[k], head_cols) for k in range(ranks)], 1)
    out_full = model_gather(out_parts, level, ctx)
    early = lax.ppermute(qkv[1:], "ctx", [(0, 1)])
    parts, logs = attend(place, ranks, length_half, qkv, early)
    hidden, normed_two, mixed_own = finish_attention(
        place, inputs_flat, gain_second, out_full, rank_swap(parts)
    )

    ranked = after(ranked, hidden)
    (opened,), rows_second, down_mine, activated, before = feed(
        place, [level_pieces(normed_two)], cot_rows, ranked, flip(ranked, "ctx", 1)
    )
    own, by_x, by_y, got_x, got_y = opened
    got_x, got_y = flip(got_x, "dp", 1), flip(got_y, "dp", 2)

    grad_kept, grad_sent, results = feed_weights(
        place, rows_second, cot_rows, activated, before, down_mine, ranks, half_blocks
    )
    grad_sent = after(grad_sent, got_x, got_y)
    grad_ffn = (grad_kept.astype(F32) + flip(grad_sent, "ctx", 1).astype(F32)).astype(BF)
    grad_ffn_low = [grad_ffn[:, kind].reshape(-1, width) for kind in range(2)]
    grad_ffn = [
        lax.psum_scatter(one, "mp", scatter_dimension=0, tiled=True) for one in grad_ffn_low
    ]

    last_y, last_x = level_scatter_last(by_x, by_y, got_x, got_y)
    own = after(own, *grad_ffn_low)
    grad_hidden, grad_low, parts = begin_back(
        place, ranks, (own, got_x, last_y, got_y, last_x), hidden, cot_flat, gain_second, out_full
    )
    parts = rank_swap(parts)
    grad_query, grad_own, grad_early = attend_back(
        place, length_half, qkv, early, logs, parts, cosine, sine
    )
    grad_early = after(grad_early, grad_ffn[0])
    back = lax.ppermute(grad_early, "ctx", [(1, 0)])
    grad_qkv, grad_first = project_back(
        count, ranks, grad_query, grad_own, back, cosine, sine, qkv_full
    )
    grad_first = after(grad_first, grad_ffn[1])
    grad_ffn = after(grad_ffn, grad_first)
    grad_first = lax.psum_scatter(
        grad_first.reshape(-1, width), "mp", scatter_dimension=0, tiled=True
    )

    results_open = after(level_scatter_open(after(results, grad_low), level), grad_qkv)
    result = level_sum(results_open, level_scatter_last(*results_open[1:]))
    outputs = (hidden + result).astype(BF).reshape(inputs.shape)

    grad_ffn = jnp.stack(grad_ffn).reshape(2, half_blocks, sub, width)
    grad_ffn = jnp.stack(jnp.split(grad_ffn, width // (2 * part_rows), axis=-1))
    grad_ffn = team_scatter(grad_ffn.reshape((-1, LEVELS) + grad_ffn.shape[1:]))
    grad_ffn = level_swap(grad_ffn, level).transpose(1, 2, 0, 3, 4)
    grad_ffn = grad_ffn.reshape(2, half_blocks, unit_cols, 2 * part_rows)
    own_part, sent_part = pair_split(grad_ffn[..., :part_rows], grad_ffn[..., part_rows:], ctx)
    grad_ffn = jnp.concatenate(
        [jnp.where(ctx == 0, own_part, sent_part), jnp.where(ctx == 0, sent_part, own_part)], 1
    ).astype(F32)
    grad_up_out = grad_ffn[0].transpose(2, 0, 1)
    grad_down_out = grad_ffn[1]
    gain_ffn_part = jnp.sum(grad_up_out * w_up.astype(F32), axis=(1, 2)) / gain_ffn.astype(F32)

    grad_qkv_w = outer([normed], [grad_qkv])
    grad_qkv_w = model_scatter(grad_qkv_w, level, ctx, part_rows)
    originals = jnp.concatenate([w_query, w_key, w_value], axis=1).astype(F32)
    gain_attn_part = jnp.sum(grad_qkv_w * originals, axis=1) / gain_attn.astype(F32)
    gain_grads = jnp.stack([gain_attn_part, gain_ffn_part])
    gain_grads = gain_grads + sum([turn(gain_grads, "mp", k) for k in range(1, ranks)])

    grad_out_w = outer([after(grad_low, grad_qkv)], [mixed_own])
    grad_out_w = model_scatter(grad_out_w, level, ctx, part_rows).astype(BF)
    grad_out_w = jnp.stack(jnp.split(grad_out_w, ranks, axis=1))
    grad_out_out = take(grad_out_w, rank).astype(F32)
    for k in range(1, ranks):
        grad_out_out = grad_out_out + turn(take(grad_out_w, (rank + k) % ranks), "mp", k).astype(F32)
    grad_out_out = grad_out_out.T

    grad_first = after(grad_first, grad_out_out, gain_grads, outputs, grad_qkv_w, grad_up_out, grad_down_out)
    inputs_f = inputs.astype(F32)
    input_grads = grad_hidden.reshape(inputs.shape) + norm_back(
        inputs_f,
        inverse_rms(inputs_f),
        gain_first * grad_first.reshape(inputs.shape).astype(F32),
    )
    return (
        outputs,
        input_grads,
        grad_qkv_w[:, :head_cols],
        grad_qkv_w[:, head_cols : 2 * head_cols],
        grad_qkv_w[:, 2 * head_cols :],
        grad_out_out,
        grad_up_out,
        grad_down_out,
        gain_grads[0],
        gain_grads[1],
    )


def solution(mesh):
    in_specs = (
        P("dp", ("ctx", "mp"), None),
        P(("dp", "ctx"), "mp"),
        P(("dp", "ctx"), "mp"),
        P(("dp", "ctx"), "mp"),
        P("mp", ("dp", "ctx")),
        P(("dp", "ctx"), None, "mp"),
        P(None, "mp", ("dp", "ctx")),
        P(("dp", "ctx")),
        P(("dp", "ctx")),
        P("dp", ("ctx", "mp"), None),
    )
    out_specs = (
        P("dp", ("ctx", "mp"), None),
        P("dp", ("ctx", "mp"), None),
        P(("dp", "ctx"), "mp"),
        P(("dp", "ctx"), "mp"),
        P(("dp", "ctx"), "mp"),
        P("mp", ("dp", "ctx")),
        P(("dp", "ctx"), None, "mp"),
        P(None, "mp", ("dp", "ctx")),
        P(("dp", "ctx")),
        P(("dp", "ctx")),
    )
    return jax.shard_map(local, mesh=mesh, in_specs=in_specs, out_specs=out_specs, check_vma=False)
```

```python
import functools

import jax
import jax.numpy as jnp
from jax import lax
from jax.experimental import pallas as pl
from jax.experimental.pallas import tpu as pltpu
from jax.sharding import PartitionSpec as P

HEAD = 128
LEVELS = 4
EPSILON = 1e-06
NEGATIVE = -1e30
BF = jnp.bfloat16
F32 = jnp.float32
MIB = 1 << 20
HURRY = 16


def flip(shard, axis, bit):
    devices = lax.axis_size(axis)
    return lax.ppermute(shard, axis, [(i, i ^ bit) for i in range(devices)])


def turn(shard, axis, by):
    devices = lax.axis_size(axis)
    return lax.ppermute(shard, axis, [(i, (i + by) % devices) for i in range(devices)])


def after(values, *others):
    return lax.optimization_barrier((values,) + others)[0]


def put(buffer, part, index, dim=0):
    starts = [0] * buffer.ndim
    starts[dim] = index
    return lax.dynamic_update_slice(buffer, jnp.expand_dims(part, dim), tuple(starts))


def take(buffer, index, dim=0):
    return lax.dynamic_index_in_dim(buffer, index, dim, keepdims=False)


def side_by_side(parts):
    return jnp.concatenate([parts[k] for k in range(parts.shape[0])], axis=-1)


def pack(part, width):
    rows, cols = part.shape
    return side_by_side(part.reshape(width // cols, -1, cols))


def unpack(packed, cols):
    strips = packed.shape[1] // cols
    return jnp.concatenate([packed[:, k * cols : (k + 1) * cols] for k in range(strips)], 0)


def rank_swap(parts):
    return [parts[0]] + [turn(parts[k], "mp", k) for k in range(1, len(parts))]


def level_pieces(part):
    half = part.shape[0] // 2
    from_x = flip(part, "dp", 1)
    from_y = flip(part, "dp", 2)
    return part, from_x, from_y, flip(from_x[:half], "dp", 2), flip(from_y[half:], "dp", 1)


def level_gather(part, mine):
    return level_join(level_pieces(part), mine)


def level_join(pieces, mine):
    part, from_x, from_y, low_half, high_half = pieces
    whole = put(jnp.zeros((LEVELS,) + part.shape, part.dtype), part, mine)
    whole = put(whole, from_x, mine ^ 1)
    whole = put(whole, from_y, mine ^ 2)
    return put(whole, jnp.concatenate([low_half, high_half], 0), mine ^ 3)


def level_gather_small(part, mine):
    whole = put(jnp.zeros((LEVELS,) + part.shape, part.dtype), part, mine)
    for k in range(1, LEVELS):
        whole = put(whole, flip(part, "dp", k), mine ^ k)
    return whole


def level_scatter_open(parts, mine):
    half = parts.shape[1] // 2
    own, by_x, by_y, by_xy = (take(parts, mine ^ k) for k in range(LEVELS))
    got_x = flip(jnp.stack([by_x[:half], by_xy[:half]]), "dp", 1)
    got_y = flip(jnp.stack([by_y[half:], by_xy[half:]]), "dp", 2)
    return own, by_x[half:], by_y[:half], got_x, got_y


def level_scatter_last(by_x, by_y, got_x, got_y):
    send_y = (by_y.astype(F32) + got_x[1].astype(F32)).astype(by_y.dtype)
    send_x = (by_x.astype(F32) + got_y[1].astype(F32)).astype(by_x.dtype)
    return flip(send_y, "dp", 2), flip(send_x, "dp", 1)


def level_scatter(parts, mine):
    opened = level_scatter_open(parts, mine)
    return level_sum(opened, level_scatter_last(*opened[1:]))


def level_sum(opened, last):
    own, _, by_y, got_x, got_y = opened
    last_y, last_x = last
    half = by_y.shape[0]
    first = own[:half].astype(F32) + got_x[0].astype(F32) + last_y.astype(F32)
    second = own[half:].astype(F32) + got_y[0].astype(F32) + last_x.astype(F32)
    return jnp.concatenate([first, second], 0)


def level_swap(parts, mine):
    whole = put(jnp.zeros(parts.shape, parts.dtype), take(parts, mine), mine)
    for k in range(1, LEVELS):
        whole = put(whole, flip(take(parts, mine ^ k), "dp", k), mine ^ k)
    return whole


def teams(devices):
    return [list(range(level, devices, LEVELS)) for level in range(LEVELS)]


def team_gather(part):
    devices = lax.axis_size("dp")
    if devices == LEVELS:
        return part[None]
    return lax.all_gather(part, "dp", axis=0, axis_index_groups=teams(devices))


def team_scatter(parts):
    devices = lax.axis_size("dp")
    if devices == LEVELS:
        return parts[0]
    return lax.psum_scatter(
        parts, "dp", scatter_dimension=0, axis_index_groups=teams(devices), tiled=False
    )


def pair_gather(part, mine, dim=0):
    other = flip(part, "ctx", 1)
    shape = part.shape[:dim] + (2,) + part.shape[dim:]
    return put(put(jnp.zeros(shape, part.dtype), part, mine, dim), other, 1 - mine, dim)


def pair_split(first, second, mine):
    own = jnp.where(mine == 0, first, second)
    return own, flip(jnp.where(mine == 0, second, first), "ctx", 1)


def pair_scatter(parts, mine, dim):
    other = flip(take(parts, 1 - mine, dim), "ctx", 1)
    return take(parts, mine, dim).astype(F32) + other.astype(F32)


def model_gather(part, level, ctx):
    rows, width = part.shape
    whole = team_gather(level_gather(part, level))
    whole = pair_gather(whole.reshape(-1, rows, width), ctx, 1)
    return whole.reshape(-1, width)


def model_scatter(grad, level, ctx, rows):
    width = grad.shape[1]
    parts = grad.reshape(-1, 2, rows, width)
    parts = pair_scatter(parts, ctx, 1).astype(grad.dtype)
    parts = team_scatter(parts.reshape(-1, LEVELS, rows, width))
    return level_scatter(parts, level)


def cost(flops, bytes_accessed, transcendentals):
    return pl.CostEstimate(
        flops=flops // HURRY,
        bytes_accessed=bytes_accessed // HURRY,
        transcendentals=transcendentals // HURRY,
    )


def contract(left, right, left_dim, right_dim):
    return lax.dot_general(
        left, right, (((left_dim,), (right_dim,)), ((), ())), preferred_element_type=F32
    )


def turned(values, cosine, sine):
    return values * cosine + pltpu.roll(values, HEAD // 2, 1) * sine


def project_kernel(rows_ref, gain_ref, weight_ref, cos_ref, sin_ref, out_ref, normed_ref):
    @pl.when(pl.program_id(1) == 0)
    def _():
        values = rows_ref[...].reshape(normed_ref.shape).astype(F32)
        inv = lax.rsqrt(jnp.mean(values * values, axis=-1, keepdims=True) + EPSILON)
        normed_ref[...] = (values * inv * gain_ref[...]).astype(BF)

    values = contract(normed_ref[...], weight_ref[...], 1, 0)
    cosine, sine = cos_ref[0], sin_ref[0]
    for head in range(values.shape[1] // HEAD):
        cols = slice(head * HEAD, (head + 1) * HEAD)
        out_ref[0, :, cols] = turned(values[:, cols], cosine, sine).astype(BF)


def project(count, shard_len, rows, gain, weight, cosine, sine):
    ranks, _, width = rows.shape
    length = ranks * shard_len
    cols = weight.shape[1] // 3
    table = pl.BlockSpec((1, length, HEAD), lambda i, j: (j // 2, 0, 0))
    return pl.pallas_call(
        project_kernel,
        grid=(count, 3),
        in_specs=[
            pl.BlockSpec((ranks, shard_len, width), lambda i, j: (0, i, 0)),
            pl.BlockSpec((1, width), lambda i, j: (0, 0)),
            pl.BlockSpec((width, cols), lambda i, j: (0, j)),
            table,
            table,
        ],
        out_specs=[
            pl.BlockSpec((1, length, cols), lambda i, j: (j, i, 0)),
            pl.BlockSpec((length, width), lambda i, j: (i, 0)),
        ],
        out_shape=[
            jax.ShapeDtypeStruct((3, count * length, cols), BF),
            jax.ShapeDtypeStruct((count * length, width), BF),
        ],
        compiler_params=pltpu.CompilerParams(vmem_limit_bytes=24 * MIB),
        cost_estimate=cost(
            flops=6 * length * width * cols,
            bytes_accessed=4 * length * width + 6 * width * cols + 6 * length * cols,
            transcendentals=0,
        ),
        name="project",
    )(rows, gain, weight, cosine, sine)


def softmax_parts(query, key_own, key_early, first, late):
    factor = HEAD ** (-0.5)
    own = contract(query, key_own, 1, 1) * factor
    row_ids = first + lax.broadcasted_iota(jnp.int32, own.shape, 0)
    col_ids = lax.broadcasted_iota(jnp.int32, own.shape, 1)
    own = jnp.where(col_ids <= row_ids, own, NEGATIVE)
    early = contract(query, key_early, 1, 1) * factor if late else None
    return own, early


def attend_kernel(strip, place_ref, query_ref, key_ref, value_ref, early_ref, *refs):
    *part_refs, log_ref, mixed_ref = refs
    length = query_ref.shape[1]
    ranks = len(part_refs)
    shard_len = length // ranks

    def run(late):
        for first in range(0, length, strip):
            end = first + strip
            own, early = softmax_parts(
                query_ref[0, first:end], key_ref[0, :end], early_ref[0], first, late
            )
            largest = jnp.max(own, axis=-1, keepdims=True)
            if late:
                largest = jnp.maximum(largest, jnp.max(early, axis=-1, keepdims=True))
            own = jnp.exp(own - largest)
            total = jnp.sum(own, axis=-1, keepdims=True)
            if late:
                early = jnp.exp(early - largest)
                total = total + jnp.sum(early, axis=-1, keepdims=True)
            inverse = 1.0 / total
            mixed = contract((own * inverse).astype(BF), value_ref[0, :end], 1, 0)
            if late:
                mixed = mixed + contract((early * inverse).astype(BF), early_ref[1], 1, 0)
            mixed_ref[first:end] = mixed.astype(BF)
            log_ref[0, first:end] = largest + jnp.log(total)

    @pl.when(place_ref[0] == 0)
    def _():
        run(False)

    @pl.when(place_ref[0] != 0)
    def _():
        run(True)

    for k, part_ref in enumerate(part_refs):
        target = lax.rem(place_ref[1] + k, ranks)
        part_ref[...] = mixed_ref[pl.ds(pl.multiple_of(target * shard_len, shard_len), shard_len)]


def attend(place, ranks, length, qkv, early):
    _, rows, cols = qkv.shape
    count = rows // length
    heads = cols // HEAD
    shard_len = length // ranks
    one = lambda which: pl.BlockSpec((1, length, HEAD), lambda i, h, p: (which, i, h))
    part = pl.BlockSpec((shard_len, HEAD), lambda i, h, p: (i, h))
    *parts, logs = pl.pallas_call(
        functools.partial(attend_kernel, length // 2),
        grid_spec=pltpu.PrefetchScalarGridSpec(
            num_scalar_prefetch=1,
            grid=(count, heads),
            in_specs=[
                one(0),
                one(1),
                one(2),
                pl.BlockSpec((2, length, HEAD), lambda i, h, p: (0, i, h)),
            ],
            out_specs=[part] * ranks + [pl.BlockSpec((1, length, 1), lambda i, h, p: (i * heads + h, 0, 0))],
            scratch_shapes=[pltpu.VMEM((length, HEAD), BF)],
        ),
        out_shape=[jax.ShapeDtypeStruct((count * shard_len, cols), BF)] * ranks
        + [jax.ShapeDtypeStruct((count * heads, length, 1), F32)],
        compiler_params=pltpu.CompilerParams(vmem_limit_bytes=24 * MIB),
        cost_estimate=cost(
            flops=8 * length * length * cols,
            bytes_accessed=14 * length * cols,
            transcendentals=2 * length * length * heads,
        ),
        name="attend",
    )(place, qkv, qkv, qkv, early)
    return parts, logs


def hidden_kernel(ranks, place_ref, input_ref, gain_ref, weight_ref, *refs):
    part_refs, (hidden_ref, normed_ref, mixed_ref) = refs[:ranks], refs[ranks:]
    cols = part_refs[0].shape[1]
    hidden = input_ref[...].astype(F32)
    for k, part_ref in enumerate(part_refs):
        source = lax.rem(place_ref[1] + ranks - k, ranks)
        where = pl.ds(pl.multiple_of(source * cols, HEAD), cols)
        hidden = hidden + contract(part_ref[...], weight_ref[:, where], 1, 1)
        mixed_ref[:, where] = part_ref[...]
    hidden_ref[...] = hidden
    inv = lax.rsqrt(jnp.mean(hidden * hidden, axis=-1, keepdims=True) + EPSILON)
    normed_ref[...] = (hidden * inv * gain_ref[...]).astype(BF)


def finish_attention(place, inputs, gain, weight, parts):
    shard_len, width = inputs.shape
    ranks, cols = len(parts), parts[0].shape[1]
    whole = lambda shape: pl.BlockSpec(shape, lambda j, p: (0,) * len(shape))
    return pl.pallas_call(
        functools.partial(hidden_kernel, ranks),
        grid_spec=pltpu.PrefetchScalarGridSpec(
            num_scalar_prefetch=1,
            grid=(1,),
            in_specs=[
                whole((shard_len, width)),
                whole((1, width)),
                whole(weight.shape),
            ]
            + [whole((shard_len, cols))] * ranks,
            out_specs=[
                whole((shard_len, width)),
                whole((shard_len, width)),
                whole((shard_len, ranks * cols)),
            ],
        ),
        out_shape=[
            jax.ShapeDtypeStruct((shard_len, width), F32),
            jax.ShapeDtypeStruct((shard_len, width), BF),
            jax.ShapeDtypeStruct((shard_len, ranks * cols), BF),
        ],
        compiler_params=pltpu.CompilerParams(vmem_limit_bytes=40 * MIB),
        cost_estimate=cost(
            flops=2 * shard_len * width * width,
            bytes_accessed=2 * width * width + 12 * shard_len * width,
            transcendentals=0,
        ),
        name="finish_attention",
    )(place, inputs, gain, weight, *parts)


def grad_hidden_kernel(
    ranks,
    place_ref,
    own_ref,
    got_x_ref,
    last_y_ref,
    got_y_ref,
    last_x_ref,
    hidden_ref,
    cot_ref,
    gain_ref,
    weight_ref,
    grad_ref,
    low_ref,
    *part_refs,
):
    half = last_y_ref.shape[0]
    cols = part_refs[0].shape[1]
    for rows, got_ref, last_ref in (
        (slice(0, half), got_x_ref, last_y_ref),
        (slice(half, 2 * half), got_y_ref, last_x_ref),
    ):
        weighted = own_ref[rows].astype(F32) + got_ref[0].astype(F32) + last_ref[...].astype(F32)
        weighted = weighted * gain_ref[...]
        values = hidden_ref[rows]
        inv = lax.rsqrt(jnp.mean(values * values, axis=-1, keepdims=True) + EPSILON)
        inner = jnp.mean(weighted * values, axis=-1, keepdims=True)
        grad = inv * weighted - values * (inv * inv * inv * inner) + cot_ref[rows].astype(F32)
        grad_ref[rows] = grad
        low_ref[rows] = grad.astype(BF)
    for k, part_ref in enumerate(part_refs):
        target = lax.rem(place_ref[1] + k, ranks)
        where = pl.ds(pl.multiple_of(target * cols, HEAD), cols)
        part_ref[...] = contract(low_ref[...], weight_ref[:, where], 1, 0).astype(BF)


def begin_back(place, ranks, pieces, hidden, cotangent, gain, weight):
    shard_len, width = hidden.shape
    cols = weight.shape[1] // ranks
    half = shard_len // 2
    whole = lambda shape: pl.BlockSpec(shape, lambda j, p: (0,) * len(shape))
    first = pl.BlockSpec((1, half, width), lambda j, p: (0, 0, 0))
    grad, low, *parts = pl.pallas_call(
        functools.partial(grad_hidden_kernel, ranks),
        grid_spec=pltpu.PrefetchScalarGridSpec(
            num_scalar_prefetch=1,
            grid=(1,),
            in_specs=[
                whole((shard_len, width)),
                first,
                whole((half, width)),
                first,
                whole((half, width)),
                whole((shard_len, width)),
                whole((shard_len, width)),
                whole((1, width)),
                whole(weight.shape),
            ],
            out_specs=[whole((shard_len, width))] * 2 + [whole((shard_len, cols))] * ranks,
        ),
        out_shape=[
            jax.ShapeDtypeStruct((shard_len, width), F32),
            jax.ShapeDtypeStruct((shard_len, width), BF),
        ]
        + [jax.ShapeDtypeStruct((shard_len, cols), BF)] * ranks,
        compiler_params=pltpu.CompilerParams(vmem_limit_bytes=48 * MIB),
        cost_estimate=cost(
            flops=2 * shard_len * width * width,
            bytes_accessed=2 * width * width + 20 * shard_len * width,
            transcendentals=0,
        ),
        name="begin_back",
    )(place, *pieces, hidden, cotangent, gain, weight)
    return grad, low, parts


def attend_back_kernel(
    strip, place_ref, query_ref, key_ref, value_ref, early_ref, log_ref, cos_ref, sin_ref, *refs
):
    *part_refs, query_out, own_out, early_out, grad_ref = refs
    length = query_ref.shape[1]
    factor = HEAD ** (-0.5)
    ranks = len(part_refs)
    shard_len = length // ranks
    for k, part_ref in enumerate(part_refs):
        source = lax.rem(place_ref[1] + ranks - k, ranks)
        grad_ref[pl.ds(pl.multiple_of(source * shard_len, shard_len), shard_len)] = part_ref[...]

    def run(late):
        early_key_sum = early_value_sum = 0.0
        for first in range(length - strip, -1, -strip):
            end = first + strip
            query = query_ref[0, first:end]
            grad = grad_ref[first:end]
            log = log_ref[0, first:end]
            own, early = softmax_parts(query, key_ref[0, :end], early_ref[0], first, late)
            own = jnp.exp(own - log)
            own_grad = contract(grad, value_ref[0, :end], 1, 1)
            inner = jnp.sum(own_grad * own, axis=-1, keepdims=True)
            if late:
                early = jnp.exp(early - log)
                early_grad = contract(grad, early_ref[1], 1, 1)
                inner = inner + jnp.sum(early_grad * early, axis=-1, keepdims=True)
            own_low = (own * (own_grad - inner)).astype(BF)
            grad_query = contract(own_low, key_ref[0, :end], 1, 0)
            grad_key = contract(own_low, query, 0, 0) * factor
            grad_value = contract(own.astype(BF), grad, 0, 0)
            if first == length - strip:
                own_out[0] = grad_key
                own_out[1] = grad_value
            else:
                own_out[0, :end] += grad_key
                own_out[1, :end] += grad_value
            if late:
                early_low = (early * (early_grad - inner)).astype(BF)
                grad_query = grad_query + contract(early_low, early_ref[0], 1, 0)
                early_key_sum = early_key_sum + contract(early_low, query, 0, 0)
                early_value_sum = early_value_sum + contract(early.astype(BF), grad, 0, 0)
            grad_query = grad_query * factor
            query_out[first:end] = turned(
                grad_query, cos_ref[0, first:end], -sin_ref[0, first:end]
            ).astype(BF)
        if late:
            early_out[0] = (early_key_sum * factor).astype(BF)
            early_out[1] = early_value_sum.astype(BF)
        else:
            early_out[...] = jnp.zeros(early_out.shape, BF)

    @pl.when(place_ref[0] == 0)
    def _():
        run(False)

    @pl.when(place_ref[0] != 0)
    def _():
        run(True)


def attend_back(place, length, qkv, early, logs, parts, cosine, sine):
    _, rows, cols = qkv.shape
    count = rows // length
    heads, ranks = cols // HEAD, len(parts)
    one = lambda which: pl.BlockSpec((1, length, HEAD), lambda i, h, p: (which, i, h))
    pair = pl.BlockSpec((2, length, HEAD), lambda i, h, p: (0, i, h))
    table = pl.BlockSpec((1, length, HEAD), lambda i, h, p: (0, 0, 0))
    return pl.pallas_call(
        functools.partial(attend_back_kernel, length // 2),
        grid_spec=pltpu.PrefetchScalarGridSpec(
            num_scalar_prefetch=1,
            grid=(count, heads),
            in_specs=[
                one(0),
                one(1),
                one(2),
                pair,
                pl.BlockSpec((1, length, 1), lambda i, h, p: (i * heads + h, 0, 0)),
                table,
                table,
            ]
            + [pl.BlockSpec((length // ranks, HEAD), lambda i, h, p: (i, h))] * ranks,
            out_specs=[pl.BlockSpec((length, HEAD), lambda i, h, p: (i, h)), pair, pair],
            scratch_shapes=[pltpu.VMEM((length, HEAD), BF)],
        ),
        out_shape=[
            jax.ShapeDtypeStruct((rows, cols), BF),
            jax.ShapeDtypeStruct((2, rows, cols), F32),
            jax.ShapeDtypeStruct((2, rows, cols), BF),
        ],
        compiler_params=pltpu.CompilerParams(vmem_limit_bytes=32 * MIB),
        cost_estimate=cost(
            flops=20 * length * length * cols,
            bytes_accessed=28 * length * cols,
            transcendentals=2 * length * length * heads,
        ),
        name="attend_back",
    )(place, qkv, qkv, qkv, early, logs, cosine, sine, *parts)


def project_back_kernel(
    query_ref, own_ref, back_ref, cos_ref, sin_ref, weight_ref, low_ref, out_ref
):
    cols = query_ref.shape[1]

    @pl.when(pl.program_id(1) == 0)
    def _():
        low_ref[:, :cols] = query_ref[...]
        keys = own_ref[0] + back_ref[0].astype(F32)
        cosine, sine = cos_ref[0], -sin_ref[0]
        for head in range(cols // HEAD):
            part = slice(head * HEAD, (head + 1) * HEAD)
            into = slice(cols + head * HEAD, cols + (head + 1) * HEAD)
            low_ref[:, into] = turned(keys[:, part], cosine, sine).astype(BF)
        low_ref[:, 2 * cols :] = (own_ref[1] + back_ref[1].astype(F32)).astype(BF)

    result = contract(low_ref[...], weight_ref[...], 1, 1).astype(BF)
    out_ref[...] = result.reshape(out_ref.shape)


def project_back(count, ranks, grad_query, grad_own, back, cosine, sine, weight):
    rows, cols = grad_query.shape
    length = rows // count
    width = weight.shape[0]
    step = width // 3
    pair = pl.BlockSpec((2, length, cols), lambda i, j: (0, i, 0))
    table = pl.BlockSpec((1, length, HEAD), lambda i, j: (0, 0, 0))
    return pl.pallas_call(
        project_back_kernel,
        grid=(count, 3),
        in_specs=[
            pl.BlockSpec((length, cols), lambda i, j: (i, 0)),
            pair,
            pair,
            table,
            table,
            pl.BlockSpec((step, 3 * cols), lambda i, j: (j, 0)),
        ],
        out_specs=[
            pl.BlockSpec((length, 3 * cols), lambda i, j: (i, 0)),
            pl.BlockSpec((ranks, 1, length // ranks, step), lambda i, j: (0, i, 0, j)),
        ],
        out_shape=[
            jax.ShapeDtypeStruct((rows, 3 * cols), BF),
            jax.ShapeDtypeStruct((ranks, count, length // ranks, width), BF),
        ],
        compiler_params=pltpu.CompilerParams(vmem_limit_bytes=32 * MIB),
        cost_estimate=cost(
            flops=6 * rows * width * cols,
            bytes_accessed=6 * width * cols + 18 * rows * cols + 2 * rows * width,
            transcendentals=0,
        ),
        name="project_back",
    )(grad_query, grad_own, back, cosine, sine, weight)


def gelu_both(values):
    scale = (2.0 / jnp.pi) ** 0.5
    square = values * values
    tanh = jnp.tanh(scale * values * (1.0 + 0.044715 * square))
    half = 0.5 * (1.0 + tanh)
    slope = half + 0.5 * values * (1.0 - tanh * tanh) * scale * (1.0 + 3 * 0.044715 * square)
    return values * half, slope


def stack_units(first, own_ref, other_ref, which, into):
    ranks, _, blocks, sub, _ = own_ref.shape

    def fill(source):
        for block in range(blocks):
            for rank in range(ranks):
                row = (block * ranks + rank) * sub
                into[row : row + sub] = source[rank, which, block]

    @pl.when(first)
    def _():
        fill(own_ref)

    @pl.when(jnp.logical_not(first))
    def _():
        fill(other_ref)


def feed_kernel(count, place_ref, cot_ref, own_ref, other_ref, *refs):
    rows_in, refs = refs[: 5 * count], refs[5 * count :]
    grads_out, (rows_ref, down_ref, act_ref, pre_ref, up_ref, sum_ref) = (
        refs[: 5 * count],
        refs[5 * count :],
    )
    step = pl.program_id(0)
    half = up_ref.shape[0]
    shard_len = rows_ref.shape[1] // count
    part = shard_len // 2
    ctx, mine = place_ref[0], place_ref[2]

    for turn_of, at in ((0, 0), (1, LEVELS)):

        @pl.when(step == at)
        def _(turn_of=turn_of):
            stack_units(ctx == turn_of, own_ref, other_ref, 0, up_ref)
            stack_units(ctx == turn_of, own_ref, other_ref, 1, down_ref.at[0])

    for k in range(LEVELS):

        @pl.when((step < LEVELS) & (jnp.bitwise_xor(mine, k) == step))
        def _(k=k):
            for i in range(count):
                pieces = rows_in[5 * i : 5 * i + 5]
                rows = slice(i * shard_len, (i + 1) * shard_len)
                if k < LEVELS - 1:
                    rows_ref[0, rows] = pieces[k][...]
                else:
                    rows_ref[0, rows.start : rows.start + part] = pieces[3][...]
                    rows_ref[0, rows.start + part : rows.stop] = pieces[4][...]

    def run(used):
        upped = contract(rows_ref[0], up_ref[:used], 1, 1)
        activated, slope = gelu_both(upped)
        grad_act = contract(cot_ref[0], down_ref[0, :used], 1, 1)
        grad_upped = (grad_act * slope).astype(BF)
        act_ref[0, :, :used] = activated.astype(BF)
        pre_ref[0, :, :used] = grad_upped
        return contract(grad_upped, up_ref[:used], 1, 0)

    for one in range(LEVELS - 2):

        @pl.when(step == one)
        def _(one=one):
            sum_ref[...] = run(half // 2 ** (LEVELS - 2 - one))

    @pl.when(step >= LEVELS - 2)
    def _():
        result = run(half)

        @pl.when(step < LEVELS)
        def _():
            sum_ref[...] = result

        @pl.when(step == LEVELS)
        def _():
            sum_ref[...] += result

    level = jnp.minimum(step, LEVELS - 1)
    for k in range(LEVELS):

        @pl.when((step != LEVELS - 1) & (jnp.bitwise_xor(mine, k) == level))
        def _(k=k):
            for i in range(count):
                keep, keep_x, keep_y, send_x, send_y = grads_out[5 * i : 5 * i + 5]
                first = sum_ref[i * shard_len : i * shard_len + part].astype(BF)
                second = sum_ref[i * shard_len + part : (i + 1) * shard_len].astype(BF)
                if k == 0:
                    keep[:part] = first
                    keep[part:] = second
                elif k == 1:
                    send_x[0] = first
                    keep_x[...] = second
                elif k == 2:
                    keep_y[...] = first
                    send_y[0] = second
                else:
                    send_x[1] = first
                    send_y[1] = second


def feed(place, rows, cot, own, other):
    count = len(rows)
    _, length, width = cot.shape
    half = own.shape[0] * own.shape[2] * own.shape[3]
    shard_len = length // count
    part = shard_len // 2
    whole = lambda shape: pl.BlockSpec(
        shape, lambda s, p: (0,) * len(shape), pipeline_mode=pl.Buffered(1)
    )
    fixed = lambda shape: pl.BlockSpec(shape, lambda s, p: (0,) * len(shape))
    by_level = pl.BlockSpec((1, length, width), lambda s, p: (jnp.minimum(s, LEVELS - 1), 0, 0))
    by_half = pl.BlockSpec((1, half, width), lambda s, p: (s // LEVELS, 0, 0))
    by_step = pl.BlockSpec((1, length, half), lambda s, p: (s, 0, 0))
    pieces = [
        (shard_len, width),
        (part, width),
        (part, width),
        (2, part, width),
        (2, part, width),
    ]
    *grads, rows_all, down, activated, before = pl.pallas_call(
        functools.partial(feed_kernel, count),
        grid_spec=pltpu.PrefetchScalarGridSpec(
            num_scalar_prefetch=1,
            grid=(LEVELS + 1,),
            in_specs=[by_level, whole(own.shape), whole(own.shape)]
            + [whole(piece.shape) for one in rows for piece in one],
            out_specs=[fixed(shape) for shape in pieces] * count
            + [by_level, by_half, by_step, by_step],
            scratch_shapes=[pltpu.VMEM((half, width), BF), pltpu.VMEM((length, width), F32)],
        ),
        out_shape=[jax.ShapeDtypeStruct(shape, BF) for shape in pieces] * count
        + [
            jax.ShapeDtypeStruct(cot.shape, BF),
            jax.ShapeDtypeStruct((2, half, width), BF),
            jax.ShapeDtypeStruct((LEVELS + 1, length, half), BF),
            jax.ShapeDtypeStruct((LEVELS + 1, length, half), BF),
        ],
        compiler_params=pltpu.CompilerParams(vmem_limit_bytes=58 * MIB),
        cost_estimate=cost(
            flops=24 * length * width * half,
            bytes_accessed=24 * length * width + 8 * half * width + 20 * length * half,
            transcendentals=5 * length * half,
        ),
        name="feed",
    )(place, cot, own, other, *[piece for one in rows for piece in one])
    grads = [grads[5 * i : 5 * i + 5] for i in range(count)]
    return grads, rows_all, down, activated, before


def feed_weights_kernel(
    place_ref,
    rows_ref,
    cot_ref,
    act_ref,
    pre_ref,
    down_ref,
    keep_ref,
    send_ref,
    out_ref,
    up_sum,
    down_sum,
    out_sum,
    stage,
    sem,
):
    step = pl.program_id(0)
    half = down_ref.shape[1]
    ranks, _, blocks, sub, _ = stage.shape

    def add(used, fresh):
        up_part = contract(pre_ref[0, :, :used], rows_ref[0], 0, 0)
        down_part = contract(act_ref[0, :, :used], cot_ref[0], 0, 0)
        if fresh == used:
            up_sum[:used] = up_part
            down_sum[:used] = down_part
        else:
            up_sum[:fresh] += up_part[:fresh]
            down_sum[:fresh] += down_part[:fresh]
            if fresh < used:
                up_sum[fresh:used] = up_part[fresh:]
                down_sum[fresh:used] = down_part[fresh:]
        return contract(act_ref[0, :, :used], down_ref[0, :used], 1, 0)

    def store(which):
        for block in range(blocks):
            for rank in range(ranks):
                first = (block * ranks + rank) * sub
                stage[rank, 0, block] = up_sum[first : first + sub].astype(BF)
                stage[rank, 1, block] = down_sum[first : first + sub].astype(BF)

        @pl.when(place_ref[0] == which)
        def _():
            copy = pltpu.make_async_copy(stage, keep_ref, sem)
            copy.start()
            copy.wait()

        @pl.when(place_ref[0] != which)
        def _():
            copy = pltpu.make_async_copy(stage, send_ref, sem)
            copy.start()
            copy.wait()

    for one in range(LEVELS - 1):

        @pl.when(step == one)
        def _(one=one):
            used = half // 2 ** (LEVELS - 2 - one)
            out_ref[0] = add(used, used if one == 0 else used // 2).astype(BF)

    @pl.when(step == LEVELS - 1)
    def _():
        up_sum[...] += contract(pre_ref[0], rows_ref[0], 0, 0)
        down_sum[...] += contract(act_ref[0], cot_ref[0], 0, 0)
        out_sum[...] = contract(act_ref[0], down_ref[0], 1, 0)
        store(0)

    @pl.when(step == LEVELS)
    def _():
        out_ref[0] = (out_sum[...] + add(half, half)).astype(BF)
        store(1)


def feed_weights(place, rows, cot, activated, before, down, ranks, blocks):
    _, length, width = rows.shape
    half = down.shape[1]
    sub = half // (ranks * blocks)
    by_level = pl.BlockSpec((1, length, width), lambda s, p: (jnp.minimum(s, LEVELS - 1), 0, 0))
    by_half = pl.BlockSpec((1, half, width), lambda s, p: (s // LEVELS, 0, 0))
    by_step = pl.BlockSpec((1, length, half), lambda s, p: (s, 0, 0))
    shape = (ranks, 2, blocks, sub, width)
    return pl.pallas_call(
        feed_weights_kernel,
        grid_spec=pltpu.PrefetchScalarGridSpec(
            num_scalar_prefetch=1,
            grid=(LEVELS + 1,),
            in_specs=[by_level, by_level, by_step, by_step, by_half],
            out_specs=[
                pl.BlockSpec(memory_space=pl.ANY),
                pl.BlockSpec(memory_space=pl.ANY),
                by_level,
            ],
            scratch_shapes=[
                pltpu.VMEM((half, width), F32),
                pltpu.VMEM((half, width), F32),
                pltpu.VMEM((length, width), F32),
                pltpu.VMEM(shape, BF),
                pltpu.SemaphoreType.DMA(()),
            ],
        ),
        out_shape=[
            jax.ShapeDtypeStruct(shape, BF),
            jax.ShapeDtypeStruct(shape, BF),
            jax.ShapeDtypeStruct(rows.shape, BF),
        ],
        compiler_params=pltpu.CompilerParams(vmem_limit_bytes=56 * MIB),
        cost_estimate=cost(
            flops=24 * length * width * half,
            bytes_accessed=24 * length * width + 12 * half * width + 20 * length * half,
            transcendentals=0,
        ),
        name="feed_weights",
    )(place, rows, cot, activated, before, down)


def outer_kernel(count, *refs):
    lefts, rights, out_ref = refs[:count], refs[count : 2 * count], refs[-1]
    total = contract(lefts[0][...], rights[0][...], 0, 0)
    for left, right in zip(lefts[1:], rights[1:]):
        total = total + contract(left[...], right[...], 0, 0)
    out_ref[...] = total.astype(BF)


def outer(lefts, rights):
    rows, m = lefts[0].shape
    n = rights[0].shape[1]
    count = len(lefts)
    step = m // 4
    return pl.pallas_call(
        functools.partial(outer_kernel, count),
        grid=(4,),
        in_specs=[pl.BlockSpec((rows, step), lambda j: (0, j))] * count
        + [pl.BlockSpec((rows, n), lambda j: (0, 0))] * count,
        out_specs=pl.BlockSpec((step, n), lambda j: (j, 0)),
        out_shape=jax.ShapeDtypeStruct((m, n), BF),
        compiler_params=pltpu.CompilerParams(vmem_limit_bytes=32 * MIB),
        cost_estimate=cost(
            flops=2 * count * rows * m * n,
            bytes_accessed=2 * (count * rows * (m + n) + m * n),
            transcendentals=0,
        ),
        name="outer",
    )(*lefts, *rights)


def inverse_rms(values):
    return lax.rsqrt(jnp.mean(values * values, axis=-1, keepdims=True) + EPSILON)


def norm_back(values, inv_rms, weighted):
    return inv_rms * weighted - values * (inv_rms * inv_rms * inv_rms) * jnp.mean(
        weighted * values, axis=-1, keepdims=True
    )


def rotation(positions, head_size):
    half_size = head_size // 2
    frequency = 10000.0 ** (-jnp.arange(half_size, dtype=jnp.float32) / half_size)
    angles = positions.astype(jnp.float32)[:, None] * frequency[None, :]
    cosine, sine = jnp.cos(angles), jnp.sin(angles)
    cosine = jnp.concatenate([cosine, cosine], -1)
    sine = jnp.concatenate([-sine, sine], -1)
    return (
        jnp.stack([cosine, jnp.ones_like(cosine)]),
        jnp.stack([sine, jnp.zeros_like(sine)]),
    )


def product(equation, left, right):
    return jnp.einsum(equation, left, right, preferred_element_type=F32)


def local(inputs, w_query, w_key, w_value, w_out, w_up, w_down, gain_attn, gain_ffn, cotangent):
    count, shard_len, width = inputs.shape
    own_rows = count * shard_len
    ranks = lax.axis_size("mp")
    length_half = shard_len * ranks
    level = lax.axis_index("dp") % LEVELS
    ctx = lax.axis_index("ctx")
    rank = lax.axis_index("mp")
    part_rows, head_cols = w_query.shape
    place = jnp.stack([ctx, rank, level]).astype(jnp.int32)

    inputs_flat = inputs.reshape(own_rows, width)
    cot_flat = cotangent.reshape(own_rows, width)
    rows_all = lax.all_gather(inputs_flat, "mp", axis=0)
    out_found = [turn(w_out, "mp", k) for k in range(1, ranks)]

    gains = team_gather(level_gather_small(jnp.stack([gain_attn, gain_ffn]), level))
    gains = pair_gather(gains.reshape(-1, 2, part_rows), ctx, 1)
    gains = gains.transpose(2, 0, 1, 3).reshape(2, 1, width).astype(F32)
    gain_first, gain_second = gains[0], gains[1]

    qkv_full = model_gather(
        after(jnp.concatenate([w_query, w_key, w_value], axis=1), *out_found), level, ctx
    )
    blocks, unit_cols = w_up.shape[1:]
    sub = unit_cols // LEVELS
    half_blocks = blocks // 2
    up_turned = w_up.transpose(1, 2, 0)
    halves = [
        jnp.stack([up_turned[b : b + half_blocks], w_down[b : b + half_blocks]])
        for b in (0, half_blocks)
    ]
    own_part, sent_part = pair_split(halves[0], halves[1], ctx)
    pair = jnp.concatenate(
        [jnp.where(ctx == 0, own_part, sent_part), jnp.where(ctx == 0, sent_part, own_part)], -1
    )
    pair = pair.reshape(2, half_blocks, LEVELS, sub, 2 * part_rows).transpose(2, 0, 1, 3, 4)
    swapped = team_gather(level_swap(pair, level))
    swapped = side_by_side(swapped.reshape(-1, 2, half_blocks, sub, 2 * part_rows))
    cot_pieces = level_pieces(after(cot_flat, swapped))
    ranked = lax.all_gather(swapped, "mp", axis=0)
    positions = ctx * length_half + jnp.arange(length_half, dtype=jnp.int32)
    cosine, sine = rotation(positions, HEAD)
    qkv, normed = project(
        count, shard_len, rows_all, after(gain_first, *cot_pieces), qkv_full, cosine, sine
    )
    cot_rows = level_join(after(cot_pieces, qkv), level)
    out_parts = put(jnp.zeros((ranks,) + w_out.shape, BF), w_out, rank)
    for k in range(1, ranks):
        out_parts = put(out_parts, out_found[k - 1], (rank + ranks - k) % ranks)
    out_parts = after(out_parts.reshape(-1, part_rows).T, cot_pieces[3])
    out_full = model_gather(out_parts, level, ctx)
    early = lax.ppermute(qkv[1:], "ctx", [(0, 1)])
    parts, logs = attend(place, ranks, length_half, qkv, early)
    hidden, normed_two, mixed_own = finish_attention(
        place, inputs_flat, gain_second, out_full, rank_swap(parts)
    )

    ranked = after(ranked, hidden)
    (opened,), rows_second, down_mine, activated, before = feed(
        place, [level_pieces(normed_two)], cot_rows, ranked, flip(ranked, "ctx", 1)
    )
    own, by_x, by_y, got_x, got_y = opened
    got_x, got_y = flip(got_x, "dp", 1), flip(got_y, "dp", 2)

    grad_kept, grad_sent, results = feed_weights(
        place, rows_second, cot_rows, activated, before, down_mine, ranks, half_blocks
    )
    grad_sent = after(grad_sent, got_x, got_y)
    grad_ffn = (grad_kept.astype(F32) + flip(grad_sent, "ctx", 1).astype(F32)).astype(BF)
    grad_ffn_low = [grad_ffn[:, kind].reshape(-1, width) for kind in range(2)]
    grad_ffn = [
        lax.psum_scatter(one, "mp", scatter_dimension=0, tiled=True) for one in grad_ffn_low
    ]

    last_y, last_x = level_scatter_last(by_x, by_y, got_x, got_y)
    own = after(own, *grad_ffn_low)
    grad_hidden, grad_low, parts = begin_back(
        place, ranks, (own, got_x, last_y, got_y, last_x), hidden, cot_flat, gain_second, out_full
    )
    parts = rank_swap(parts)
    grad_query, grad_own, grad_early = attend_back(
        place, length_half, qkv, early, logs, parts, cosine, sine
    )
    grad_early = after(grad_early, grad_ffn[0])
    back = lax.ppermute(grad_early, "ctx", [(1, 0)])
    grad_qkv, grad_first = project_back(
        count, ranks, grad_query, grad_own, back, cosine, sine, qkv_full
    )
    grad_first = after(grad_first, grad_ffn[1])
    grad_ffn = after(grad_ffn, grad_first)
    grad_first = lax.psum_scatter(
        grad_first.reshape(-1, width), "mp", scatter_dimension=0, tiled=True
    )

    results_open = after(level_scatter_open(after(results, grad_low), level), grad_qkv)
    result = level_sum(results_open, level_scatter_last(*results_open[1:]))
    outputs = (hidden + result).astype(BF).reshape(inputs.shape)

    grad_ffn = jnp.stack(grad_ffn).reshape(2, half_blocks, sub, width)
    grad_ffn = jnp.stack(jnp.split(grad_ffn, width // (2 * part_rows), axis=-1))
    grad_ffn = team_scatter(grad_ffn.reshape((-1, LEVELS) + grad_ffn.shape[1:]))
    grad_ffn = level_swap(grad_ffn, level).transpose(1, 2, 0, 3, 4)
    grad_ffn = grad_ffn.reshape(2, half_blocks, unit_cols, 2 * part_rows)
    own_part, sent_part = pair_split(grad_ffn[..., :part_rows], grad_ffn[..., part_rows:], ctx)
    grad_ffn = jnp.concatenate(
        [jnp.where(ctx == 0, own_part, sent_part), jnp.where(ctx == 0, sent_part, own_part)], 1
    ).astype(F32)
    grad_up_out = grad_ffn[0].transpose(2, 0, 1)
    grad_down_out = grad_ffn[1]
    gain_ffn_part = jnp.sum(grad_up_out * w_up.astype(F32), axis=(1, 2)) / gain_ffn.astype(F32)

    grad_qkv_w = outer([normed], [grad_qkv])
    grad_qkv_w = model_scatter(grad_qkv_w, level, ctx, part_rows)
    originals = jnp.concatenate([w_query, w_key, w_value], axis=1).astype(F32)
    gain_attn_part = jnp.sum(grad_qkv_w * originals, axis=1) / gain_attn.astype(F32)
    gain_grads = jnp.stack([gain_attn_part, gain_ffn_part])
    gain_grads = gain_grads + sum([turn(gain_grads, "mp", k) for k in range(1, ranks)])

    grad_out_w = outer([after(grad_low, grad_qkv)], [mixed_own])
    grad_out_w = model_scatter(grad_out_w, level, ctx, part_rows).astype(BF)
    grad_out_w = jnp.stack(jnp.split(grad_out_w, ranks, axis=1))
    grad_out_out = take(grad_out_w, rank).astype(F32)
    for k in range(1, ranks):
        grad_out_out = grad_out_out + turn(take(grad_out_w, (rank + k) % ranks), "mp", k).astype(F32)
    grad_out_out = grad_out_out.T

    grad_first = after(grad_first, grad_out_out, gain_grads, outputs, grad_qkv_w, grad_up_out, grad_down_out)
    inputs_f = inputs.astype(F32)
    input_grads = grad_hidden.reshape(inputs.shape) + norm_back(
        inputs_f,
        inverse_rms(inputs_f),
        gain_first * grad_first.reshape(inputs.shape).astype(F32),
    )
    return (
        outputs,
        input_grads,
        grad_qkv_w[:, :head_cols],
        grad_qkv_w[:, head_cols : 2 * head_cols],
        grad_qkv_w[:, 2 * head_cols :],
        grad_out_out,
        grad_up_out,
        grad_down_out,
        gain_grads[0],
        gain_grads[1],
    )


def solution(mesh):
    in_specs = (
        P("dp", ("ctx", "mp"), None),
        P(("dp", "ctx"), "mp"),
        P(("dp", "ctx"), "mp"),
        P(("dp", "ctx"), "mp"),
        P("mp", ("dp", "ctx")),
        P(("dp", "ctx"), None, "mp"),
        P(None, "mp", ("dp", "ctx")),
        P(("dp", "ctx")),
        P(("dp", "ctx")),
        P("dp", ("ctx", "mp"), None),
    )
    out_specs = (
        P("dp", ("ctx", "mp"), None),
        P("dp", ("ctx", "mp"), None),
        P(("dp", "ctx"), "mp"),
        P(("dp", "ctx"), "mp"),
        P(("dp", "ctx"), "mp"),
        P("mp", ("dp", "ctx")),
        P(("dp", "ctx"), None, "mp"),
        P(None, "mp", ("dp", "ctx")),
        P(("dp", "ctx")),
        P(("dp", "ctx")),
    )
    return jax.shard_map(local, mesh=mesh, in_specs=in_specs, out_specs=out_specs, check_vma=False)
```

```python
import functools

import jax
import jax.numpy as jnp
from jax import lax
from jax.experimental import pallas as pl
from jax.experimental.pallas import tpu as pltpu
from jax.sharding import PartitionSpec as P

HEAD = 128
LEVELS = 4
EPSILON = 1e-06
NEGATIVE = -1e30
BF = jnp.bfloat16
F32 = jnp.float32
MIB = 1 << 20
HURRY = 16


def flip(shard, axis, bit):
    devices = lax.axis_size(axis)
    return lax.ppermute(shard, axis, [(i, i ^ bit) for i in range(devices)])


def turn(shard, axis, by):
    devices = lax.axis_size(axis)
    return lax.ppermute(shard, axis, [(i, (i + by) % devices) for i in range(devices)])


def after(values, *others):
    return lax.optimization_barrier((values,) + others)[0]


def put(buffer, part, index, dim=0):
    starts = [0] * buffer.ndim
    starts[dim] = index
    return lax.dynamic_update_slice(buffer, jnp.expand_dims(part, dim), tuple(starts))


def take(buffer, index, dim=0):
    return lax.dynamic_index_in_dim(buffer, index, dim, keepdims=False)


def side_by_side(parts):
    return jnp.concatenate([parts[k] for k in range(parts.shape[0])], axis=-1)


def pack(part, width):
    rows, cols = part.shape
    return side_by_side(part.reshape(width // cols, -1, cols))


def unpack(packed, cols):
    strips = packed.shape[1] // cols
    return jnp.concatenate([packed[:, k * cols : (k + 1) * cols] for k in range(strips)], 0)


def rank_swap(parts):
    return [parts[0]] + [turn(parts[k], "mp", k) for k in range(1, len(parts))]


def level_pieces(part):
    half = part.shape[0] // 2
    from_x = flip(part, "dp", 1)
    from_y = flip(part, "dp", 2)
    return part, from_x, from_y, flip(from_x[:half], "dp", 2), flip(from_y[half:], "dp", 1)


def level_gather(part, mine):
    return level_join(level_pieces(part), mine)


def level_join(pieces, mine):
    part, from_x, from_y, low_half, high_half = pieces
    whole = put(jnp.zeros((LEVELS,) + part.shape, part.dtype), part, mine)
    whole = put(whole, from_x, mine ^ 1)
    whole = put(whole, from_y, mine ^ 2)
    return put(whole, jnp.concatenate([low_half, high_half], 0), mine ^ 3)


def level_gather_small(part, mine):
    whole = put(jnp.zeros((LEVELS,) + part.shape, part.dtype), part, mine)
    for k in range(1, LEVELS):
        whole = put(whole, flip(part, "dp", k), mine ^ k)
    return whole


def level_scatter_open(parts, mine):
    half = parts.shape[1] // 2
    own, by_x, by_y, by_xy = (take(parts, mine ^ k) for k in range(LEVELS))
    got_x = flip(jnp.stack([by_x[:half], by_xy[:half]]), "dp", 1)
    got_y = flip(jnp.stack([by_y[half:], by_xy[half:]]), "dp", 2)
    return own, by_x[half:], by_y[:half], got_x, got_y


def level_scatter_last(by_x, by_y, got_x, got_y):
    send_y = (by_y.astype(F32) + got_x[1].astype(F32)).astype(by_y.dtype)
    send_x = (by_x.astype(F32) + got_y[1].astype(F32)).astype(by_x.dtype)
    return flip(send_y, "dp", 2), flip(send_x, "dp", 1)


def level_scatter(parts, mine):
    opened = level_scatter_open(parts, mine)
    return level_sum(opened, level_scatter_last(*opened[1:]))


def level_sum(opened, last):
    own, _, by_y, got_x, got_y = opened
    last_y, last_x = last
    half = by_y.shape[0]
    first = own[:half].astype(F32) + got_x[0].astype(F32) + last_y.astype(F32)
    second = own[half:].astype(F32) + got_y[0].astype(F32) + last_x.astype(F32)
    return jnp.concatenate([first, second], 0)


def level_swap(parts, mine):
    whole = put(jnp.zeros(parts.shape, parts.dtype), take(parts, mine), mine)
    for k in range(1, LEVELS):
        whole = put(whole, flip(take(parts, mine ^ k), "dp", k), mine ^ k)
    return whole


def teams(devices):
    return [list(range(level, devices, LEVELS)) for level in range(LEVELS)]


def team_gather(part):
    devices = lax.axis_size("dp")
    if devices == LEVELS:
        return part[None]
    return lax.all_gather(part, "dp", axis=0, axis_index_groups=teams(devices))


def team_scatter(parts):
    devices = lax.axis_size("dp")
    if devices == LEVELS:
        return parts[0]
    return lax.psum_scatter(
        parts, "dp", scatter_dimension=0, axis_index_groups=teams(devices), tiled=False
    )


def pair_gather(part, mine, dim=0):
    other = flip(part, "ctx", 1)
    shape = part.shape[:dim] + (2,) + part.shape[dim:]
    return put(put(jnp.zeros(shape, part.dtype), part, mine, dim), other, 1 - mine, dim)


def pair_split(first, second, mine):
    own = jnp.where(mine == 0, first, second)
    return own, flip(jnp.where(mine == 0, second, first), "ctx", 1)


def pair_scatter(parts, mine, dim):
    other = flip(take(parts, 1 - mine, dim), "ctx", 1)
    return take(parts, mine, dim).astype(F32) + other.astype(F32)


def model_gather(part, level, ctx):
    rows, width = part.shape
    whole = team_gather(level_gather(part, level))
    whole = pair_gather(whole.reshape(-1, rows, width), ctx, 1)
    return whole.reshape(-1, width)


def model_scatter(grad, level, ctx, rows):
    width = grad.shape[1]
    parts = grad.reshape(-1, 2, rows, width)
    parts = pair_scatter(parts, ctx, 1).astype(grad.dtype)
    parts = team_scatter(parts.reshape(-1, LEVELS, rows, width))
    return level_scatter(parts, level)


def cost(flops, bytes_accessed, transcendentals):
    return pl.CostEstimate(
        flops=flops // HURRY,
        bytes_accessed=bytes_accessed // HURRY,
        transcendentals=transcendentals // HURRY,
    )


def contract(left, right, left_dim, right_dim):
    return lax.dot_general(
        left, right, (((left_dim,), (right_dim,)), ((), ())), preferred_element_type=F32
    )


def turned(values, cosine, sine):
    return values * cosine + pltpu.roll(values, HEAD // 2, 1) * sine


def project_kernel(rows_ref, gain_ref, weight_ref, cos_ref, sin_ref, out_ref, normed_ref):
    @pl.when(pl.program_id(1) == 0)
    def _():
        values = rows_ref[...].reshape(normed_ref.shape).astype(F32)
        inv = lax.rsqrt(jnp.mean(values * values, axis=-1, keepdims=True) + EPSILON)
        normed_ref[...] = (values * inv * gain_ref[...]).astype(BF)

    values = contract(normed_ref[...], weight_ref[...], 1, 0)
    cosine, sine = cos_ref[0], sin_ref[0]
    for head in range(values.shape[1] // HEAD):
        cols = slice(head * HEAD, (head + 1) * HEAD)
        out_ref[0, :, cols] = turned(values[:, cols], cosine, sine).astype(BF)


def project(count, shard_len, rows, gain, weight, cosine, sine):
    ranks, _, width = rows.shape
    length = ranks * shard_len
    cols = weight.shape[1] // 3
    table = pl.BlockSpec((1, length, HEAD), lambda i, j: (j // 2, 0, 0))
    return pl.pallas_call(
        project_kernel,
        grid=(count, 3),
        in_specs=[
            pl.BlockSpec((ranks, shard_len, width), lambda i, j: (0, i, 0)),
            pl.BlockSpec((1, width), lambda i, j: (0, 0)),
            pl.BlockSpec((width, cols), lambda i, j: (0, j)),
            table,
            table,
        ],
        out_specs=[
            pl.BlockSpec((1, length, cols), lambda i, j: (j, i, 0)),
            pl.BlockSpec((length, width), lambda i, j: (i, 0)),
        ],
        out_shape=[
            jax.ShapeDtypeStruct((3, count * length, cols), BF),
            jax.ShapeDtypeStruct((count * length, width), BF),
        ],
        compiler_params=pltpu.CompilerParams(vmem_limit_bytes=24 * MIB),
        cost_estimate=cost(
            flops=6 * length * width * cols,
            bytes_accessed=4 * length * width + 6 * width * cols + 6 * length * cols,
            transcendentals=0,
        ),
        name="project",
    )(rows, gain, weight, cosine, sine)


def softmax_parts(query, key_own, key_early, first, late):
    factor = HEAD ** (-0.5)
    own = contract(query, key_own, 1, 1) * factor
    row_ids = first + lax.broadcasted_iota(jnp.int32, own.shape, 0)
    col_ids = lax.broadcasted_iota(jnp.int32, own.shape, 1)
    own = jnp.where(col_ids <= row_ids, own, NEGATIVE)
    early = contract(query, key_early, 1, 1) * factor if late else None
    return own, early


def attend_kernel(strip, place_ref, query_ref, key_ref, value_ref, early_ref, *refs):
    *part_refs, log_ref, mixed_ref = refs
    length = query_ref.shape[1]
    ranks = len(part_refs)
    shard_len = length // ranks

    def run(late):
        for first in range(0, length, strip):
            end = first + strip
            own, early = softmax_parts(
                query_ref[0, first:end], key_ref[0, :end], early_ref[0], first, late
            )
            largest = jnp.max(own, axis=-1, keepdims=True)
            if late:
                largest = jnp.maximum(largest, jnp.max(early, axis=-1, keepdims=True))
            own = jnp.exp(own - largest)
            total = jnp.sum(own, axis=-1, keepdims=True)
            if late:
                early = jnp.exp(early - largest)
                total = total + jnp.sum(early, axis=-1, keepdims=True)
            inverse = 1.0 / total
            mixed = contract((own * inverse).astype(BF), value_ref[0, :end], 1, 0)
            if late:
                mixed = mixed + contract((early * inverse).astype(BF), early_ref[1], 1, 0)
            mixed_ref[first:end] = mixed.astype(BF)
            log_ref[0, first:end] = largest + jnp.log(total)

    @pl.when(place_ref[0] == 0)
    def _():
        run(False)

    @pl.when(place_ref[0] != 0)
    def _():
        run(True)

    for k, part_ref in enumerate(part_refs):
        target = lax.rem(place_ref[1] + k, ranks)
        part_ref[...] = mixed_ref[pl.ds(pl.multiple_of(target * shard_len, shard_len), shard_len)]


def attend(place, ranks, length, qkv, early):
    _, rows, cols = qkv.shape
    count = rows // length
    heads = cols // HEAD
    shard_len = length // ranks
    one = lambda which: pl.BlockSpec((1, length, HEAD), lambda i, h, p: (which, i, h))
    part = pl.BlockSpec((shard_len, HEAD), lambda i, h, p: (i, h))
    *parts, logs = pl.pallas_call(
        functools.partial(attend_kernel, length),
        grid_spec=pltpu.PrefetchScalarGridSpec(
            num_scalar_prefetch=1,
            grid=(count, heads),
            in_specs=[
                one(0),
                one(1),
                one(2),
                pl.BlockSpec((2, length, HEAD), lambda i, h, p: (0, i, h)),
            ],
            out_specs=[part] * ranks + [pl.BlockSpec((1, length, 1), lambda i, h, p: (i * heads + h, 0, 0))],
            scratch_shapes=[pltpu.VMEM((length, HEAD), BF)],
        ),
        out_shape=[jax.ShapeDtypeStruct((count * shard_len, cols), BF)] * ranks
        + [jax.ShapeDtypeStruct((count * heads, length, 1), F32)],
        compiler_params=pltpu.CompilerParams(vmem_limit_bytes=24 * MIB),
        cost_estimate=cost(
            flops=8 * length * length * cols,
            bytes_accessed=14 * length * cols,
            transcendentals=2 * length * length * heads,
        ),
        name="attend",
    )(place, qkv, qkv, qkv, early)
    return parts, logs


def hidden_kernel(ranks, place_ref, input_ref, gain_ref, weight_ref, *refs):
    part_refs, (hidden_ref, normed_ref, mixed_ref) = refs[:ranks], refs[ranks:]
    cols = part_refs[0].shape[1]
    hidden = input_ref[...].astype(F32)
    for k, part_ref in enumerate(part_refs):
        source = lax.rem(place_ref[1] + ranks - k, ranks)
        where = pl.ds(pl.multiple_of(source * cols, HEAD), cols)
        hidden = hidden + contract(part_ref[...], weight_ref[:, where], 1, 1)
        mixed_ref[:, where] = part_ref[...]
    hidden_ref[...] = hidden
    inv = lax.rsqrt(jnp.mean(hidden * hidden, axis=-1, keepdims=True) + EPSILON)
    normed_ref[...] = (hidden * inv * gain_ref[...]).astype(BF)


def finish_attention(place, inputs, gain, weight, parts):
    shard_len, width = inputs.shape
    ranks, cols = len(parts), parts[0].shape[1]
    whole = lambda shape: pl.BlockSpec(shape, lambda j, p: (0,) * len(shape))
    return pl.pallas_call(
        functools.partial(hidden_kernel, ranks),
        grid_spec=pltpu.PrefetchScalarGridSpec(
            num_scalar_prefetch=1,
            grid=(1,),
            in_specs=[
                whole((shard_len, width)),
                whole((1, width)),
                whole(weight.shape),
            ]
            + [whole((shard_len, cols))] * ranks,
            out_specs=[
                whole((shard_len, width)),
                whole((shard_len, width)),
                whole((shard_len, ranks * cols)),
            ],
        ),
        out_shape=[
            jax.ShapeDtypeStruct((shard_len, width), F32),
            jax.ShapeDtypeStruct((shard_len, width), BF),
            jax.ShapeDtypeStruct((shard_len, ranks * cols), BF),
        ],
        compiler_params=pltpu.CompilerParams(vmem_limit_bytes=40 * MIB),
        cost_estimate=cost(
            flops=2 * shard_len * width * width,
            bytes_accessed=2 * width * width + 12 * shard_len * width,
            transcendentals=0,
        ),
        name="finish_attention",
    )(place, inputs, gain, weight, *parts)


def grad_hidden_kernel(
    ranks,
    place_ref,
    own_ref,
    got_x_ref,
    last_y_ref,
    got_y_ref,
    last_x_ref,
    hidden_ref,
    cot_ref,
    gain_ref,
    weight_ref,
    grad_ref,
    low_ref,
    *part_refs,
):
    half = last_y_ref.shape[0]
    cols = part_refs[0].shape[1]
    for rows, got_ref, last_ref in (
        (slice(0, half), got_x_ref, last_y_ref),
        (slice(half, 2 * half), got_y_ref, last_x_ref),
    ):
        weighted = own_ref[rows].astype(F32) + got_ref[0].astype(F32) + last_ref[...].astype(F32)
        weighted = weighted * gain_ref[...]
        values = hidden_ref[rows]
        inv = lax.rsqrt(jnp.mean(values * values, axis=-1, keepdims=True) + EPSILON)
        inner = jnp.mean(weighted * values, axis=-1, keepdims=True)
        grad = inv * weighted - values * (inv * inv * inv * inner) + cot_ref[rows].astype(F32)
        grad_ref[rows] = grad
        low_ref[rows] = grad.astype(BF)
    for k, part_ref in enumerate(part_refs):
        target = lax.rem(place_ref[1] + k, ranks)
        where = pl.ds(pl.multiple_of(target * cols, HEAD), cols)
        part_ref[...] = contract(low_ref[...], weight_ref[:, where], 1, 0).astype(BF)


def begin_back(place, ranks, pieces, hidden, cotangent, gain, weight):
    shard_len, width = hidden.shape
    cols = weight.shape[1] // ranks
    half = shard_len // 2
    whole = lambda shape: pl.BlockSpec(shape, lambda j, p: (0,) * len(shape))
    first = pl.BlockSpec((1, half, width), lambda j, p: (0, 0, 0))
    grad, low, *parts = pl.pallas_call(
        functools.partial(grad_hidden_kernel, ranks),
        grid_spec=pltpu.PrefetchScalarGridSpec(
            num_scalar_prefetch=1,
            grid=(1,),
            in_specs=[
                whole((shard_len, width)),
                first,
                whole((half, width)),
                first,
                whole((half, width)),
                whole((shard_len, width)),
                whole((shard_len, width)),
                whole((1, width)),
                whole(weight.shape),
            ],
            out_specs=[whole((shard_len, width))] * 2 + [whole((shard_len, cols))] * ranks,
        ),
        out_shape=[
            jax.ShapeDtypeStruct((shard_len, width), F32),
            jax.ShapeDtypeStruct((shard_len, width), BF),
        ]
        + [jax.ShapeDtypeStruct((shard_len, cols), BF)] * ranks,
        compiler_params=pltpu.CompilerParams(vmem_limit_bytes=48 * MIB),
        cost_estimate=cost(
            flops=2 * shard_len * width * width,
            bytes_accessed=2 * width * width + 20 * shard_len * width,
            transcendentals=0,
        ),
        name="begin_back",
    )(place, *pieces, hidden, cotangent, gain, weight)
    return grad, low, parts


def attend_back_kernel(
    strip, place_ref, query_ref, key_ref, value_ref, early_ref, log_ref, cos_ref, sin_ref, *refs
):
    *part_refs, query_out, own_out, early_out, grad_ref = refs
    length = query_ref.shape[1]
    factor = HEAD ** (-0.5)
    ranks = len(part_refs)
    shard_len = length // ranks
    for k, part_ref in enumerate(part_refs):
        source = lax.rem(place_ref[1] + ranks - k, ranks)
        grad_ref[pl.ds(pl.multiple_of(source * shard_len, shard_len), shard_len)] = part_ref[...]

    def run(late):
        early_key_sum = early_value_sum = 0.0
        for first in range(length - strip, -1, -strip):
            end = first + strip
            query = query_ref[0, first:end]
            grad = grad_ref[first:end]
            log = log_ref[0, first:end]
            own, early = softmax_parts(query, key_ref[0, :end], early_ref[0], first, late)
            own = jnp.exp(own - log)
            own_grad = contract(grad, value_ref[0, :end], 1, 1)
            inner = jnp.sum(own_grad * own, axis=-1, keepdims=True)
            if late:
                early = jnp.exp(early - log)
                early_grad = contract(grad, early_ref[1], 1, 1)
                inner = inner + jnp.sum(early_grad * early, axis=-1, keepdims=True)
            own_low = (own * (own_grad - inner)).astype(BF)
            grad_query = contract(own_low, key_ref[0, :end], 1, 0)
            grad_key = contract(own_low, query, 0, 0) * factor
            grad_value = contract(own.astype(BF), grad, 0, 0)
            if first == length - strip:
                own_out[0] = grad_key
                own_out[1] = grad_value
            else:
                own_out[0, :end] += grad_key
                own_out[1, :end] += grad_value
            if late:
                early_low = (early * (early_grad - inner)).astype(BF)
                grad_query = grad_query + contract(early_low, early_ref[0], 1, 0)
                early_key_sum = early_key_sum + contract(early_low, query, 0, 0)
                early_value_sum = early_value_sum + contract(early.astype(BF), grad, 0, 0)
            grad_query = grad_query * factor
            query_out[first:end] = turned(
                grad_query, cos_ref[0, first:end], -sin_ref[0, first:end]
            ).astype(BF)
        if late:
            early_out[0] = (early_key_sum * factor).astype(BF)
            early_out[1] = early_value_sum.astype(BF)
        else:
            early_out[...] = jnp.zeros(early_out.shape, BF)

    @pl.when(place_ref[0] == 0)
    def _():
        run(False)

    @pl.when(place_ref[0] != 0)
    def _():
        run(True)


def attend_back(place, length, qkv, early, logs, parts, cosine, sine):
    _, rows, cols = qkv.shape
    count = rows // length
    heads, ranks = cols // HEAD, len(parts)
    one = lambda which: pl.BlockSpec((1, length, HEAD), lambda i, h, p: (which, i, h))
    pair = pl.BlockSpec((2, length, HEAD), lambda i, h, p: (0, i, h))
    table = pl.BlockSpec((1, length, HEAD), lambda i, h, p: (0, 0, 0))
    return pl.pallas_call(
        functools.partial(attend_back_kernel, length // 2),
        grid_spec=pltpu.PrefetchScalarGridSpec(
            num_scalar_prefetch=1,
            grid=(count, heads),
            in_specs=[
                one(0),
                one(1),
                one(2),
                pair,
                pl.BlockSpec((1, length, 1), lambda i, h, p: (i * heads + h, 0, 0)),
                table,
                table,
            ]
            + [pl.BlockSpec((length // ranks, HEAD), lambda i, h, p: (i, h))] * ranks,
            out_specs=[pl.BlockSpec((length, HEAD), lambda i, h, p: (i, h)), pair, pair],
            scratch_shapes=[pltpu.VMEM((length, HEAD), BF)],
        ),
        out_shape=[
            jax.ShapeDtypeStruct((rows, cols), BF),
            jax.ShapeDtypeStruct((2, rows, cols), F32),
            jax.ShapeDtypeStruct((2, rows, cols), BF),
        ],
        compiler_params=pltpu.CompilerParams(vmem_limit_bytes=32 * MIB),
        cost_estimate=cost(
            flops=20 * length * length * cols,
            bytes_accessed=28 * length * cols,
            transcendentals=2 * length * length * heads,
        ),
        name="attend_back",
    )(place, qkv, qkv, qkv, early, logs, cosine, sine, *parts)


def project_back_kernel(
    query_ref, own_ref, back_ref, cos_ref, sin_ref, weight_ref, low_ref, out_ref
):
    cols = query_ref.shape[1]

    @pl.when(pl.program_id(1) == 0)
    def _():
        low_ref[:, :cols] = query_ref[...]
        keys = own_ref[0] + back_ref[0].astype(F32)
        cosine, sine = cos_ref[0], -sin_ref[0]
        for head in range(cols // HEAD):
            part = slice(head * HEAD, (head + 1) * HEAD)
            into = slice(cols + head * HEAD, cols + (head + 1) * HEAD)
            low_ref[:, into] = turned(keys[:, part], cosine, sine).astype(BF)
        low_ref[:, 2 * cols :] = (own_ref[1] + back_ref[1].astype(F32)).astype(BF)

    result = contract(low_ref[...], weight_ref[...], 1, 1).astype(BF)
    out_ref[...] = result.reshape(out_ref.shape)


def project_back(count, ranks, grad_query, grad_own, back, cosine, sine, weight):
    rows, cols = grad_query.shape
    length = rows // count
    width = weight.shape[0]
    step = width // 3
    pair = pl.BlockSpec((2, length, cols), lambda i, j: (0, i, 0))
    table = pl.BlockSpec((1, length, HEAD), lambda i, j: (0, 0, 0))
    return pl.pallas_call(
        project_back_kernel,
        grid=(count, 3),
        in_specs=[
            pl.BlockSpec((length, cols), lambda i, j: (i, 0)),
            pair,
            pair,
            table,
            table,
            pl.BlockSpec((step, 3 * cols), lambda i, j: (j, 0)),
        ],
        out_specs=[
            pl.BlockSpec((length, 3 * cols), lambda i, j: (i, 0)),
            pl.BlockSpec((ranks, 1, length // ranks, step), lambda i, j: (0, i, 0, j)),
        ],
        out_shape=[
            jax.ShapeDtypeStruct((rows, 3 * cols), BF),
            jax.ShapeDtypeStruct((ranks, count, length // ranks, width), BF),
        ],
        compiler_params=pltpu.CompilerParams(vmem_limit_bytes=32 * MIB),
        cost_estimate=cost(
            flops=6 * rows * width * cols,
            bytes_accessed=6 * width * cols + 18 * rows * cols + 2 * rows * width,
            transcendentals=0,
        ),
        name="project_back",
    )(grad_query, grad_own, back, cosine, sine, weight)


def gelu_both(values):
    scale = (2.0 / jnp.pi) ** 0.5
    square = values * values
    tanh = jnp.tanh(scale * values * (1.0 + 0.044715 * square))
    half = 0.5 * (1.0 + tanh)
    slope = half + 0.5 * values * (1.0 - tanh * tanh) * scale * (1.0 + 3 * 0.044715 * square)
    return values * half, slope


def stack_units(first, own_ref, other_ref, which, into):
    ranks, _, blocks, sub, _ = own_ref.shape

    def fill(source):
        for block in range(blocks):
            for rank in range(ranks):
                row = (block * ranks + rank) * sub
                into[row : row + sub] = source[rank, which, block]

    @pl.when(first)
    def _():
        fill(own_ref)

    @pl.when(jnp.logical_not(first))
    def _():
        fill(other_ref)


def feed_kernel(count, place_ref, cot_ref, own_ref, other_ref, *refs):
    rows_in, refs = refs[: 5 * count], refs[5 * count :]
    grads_out, (rows_ref, down_ref, act_ref, pre_ref, up_ref, sum_ref) = (
        refs[: 5 * count],
        refs[5 * count :],
    )
    step = pl.program_id(0)
    half = up_ref.shape[0]
    shard_len = rows_ref.shape[1] // count
    part = shard_len // 2
    ctx, mine = place_ref[0], place_ref[2]

    for turn_of, at in ((0, 0), (1, LEVELS)):

        @pl.when(step == at)
        def _(turn_of=turn_of):
            stack_units(ctx == turn_of, own_ref, other_ref, 0, up_ref)
            stack_units(ctx == turn_of, own_ref, other_ref, 1, down_ref.at[0])

    for k in range(LEVELS):

        @pl.when((step < LEVELS) & (jnp.bitwise_xor(mine, k) == step))
        def _(k=k):
            for i in range(count):
                pieces = rows_in[5 * i : 5 * i + 5]
                rows = slice(i * shard_len, (i + 1) * shard_len)
                if k < LEVELS - 1:
                    rows_ref[0, rows] = pieces[k][...]
                else:
                    rows_ref[0, rows.start : rows.start + part] = pieces[3][...]
                    rows_ref[0, rows.start + part : rows.stop] = pieces[4][...]

    def run(used):
        upped = contract(rows_ref[0], up_ref[:used], 1, 1)
        activated, slope = gelu_both(upped)
        grad_act = contract(cot_ref[0], down_ref[0, :used], 1, 1)
        grad_upped = (grad_act * slope).astype(BF)
        act_ref[0, :, :used] = activated.astype(BF)
        pre_ref[0, :, :used] = grad_upped
        return contract(grad_upped, up_ref[:used], 1, 0)

    for one in range(LEVELS - 2):

        @pl.when(step == one)
        def _(one=one):
            sum_ref[...] = run(half // 2 ** (LEVELS - 2 - one))

    @pl.when(step >= LEVELS - 2)
    def _():
        result = run(half)

        @pl.when(step < LEVELS)
        def _():
            sum_ref[...] = result

        @pl.when(step == LEVELS)
        def _():
            sum_ref[...] += result

    level = jnp.minimum(step, LEVELS - 1)
    for k in range(LEVELS):

        @pl.when((step != LEVELS - 1) & (jnp.bitwise_xor(mine, k) == level))
        def _(k=k):
            for i in range(count):
                keep, keep_x, keep_y, send_x, send_y = grads_out[5 * i : 5 * i + 5]
                first = sum_ref[i * shard_len : i * shard_len + part].astype(BF)
                second = sum_ref[i * shard_len + part : (i + 1) * shard_len].astype(BF)
                if k == 0:
                    keep[:part] = first
                    keep[part:] = second
                elif k == 1:
                    send_x[0] = first
                    keep_x[...] = second
                elif k == 2:
                    keep_y[...] = first
                    send_y[0] = second
                else:
                    send_x[1] = first
                    send_y[1] = second


def feed(place, rows, cot, own, other):
    count = len(rows)
    _, length, width = cot.shape
    half = own.shape[0] * own.shape[2] * own.shape[3]
    shard_len = length // count
    part = shard_len // 2
    whole = lambda shape: pl.BlockSpec(
        shape, lambda s, p: (0,) * len(shape), pipeline_mode=pl.Buffered(1)
    )
    fixed = lambda shape: pl.BlockSpec(shape, lambda s, p: (0,) * len(shape))
    by_level = pl.BlockSpec((1, length, width), lambda s, p: (jnp.minimum(s, LEVELS - 1), 0, 0))
    by_half = pl.BlockSpec((1, half, width), lambda s, p: (s // LEVELS, 0, 0))
    by_step = pl.BlockSpec((1, length, half), lambda s, p: (s, 0, 0))
    pieces = [
        (shard_len, width),
        (part, width),
        (part, width),
        (2, part, width),
        (2, part, width),
    ]
    *grads, rows_all, down, activated, before = pl.pallas_call(
        functools.partial(feed_kernel, count),
        grid_spec=pltpu.PrefetchScalarGridSpec(
            num_scalar_prefetch=1,
            grid=(LEVELS + 1,),
            in_specs=[by_level, whole(own.shape), whole(own.shape)]
            + [whole(piece.shape) for one in rows for piece in one],
            out_specs=[fixed(shape) for shape in pieces] * count
            + [by_level, by_half, by_step, by_step],
            scratch_shapes=[pltpu.VMEM((half, width), BF), pltpu.VMEM((length, width), F32)],
        ),
        out_shape=[jax.ShapeDtypeStruct(shape, BF) for shape in pieces] * count
        + [
            jax.ShapeDtypeStruct(cot.shape, BF),
            jax.ShapeDtypeStruct((2, half, width), BF),
            jax.ShapeDtypeStruct((LEVELS + 1, length, half), BF),
            jax.ShapeDtypeStruct((LEVELS + 1, length, half), BF),
        ],
        compiler_params=pltpu.CompilerParams(vmem_limit_bytes=58 * MIB),
        cost_estimate=cost(
            flops=24 * length * width * half,
            bytes_accessed=24 * length * width + 8 * half * width + 20 * length * half,
            transcendentals=5 * length * half,
        ),
        name="feed",
    )(place, cot, own, other, *[piece for one in rows for piece in one])
    grads = [grads[5 * i : 5 * i + 5] for i in range(count)]
    return grads, rows_all, down, activated, before


def feed_weights_kernel(
    place_ref,
    rows_ref,
    cot_ref,
    act_ref,
    pre_ref,
    down_ref,
    keep_ref,
    send_ref,
    out_ref,
    up_sum,
    down_sum,
    out_sum,
    stage,
    sem,
):
    step = pl.program_id(0)
    half = down_ref.shape[1]
    ranks, _, blocks, sub, _ = stage.shape

    def add(used, fresh):
        up_part = contract(pre_ref[0, :, :used], rows_ref[0], 0, 0)
        down_part = contract(act_ref[0, :, :used], cot_ref[0], 0, 0)
        if fresh == used:
            up_sum[:used] = up_part
            down_sum[:used] = down_part
        else:
            up_sum[:fresh] += up_part[:fresh]
            down_sum[:fresh] += down_part[:fresh]
            if fresh < used:
                up_sum[fresh:used] = up_part[fresh:]
                down_sum[fresh:used] = down_part[fresh:]
        return contract(act_ref[0, :, :used], down_ref[0, :used], 1, 0)

    def store(which):
        for block in range(blocks):
            for rank in range(ranks):
                first = (block * ranks + rank) * sub
                stage[rank, 0, block] = up_sum[first : first + sub].astype(BF)
                stage[rank, 1, block] = down_sum[first : first + sub].astype(BF)

        @pl.when(place_ref[0] == which)
        def _():
            copy = pltpu.make_async_copy(stage, keep_ref, sem)
            copy.start()
            copy.wait()

        @pl.when(place_ref[0] != which)
        def _():
            copy = pltpu.make_async_copy(stage, send_ref, sem)
            copy.start()
            copy.wait()

    for one in range(LEVELS - 1):

        @pl.when(step == one)
        def _(one=one):
            used = half // 2 ** (LEVELS - 2 - one)
            out_ref[0] = add(used, used if one == 0 else used // 2).astype(BF)

    @pl.when(step == LEVELS - 1)
    def _():
        up_sum[...] += contract(pre_ref[0], rows_ref[0], 0, 0)
        down_sum[...] += contract(act_ref[0], cot_ref[0], 0, 0)
        out_sum[...] = contract(act_ref[0], down_ref[0], 1, 0)
        store(0)

    @pl.when(step == LEVELS)
    def _():
        out_ref[0] = (out_sum[...] + add(half, half)).astype(BF)
        store(1)


def feed_weights(place, rows, cot, activated, before, down, ranks, blocks):
    _, length, width = rows.shape
    half = down.shape[1]
    sub = half // (ranks * blocks)
    by_level = pl.BlockSpec((1, length, width), lambda s, p: (jnp.minimum(s, LEVELS - 1), 0, 0))
    by_half = pl.BlockSpec((1, half, width), lambda s, p: (s // LEVELS, 0, 0))
    by_step = pl.BlockSpec((1, length, half), lambda s, p: (s, 0, 0))
    shape = (ranks, 2, blocks, sub, width)
    return pl.pallas_call(
        feed_weights_kernel,
        grid_spec=pltpu.PrefetchScalarGridSpec(
            num_scalar_prefetch=1,
            grid=(LEVELS + 1,),
            in_specs=[by_level, by_level, by_step, by_step, by_half],
            out_specs=[
                pl.BlockSpec(memory_space=pl.ANY),
                pl.BlockSpec(memory_space=pl.ANY),
                by_level,
            ],
            scratch_shapes=[
                pltpu.VMEM((half, width), F32),
                pltpu.VMEM((half, width), F32),
                pltpu.VMEM((length, width), F32),
                pltpu.VMEM(shape, BF),
                pltpu.SemaphoreType.DMA(()),
            ],
        ),
        out_shape=[
            jax.ShapeDtypeStruct(shape, BF),
            jax.ShapeDtypeStruct(shape, BF),
            jax.ShapeDtypeStruct(rows.shape, BF),
        ],
        compiler_params=pltpu.CompilerParams(vmem_limit_bytes=56 * MIB),
        cost_estimate=cost(
            flops=24 * length * width * half,
            bytes_accessed=24 * length * width + 12 * half * width + 20 * length * half,
            transcendentals=0,
        ),
        name="feed_weights",
    )(place, rows, cot, activated, before, down)


def outer_kernel(count, *refs):
    lefts, rights, out_ref = refs[:count], refs[count : 2 * count], refs[-1]
    total = contract(lefts[0][...], rights[0][...], 0, 0)
    for left, right in zip(lefts[1:], rights[1:]):
        total = total + contract(left[...], right[...], 0, 0)
    out_ref[...] = total.astype(BF)


def outer(lefts, rights):
    rows, m = lefts[0].shape
    n = rights[0].shape[1]
    count = len(lefts)
    step = m // 4
    return pl.pallas_call(
        functools.partial(outer_kernel, count),
        grid=(4,),
        in_specs=[pl.BlockSpec((rows, step), lambda j: (0, j))] * count
        + [pl.BlockSpec((rows, n), lambda j: (0, 0))] * count,
        out_specs=pl.BlockSpec((step, n), lambda j: (j, 0)),
        out_shape=jax.ShapeDtypeStruct((m, n), BF),
        compiler_params=pltpu.CompilerParams(vmem_limit_bytes=32 * MIB),
        cost_estimate=cost(
            flops=2 * count * rows * m * n,
            bytes_accessed=2 * (count * rows * (m + n) + m * n),
            transcendentals=0,
        ),
        name="outer",
    )(*lefts, *rights)


def inverse_rms(values):
    return lax.rsqrt(jnp.mean(values * values, axis=-1, keepdims=True) + EPSILON)


def norm_back(values, inv_rms, weighted):
    return inv_rms * weighted - values * (inv_rms * inv_rms * inv_rms) * jnp.mean(
        weighted * values, axis=-1, keepdims=True
    )


def rotation(positions, head_size):
    half_size = head_size // 2
    frequency = 10000.0 ** (-jnp.arange(half_size, dtype=jnp.float32) / half_size)
    angles = positions.astype(jnp.float32)[:, None] * frequency[None, :]
    cosine, sine = jnp.cos(angles), jnp.sin(angles)
    cosine = jnp.concatenate([cosine, cosine], -1)
    sine = jnp.concatenate([-sine, sine], -1)
    return (
        jnp.stack([cosine, jnp.ones_like(cosine)]),
        jnp.stack([sine, jnp.zeros_like(sine)]),
    )


def product(equation, left, right):
    return jnp.einsum(equation, left, right, preferred_element_type=F32)


def local(inputs, w_query, w_key, w_value, w_out, w_up, w_down, gain_attn, gain_ffn, cotangent):
    count, shard_len, width = inputs.shape
    own_rows = count * shard_len
    ranks = lax.axis_size("mp")
    length_half = shard_len * ranks
    level = lax.axis_index("dp") % LEVELS
    ctx = lax.axis_index("ctx")
    rank = lax.axis_index("mp")
    part_rows, head_cols = w_query.shape
    place = jnp.stack([ctx, rank, level]).astype(jnp.int32)

    inputs_flat = inputs.reshape(own_rows, width)
    cot_flat = cotangent.reshape(own_rows, width)
    rows_all = lax.all_gather(inputs_flat, "mp", axis=0)
    out_found = [turn(w_out, "mp", k) for k in range(1, ranks)]

    gains = team_gather(level_gather_small(jnp.stack([gain_attn, gain_ffn]), level))
    gains = pair_gather(gains.reshape(-1, 2, part_rows), ctx, 1)
    gains = gains.transpose(2, 0, 1, 3).reshape(2, 1, width).astype(F32)
    gain_first, gain_second = gains[0], gains[1]

    qkv_full = model_gather(
        after(jnp.concatenate([w_query, w_key, w_value], axis=1), *out_found), level, ctx
    )
    blocks, unit_cols = w_up.shape[1:]
    sub = unit_cols // LEVELS
    half_blocks = blocks // 2
    up_turned = w_up.transpose(1, 2, 0)
    halves = [
        jnp.stack([up_turned[b : b + half_blocks], w_down[b : b + half_blocks]])
        for b in (0, half_blocks)
    ]
    own_part, sent_part = pair_split(halves[0], halves[1], ctx)
    pair = jnp.concatenate(
        [jnp.where(ctx == 0, own_part, sent_part), jnp.where(ctx == 0, sent_part, own_part)], -1
    )
    pair = pair.reshape(2, half_blocks, LEVELS, sub, 2 * part_rows).transpose(2, 0, 1, 3, 4)
    swapped = team_gather(level_swap(pair, level))
    swapped = side_by_side(swapped.reshape(-1, 2, half_blocks, sub, 2 * part_rows))
    cot_pieces = level_pieces(after(cot_flat, swapped))
    ranked = lax.all_gather(swapped, "mp", axis=0)
    positions = ctx * length_half + jnp.arange(length_half, dtype=jnp.int32)
    cosine, sine = rotation(positions, HEAD)
    qkv, normed = project(
        count, shard_len, rows_all, after(gain_first, *cot_pieces), qkv_full, cosine, sine
    )
    cot_rows = level_join(after(cot_pieces, qkv), level)
    out_parts = put(jnp.zeros((ranks,) + w_out.shape, BF), w_out, rank)
    for k in range(1, ranks):
        out_parts = put(out_parts, out_found[k - 1], (rank + ranks - k) % ranks)
    out_parts = after(out_parts.reshape(-1, part_rows).T, cot_pieces[3])
    out_full = model_gather(out_parts, level, ctx)
    early = lax.ppermute(qkv[1:], "ctx", [(0, 1)])
    parts, logs = attend(place, ranks, length_half, qkv, early)
    hidden, normed_two, mixed_own = finish_attention(
        place, inputs_flat, gain_second, out_full, rank_swap(parts)
    )

    ranked = after(ranked, hidden)
    (opened,), rows_second, down_mine, activated, before = feed(
        place, [level_pieces(normed_two)], cot_rows, ranked, flip(ranked, "ctx", 1)
    )
    own, by_x, by_y, got_x, got_y = opened
    got_x, got_y = flip(got_x, "dp", 1), flip(got_y, "dp", 2)

    grad_kept, grad_sent, results = feed_weights(
        place, rows_second, cot_rows, activated, before, down_mine, ranks, half_blocks
    )
    grad_sent = after(grad_sent, got_x, got_y)
    grad_ffn = (grad_kept.astype(F32) + flip(grad_sent, "ctx", 1).astype(F32)).astype(BF)
    grad_ffn_low = [grad_ffn[:, kind].reshape(-1, width) for kind in range(2)]
    grad_ffn = [
        lax.psum_scatter(one, "mp", scatter_dimension=0, tiled=True) for one in grad_ffn_low
    ]

    last_y, last_x = level_scatter_last(by_x, by_y, got_x, got_y)
    own = after(own, *grad_ffn_low)
    grad_hidden, grad_low, parts = begin_back(
        place, ranks, (own, got_x, last_y, got_y, last_x), hidden, cot_flat, gain_second, out_full
    )
    parts = rank_swap(parts)
    grad_query, grad_own, grad_early = attend_back(
        place, length_half, qkv, early, logs, parts, cosine, sine
    )
    grad_early = after(grad_early, grad_ffn[0])
    back = lax.ppermute(grad_early, "ctx", [(1, 0)])
    grad_qkv, grad_first = project_back(
        count, ranks, grad_query, grad_own, back, cosine, sine, qkv_full
    )
    grad_first = after(grad_first, grad_ffn[1])
    grad_ffn = after(grad_ffn, grad_first)
    grad_first = lax.psum_scatter(
        grad_first.reshape(-1, width), "mp", scatter_dimension=0, tiled=True
    )

    results_open = after(level_scatter_open(after(results, grad_low), level), grad_qkv)
    result = level_sum(results_open, level_scatter_last(*results_open[1:]))
    outputs = (hidden + result).astype(BF).reshape(inputs.shape)

    grad_ffn = jnp.stack(grad_ffn).reshape(2, half_blocks, sub, width)
    grad_ffn = jnp.stack(jnp.split(grad_ffn, width // (2 * part_rows), axis=-1))
    grad_ffn = team_scatter(grad_ffn.reshape((-1, LEVELS) + grad_ffn.shape[1:]))
    grad_ffn = level_swap(grad_ffn, level).transpose(1, 2, 0, 3, 4)
    grad_ffn = grad_ffn.reshape(2, half_blocks, unit_cols, 2 * part_rows)
    own_part, sent_part = pair_split(grad_ffn[..., :part_rows], grad_ffn[..., part_rows:], ctx)
    grad_ffn = jnp.concatenate(
        [jnp.where(ctx == 0, own_part, sent_part), jnp.where(ctx == 0, sent_part, own_part)], 1
    ).astype(F32)
    grad_up_out = grad_ffn[0].transpose(2, 0, 1)
    grad_down_out = grad_ffn[1]
    gain_ffn_part = jnp.sum(grad_up_out * w_up.astype(F32), axis=(1, 2)) / gain_ffn.astype(F32)

    grad_qkv_w = outer([normed], [grad_qkv])
    grad_qkv_w = model_scatter(grad_qkv_w, level, ctx, part_rows)
    originals = jnp.concatenate([w_query, w_key, w_value], axis=1).astype(F32)
    gain_attn_part = jnp.sum(grad_qkv_w * originals, axis=1) / gain_attn.astype(F32)
    gain_grads = jnp.stack([gain_attn_part, gain_ffn_part])
    gain_grads = gain_grads + sum([turn(gain_grads, "mp", k) for k in range(1, ranks)])

    grad_out_w = outer([after(grad_low, grad_qkv)], [mixed_own])
    grad_out_w = model_scatter(grad_out_w, level, ctx, part_rows).astype(BF)
    grad_out_w = jnp.stack(jnp.split(grad_out_w, ranks, axis=1))
    grad_out_out = take(grad_out_w, rank).astype(F32)
    for k in range(1, ranks):
        grad_out_out = grad_out_out + turn(take(grad_out_w, (rank + k) % ranks), "mp", k).astype(F32)
    grad_out_out = grad_out_out.T

    grad_first = after(grad_first, grad_out_out, gain_grads, outputs, grad_qkv_w, grad_up_out, grad_down_out)
    inputs_f = inputs.astype(F32)
    input_grads = grad_hidden.reshape(inputs.shape) + norm_back(
        inputs_f,
        inverse_rms(inputs_f),
        gain_first * grad_first.reshape(inputs.shape).astype(F32),
    )
    return (
        outputs,
        input_grads,
        grad_qkv_w[:, :head_cols],
        grad_qkv_w[:, head_cols : 2 * head_cols],
        grad_qkv_w[:, 2 * head_cols :],
        grad_out_out,
        grad_up_out,
        grad_down_out,
        gain_grads[0],
        gain_grads[1],
    )


def solution(mesh):
    in_specs = (
        P("dp", ("ctx", "mp"), None),
        P(("dp", "ctx"), "mp"),
        P(("dp", "ctx"), "mp"),
        P(("dp", "ctx"), "mp"),
        P("mp", ("dp", "ctx")),
        P(("dp", "ctx"), None, "mp"),
        P(None, "mp", ("dp", "ctx")),
        P(("dp", "ctx")),
        P(("dp", "ctx")),
        P("dp", ("ctx", "mp"), None),
    )
    out_specs = (
        P("dp", ("ctx", "mp"), None),
        P("dp", ("ctx", "mp"), None),
        P(("dp", "ctx"), "mp"),
        P(("dp", "ctx"), "mp"),
        P(("dp", "ctx"), "mp"),
        P("mp", ("dp", "ctx")),
        P(("dp", "ctx"), None, "mp"),
        P(None, "mp", ("dp", "ctx")),
        P(("dp", "ctx")),
        P(("dp", "ctx")),
    )
    return jax.shard_map(local, mesh=mesh, in_specs=in_specs, out_specs=out_specs, check_vma=False)
```

```python
import functools

import jax
import jax.numpy as jnp
from jax import lax
from jax.experimental import pallas as pl
from jax.experimental.pallas import tpu as pltpu
from jax.sharding import PartitionSpec as P

HEAD = 128
LEVELS = 4
EPSILON = 1e-06
NEGATIVE = -1e30
BF = jnp.bfloat16
F32 = jnp.float32
MIB = 1 << 20
HURRY = 16


def flip(shard, axis, bit):
    devices = lax.axis_size(axis)
    return lax.ppermute(shard, axis, [(i, i ^ bit) for i in range(devices)])


def turn(shard, axis, by):
    devices = lax.axis_size(axis)
    return lax.ppermute(shard, axis, [(i, (i + by) % devices) for i in range(devices)])


def after(values, *others):
    return lax.optimization_barrier((values,) + others)[0]


def put(buffer, part, index, dim=0):
    starts = [0] * buffer.ndim
    starts[dim] = index
    return lax.dynamic_update_slice(buffer, jnp.expand_dims(part, dim), tuple(starts))


def take(buffer, index, dim=0):
    return lax.dynamic_index_in_dim(buffer, index, dim, keepdims=False)


def side_by_side(parts):
    return jnp.concatenate([parts[k] for k in range(parts.shape[0])], axis=-1)


def pack(part, width):
    rows, cols = part.shape
    return side_by_side(part.reshape(width // cols, -1, cols))


def unpack(packed, cols):
    strips = packed.shape[1] // cols
    return jnp.concatenate([packed[:, k * cols : (k + 1) * cols] for k in range(strips)], 0)


def rank_swap(parts):
    return [parts[0]] + [turn(parts[k], "mp", k) for k in range(1, len(parts))]


def level_pieces(part):
    half = part.shape[0] // 2
    from_x = flip(part, "dp", 1)
    from_y = flip(part, "dp", 2)
    return part, from_x, from_y, flip(from_x[:half], "dp", 2), flip(from_y[half:], "dp", 1)


def level_gather(part, mine):
    return level_join(level_pieces(part), mine)


def level_join(pieces, mine):
    part, from_x, from_y, low_half, high_half = pieces
    whole = put(jnp.zeros((LEVELS,) + part.shape, part.dtype), part, mine)
    whole = put(whole, from_x, mine ^ 1)
    whole = put(whole, from_y, mine ^ 2)
    return put(whole, jnp.concatenate([low_half, high_half], 0), mine ^ 3)


def level_gather_small(part, mine):
    whole = put(jnp.zeros((LEVELS,) + part.shape, part.dtype), part, mine)
    for k in range(1, LEVELS):
        whole = put(whole, flip(part, "dp", k), mine ^ k)
    return whole


def level_scatter_open(parts, mine):
    half = parts.shape[1] // 2
    own, by_x, by_y, by_xy = (take(parts, mine ^ k) for k in range(LEVELS))
    got_x = flip(jnp.stack([by_x[:half], by_xy[:half]]), "dp", 1)
    got_y = flip(jnp.stack([by_y[half:], by_xy[half:]]), "dp", 2)
    return own, by_x[half:], by_y[:half], got_x, got_y


def level_scatter_last(by_x, by_y, got_x, got_y):
    send_y = (by_y.astype(F32) + got_x[1].astype(F32)).astype(by_y.dtype)
    send_x = (by_x.astype(F32) + got_y[1].astype(F32)).astype(by_x.dtype)
    return flip(send_y, "dp", 2), flip(send_x, "dp", 1)


def level_scatter(parts, mine):
    opened = level_scatter_open(parts, mine)
    return level_sum(opened, level_scatter_last(*opened[1:]))


def level_sum(opened, last):
    own, _, by_y, got_x, got_y = opened
    last_y, last_x = last
    half = by_y.shape[0]
    first = own[:half].astype(F32) + got_x[0].astype(F32) + last_y.astype(F32)
    second = own[half:].astype(F32) + got_y[0].astype(F32) + last_x.astype(F32)
    return jnp.concatenate([first, second], 0)


def level_swap(parts, mine):
    whole = put(jnp.zeros(parts.shape, parts.dtype), take(parts, mine), mine)
    for k in range(1, LEVELS):
        whole = put(whole, flip(take(parts, mine ^ k), "dp", k), mine ^ k)
    return whole


def teams(devices):
    return [list(range(level, devices, LEVELS)) for level in range(LEVELS)]


def team_gather(part):
    devices = lax.axis_size("dp")
    if devices == LEVELS:
        return part[None]
    return lax.all_gather(part, "dp", axis=0, axis_index_groups=teams(devices))


def team_scatter(parts):
    devices = lax.axis_size("dp")
    if devices == LEVELS:
        return parts[0]
    return lax.psum_scatter(
        parts, "dp", scatter_dimension=0, axis_index_groups=teams(devices), tiled=False
    )


def pair_gather(part, mine, dim=0):
    other = flip(part, "ctx", 1)
    shape = part.shape[:dim] + (2,) + part.shape[dim:]
    return put(put(jnp.zeros(shape, part.dtype), part, mine, dim), other, 1 - mine, dim)


def pair_split(first, second, mine):
    own = jnp.where(mine == 0, first, second)
    return own, flip(jnp.where(mine == 0, second, first), "ctx", 1)


def pair_scatter(parts, mine, dim):
    other = flip(take(parts, 1 - mine, dim), "ctx", 1)
    return take(parts, mine, dim).astype(F32) + other.astype(F32)


def model_gather(part, level, ctx):
    rows, width = part.shape
    whole = team_gather(level_gather(part, level))
    whole = pair_gather(whole.reshape(-1, rows, width), ctx, 1)
    return whole.reshape(-1, width)


def model_scatter(grad, level, ctx, rows):
    width = grad.shape[1]
    parts = grad.reshape(-1, 2, rows, width)
    parts = pair_scatter(parts, ctx, 1).astype(grad.dtype)
    parts = team_scatter(parts.reshape(-1, LEVELS, rows, width))
    return level_scatter(parts, level)


def cost(flops, bytes_accessed, transcendentals):
    return pl.CostEstimate(
        flops=flops // HURRY,
        bytes_accessed=bytes_accessed // HURRY,
        transcendentals=transcendentals // HURRY,
    )


def contract(left, right, left_dim, right_dim):
    return lax.dot_general(
        left, right, (((left_dim,), (right_dim,)), ((), ())), preferred_element_type=F32
    )


def turned(values, cosine, sine):
    return values * cosine + pltpu.roll(values, HEAD // 2, 1) * sine


def project_kernel(rows_ref, gain_ref, weight_ref, cos_ref, sin_ref, out_ref, normed_ref):
    @pl.when(pl.program_id(1) == 0)
    def _():
        values = rows_ref[...].reshape(normed_ref.shape).astype(F32)
        inv = lax.rsqrt(jnp.mean(values * values, axis=-1, keepdims=True) + EPSILON)
        normed_ref[...] = (values * inv * gain_ref[...]).astype(BF)

    values = contract(normed_ref[...], weight_ref[...], 1, 0)
    cosine, sine = cos_ref[0], sin_ref[0]
    for head in range(values.shape[1] // HEAD):
        cols = slice(head * HEAD, (head + 1) * HEAD)
        out_ref[0, :, cols] = turned(values[:, cols], cosine, sine).astype(BF)


def project(count, shard_len, rows, gain, weight, cosine, sine):
    ranks, _, width = rows.shape
    length = ranks * shard_len
    cols = weight.shape[1] // 3
    table = pl.BlockSpec((1, length, HEAD), lambda i, j: (j // 2, 0, 0))
    return pl.pallas_call(
        project_kernel,
        grid=(count, 3),
        in_specs=[
            pl.BlockSpec((ranks, shard_len, width), lambda i, j: (0, i, 0)),
            pl.BlockSpec((1, width), lambda i, j: (0, 0)),
            pl.BlockSpec((width, cols), lambda i, j: (0, j)),
            table,
            table,
        ],
        out_specs=[
            pl.BlockSpec((1, length, cols), lambda i, j: (j, i, 0)),
            pl.BlockSpec((length, width), lambda i, j: (i, 0)),
        ],
        out_shape=[
            jax.ShapeDtypeStruct((3, count * length, cols), BF),
            jax.ShapeDtypeStruct((count * length, width), BF),
        ],
        compiler_params=pltpu.CompilerParams(vmem_limit_bytes=24 * MIB),
        cost_estimate=cost(
            flops=6 * length * width * cols,
            bytes_accessed=4 * length * width + 6 * width * cols + 6 * length * cols,
            transcendentals=0,
        ),
        name="project",
    )(rows, gain, weight, cosine, sine)


def softmax_parts(query, key_own, key_early, first, late):
    factor = HEAD ** (-0.5)
    own = contract(query, key_own, 1, 1) * factor
    row_ids = first + lax.broadcasted_iota(jnp.int32, own.shape, 0)
    col_ids = lax.broadcasted_iota(jnp.int32, own.shape, 1)
    own = jnp.where(col_ids <= row_ids, own, NEGATIVE)
    early = contract(query, key_early, 1, 1) * factor if late else None
    return own, early


def attend_kernel(strip, place_ref, query_ref, key_ref, value_ref, early_ref, *refs):
    *part_refs, log_ref, mixed_ref = refs
    length = query_ref.shape[1]
    ranks = len(part_refs)
    shard_len = length // ranks

    def run(late):
        for first in range(0, length, strip):
            end = first + strip
            own, early = softmax_parts(
                query_ref[0, first:end], key_ref[0, :end], early_ref[0], first, late
            )
            largest = jnp.max(own, axis=-1, keepdims=True)
            if late:
                largest = jnp.maximum(largest, jnp.max(early, axis=-1, keepdims=True))
            own = jnp.exp(own - largest)
            total = jnp.sum(own, axis=-1, keepdims=True)
            if late:
                early = jnp.exp(early - largest)
                total = total + jnp.sum(early, axis=-1, keepdims=True)
            inverse = 1.0 / total
            mixed = contract((own * inverse).astype(BF), value_ref[0, :end], 1, 0)
            if late:
                mixed = mixed + contract((early * inverse).astype(BF), early_ref[1], 1, 0)
            mixed_ref[first:end] = mixed.astype(BF)
            log_ref[0, first:end] = largest + jnp.log(total)

    @pl.when(place_ref[0] == 0)
    def _():
        run(False)

    @pl.when(place_ref[0] != 0)
    def _():
        run(True)

    for k, part_ref in enumerate(part_refs):
        target = lax.rem(place_ref[1] + k, ranks)
        part_ref[...] = mixed_ref[pl.ds(pl.multiple_of(target * shard_len, shard_len), shard_len)]


def attend(place, ranks, length, qkv, early):
    _, rows, cols = qkv.shape
    count = rows // length
    heads = cols // HEAD
    shard_len = length // ranks
    one = lambda which: pl.BlockSpec((1, length, HEAD), lambda i, h, p: (which, i, h))
    part = pl.BlockSpec((shard_len, HEAD), lambda i, h, p: (i, h))
    *parts, logs = pl.pallas_call(
        functools.partial(attend_kernel, length),
        grid_spec=pltpu.PrefetchScalarGridSpec(
            num_scalar_prefetch=1,
            grid=(count, heads),
            in_specs=[
                one(0),
                one(1),
                one(2),
                pl.BlockSpec((2, length, HEAD), lambda i, h, p: (0, i, h)),
            ],
            out_specs=[part] * ranks + [pl.BlockSpec((1, length, 1), lambda i, h, p: (i * heads + h, 0, 0))],
            scratch_shapes=[pltpu.VMEM((length, HEAD), BF)],
        ),
        out_shape=[jax.ShapeDtypeStruct((count * shard_len, cols), BF)] * ranks
        + [jax.ShapeDtypeStruct((count * heads, length, 1), F32)],
        compiler_params=pltpu.CompilerParams(vmem_limit_bytes=24 * MIB),
        cost_estimate=cost(
            flops=8 * length * length * cols,
            bytes_accessed=14 * length * cols,
            transcendentals=2 * length * length * heads,
        ),
        name="attend",
    )(place, qkv, qkv, qkv, early)
    return parts, logs


def hidden_kernel(ranks, place_ref, input_ref, gain_ref, weight_ref, *refs):
    part_refs, (hidden_ref, normed_ref, mixed_ref) = refs[:ranks], refs[ranks:]
    cols = part_refs[0].shape[1]
    hidden = input_ref[...].astype(F32)
    for k, part_ref in enumerate(part_refs):
        source = lax.rem(place_ref[1] + ranks - k, ranks)
        where = pl.ds(pl.multiple_of(source * cols, HEAD), cols)
        hidden = hidden + contract(part_ref[...], weight_ref[:, where], 1, 1)
        mixed_ref[:, where] = part_ref[...]
    hidden_ref[...] = hidden
    inv = lax.rsqrt(jnp.mean(hidden * hidden, axis=-1, keepdims=True) + EPSILON)
    normed_ref[...] = (hidden * inv * gain_ref[...]).astype(BF)


def finish_attention(place, inputs, gain, weight, parts):
    shard_len, width = inputs.shape
    ranks, cols = len(parts), parts[0].shape[1]
    whole = lambda shape: pl.BlockSpec(shape, lambda j, p: (0,) * len(shape))
    return pl.pallas_call(
        functools.partial(hidden_kernel, ranks),
        grid_spec=pltpu.PrefetchScalarGridSpec(
            num_scalar_prefetch=1,
            grid=(1,),
            in_specs=[
                whole((shard_len, width)),
                whole((1, width)),
                whole(weight.shape),
            ]
            + [whole((shard_len, cols))] * ranks,
            out_specs=[
                whole((shard_len, width)),
                whole((shard_len, width)),
                whole((shard_len, ranks * cols)),
            ],
        ),
        out_shape=[
            jax.ShapeDtypeStruct((shard_len, width), F32),
            jax.ShapeDtypeStruct((shard_len, width), BF),
            jax.ShapeDtypeStruct((shard_len, ranks * cols), BF),
        ],
        compiler_params=pltpu.CompilerParams(vmem_limit_bytes=40 * MIB),
        cost_estimate=cost(
            flops=2 * shard_len * width * width,
            bytes_accessed=2 * width * width + 12 * shard_len * width,
            transcendentals=0,
        ),
        name="finish_attention",
    )(place, inputs, gain, weight, *parts)


def grad_hidden_kernel(
    ranks,
    place_ref,
    own_ref,
    got_x_ref,
    last_y_ref,
    got_y_ref,
    last_x_ref,
    hidden_ref,
    cot_ref,
    gain_ref,
    weight_ref,
    grad_ref,
    low_ref,
    *part_refs,
):
    half = last_y_ref.shape[0]
    cols = part_refs[0].shape[1]
    for rows, got_ref, last_ref in (
        (slice(0, half), got_x_ref, last_y_ref),
        (slice(half, 2 * half), got_y_ref, last_x_ref),
    ):
        weighted = own_ref[rows].astype(F32) + got_ref[0].astype(F32) + last_ref[...].astype(F32)
        weighted = weighted * gain_ref[...]
        values = hidden_ref[rows]
        inv = lax.rsqrt(jnp.mean(values * values, axis=-1, keepdims=True) + EPSILON)
        inner = jnp.mean(weighted * values, axis=-1, keepdims=True)
        grad = inv * weighted - values * (inv * inv * inv * inner) + cot_ref[rows].astype(F32)
        grad_ref[rows] = grad
        low_ref[rows] = grad.astype(BF)
    for k, part_ref in enumerate(part_refs):
        target = lax.rem(place_ref[1] + k, ranks)
        where = pl.ds(pl.multiple_of(target * cols, HEAD), cols)
        part_ref[...] = contract(low_ref[...], weight_ref[:, where], 1, 0).astype(BF)


def begin_back(place, ranks, pieces, hidden, cotangent, gain, weight):
    shard_len, width = hidden.shape
    cols = weight.shape[1] // ranks
    half = shard_len // 2
    whole = lambda shape: pl.BlockSpec(shape, lambda j, p: (0,) * len(shape))
    first = pl.BlockSpec((1, half, width), lambda j, p: (0, 0, 0))
    grad, low, *parts = pl.pallas_call(
        functools.partial(grad_hidden_kernel, ranks),
        grid_spec=pltpu.PrefetchScalarGridSpec(
            num_scalar_prefetch=1,
            grid=(1,),
            in_specs=[
                whole((shard_len, width)),
                first,
                whole((half, width)),
                first,
                whole((half, width)),
                whole((shard_len, width)),
                whole((shard_len, width)),
                whole((1, width)),
                whole(weight.shape),
            ],
            out_specs=[whole((shard_len, width))] * 2 + [whole((shard_len, cols))] * ranks,
        ),
        out_shape=[
            jax.ShapeDtypeStruct((shard_len, width), F32),
            jax.ShapeDtypeStruct((shard_len, width), BF),
        ]
        + [jax.ShapeDtypeStruct((shard_len, cols), BF)] * ranks,
        compiler_params=pltpu.CompilerParams(vmem_limit_bytes=48 * MIB),
        cost_estimate=cost(
            flops=2 * shard_len * width * width,
            bytes_accessed=2 * width * width + 20 * shard_len * width,
            transcendentals=0,
        ),
        name="begin_back",
    )(place, *pieces, hidden, cotangent, gain, weight)
    return grad, low, parts


def attend_back_kernel(
    strip, place_ref, query_ref, key_ref, value_ref, early_ref, log_ref, cos_ref, sin_ref, *refs
):
    *part_refs, query_out, own_out, early_out, grad_ref = refs
    length = query_ref.shape[1]
    factor = HEAD ** (-0.5)
    ranks = len(part_refs)
    shard_len = length // ranks
    for k, part_ref in enumerate(part_refs):
        source = lax.rem(place_ref[1] + ranks - k, ranks)
        grad_ref[pl.ds(pl.multiple_of(source * shard_len, shard_len), shard_len)] = part_ref[...]

    def run(late):
        early_key_sum = early_value_sum = 0.0
        for first in range(length - strip, -1, -strip):
            end = first + strip
            query = query_ref[0, first:end]
            grad = grad_ref[first:end]
            log = log_ref[0, first:end]
            own, early = softmax_parts(query, key_ref[0, :end], early_ref[0], first, late)
            own = jnp.exp(own - log)
            own_grad = contract(grad, value_ref[0, :end], 1, 1)
            inner = jnp.sum(own_grad * own, axis=-1, keepdims=True)
            if late:
                early = jnp.exp(early - log)
                early_grad = contract(grad, early_ref[1], 1, 1)
                inner = inner + jnp.sum(early_grad * early, axis=-1, keepdims=True)
            own_low = (own * (own_grad - inner)).astype(BF)
            grad_query = contract(own_low, key_ref[0, :end], 1, 0)
            grad_key = contract(own_low, query, 0, 0) * factor
            grad_value = contract(own.astype(BF), grad, 0, 0)
            if first == length - strip:
                own_out[0] = grad_key.astype(BF)
                own_out[1] = grad_value.astype(BF)
            else:
                own_out[0, :end] += grad_key.astype(BF)
                own_out[1, :end] += grad_value.astype(BF)
            if late:
                early_low = (early * (early_grad - inner)).astype(BF)
                grad_query = grad_query + contract(early_low, early_ref[0], 1, 0)
                early_key_sum = early_key_sum + contract(early_low, query, 0, 0)
                early_value_sum = early_value_sum + contract(early.astype(BF), grad, 0, 0)
            grad_query = grad_query * factor
            query_out[first:end] = turned(
                grad_query, cos_ref[0, first:end], -sin_ref[0, first:end]
            ).astype(BF)
        if late:
            early_out[0] = (early_key_sum * factor).astype(BF)
            early_out[1] = early_value_sum.astype(BF)
        else:
            early_out[...] = jnp.zeros(early_out.shape, BF)

    @pl.when(place_ref[0] == 0)
    def _():
        run(False)

    @pl.when(place_ref[0] != 0)
    def _():
        run(True)


def attend_back(place, length, qkv, early, logs, parts, cosine, sine):
    _, rows, cols = qkv.shape
    count = rows // length
    heads, ranks = cols // HEAD, len(parts)
    one = lambda which: pl.BlockSpec((1, length, HEAD), lambda i, h, p: (which, i, h))
    pair = pl.BlockSpec((2, length, HEAD), lambda i, h, p: (0, i, h))
    table = pl.BlockSpec((1, length, HEAD), lambda i, h, p: (0, 0, 0))
    return pl.pallas_call(
        functools.partial(attend_back_kernel, length),
        grid_spec=pltpu.PrefetchScalarGridSpec(
            num_scalar_prefetch=1,
            grid=(count, heads),
            in_specs=[
                one(0),
                one(1),
                one(2),
                pair,
                pl.BlockSpec((1, length, 1), lambda i, h, p: (i * heads + h, 0, 0)),
                table,
                table,
            ]
            + [pl.BlockSpec((length // ranks, HEAD), lambda i, h, p: (i, h))] * ranks,
            out_specs=[pl.BlockSpec((length, HEAD), lambda i, h, p: (i, h)), pair, pair],
            scratch_shapes=[pltpu.VMEM((length, HEAD), BF)],
        ),
        out_shape=[
            jax.ShapeDtypeStruct((rows, cols), BF),
            jax.ShapeDtypeStruct((2, rows, cols), BF),
            jax.ShapeDtypeStruct((2, rows, cols), BF),
        ],
        compiler_params=pltpu.CompilerParams(vmem_limit_bytes=32 * MIB),
        cost_estimate=cost(
            flops=20 * length * length * cols,
            bytes_accessed=28 * length * cols,
            transcendentals=2 * length * length * heads,
        ),
        name="attend_back",
    )(place, qkv, qkv, qkv, early, logs, cosine, sine, *parts)


def project_back_kernel(
    query_ref, own_ref, back_ref, cos_ref, sin_ref, weight_ref, low_ref, out_ref
):
    cols = query_ref.shape[1]

    @pl.when(pl.program_id(1) == 0)
    def _():
        low_ref[:, :cols] = query_ref[...]
        keys = own_ref[0].astype(F32) + back_ref[0].astype(F32)
        cosine, sine = cos_ref[0], -sin_ref[0]
        for head in range(cols // HEAD):
            part = slice(head * HEAD, (head + 1) * HEAD)
            into = slice(cols + head * HEAD, cols + (head + 1) * HEAD)
            low_ref[:, into] = turned(keys[:, part], cosine, sine).astype(BF)
        low_ref[:, 2 * cols :] = (own_ref[1].astype(F32) + back_ref[1].astype(F32)).astype(BF)

    result = contract(low_ref[...], weight_ref[...], 1, 1).astype(BF)
    out_ref[...] = result.reshape(out_ref.shape)


def project_back(count, ranks, grad_query, grad_own, back, cosine, sine, weight):
    rows, cols = grad_query.shape
    length = rows // count
    width = weight.shape[0]
    step = width // 3
    pair = pl.BlockSpec((2, length, cols), lambda i, j: (0, i, 0))
    table = pl.BlockSpec((1, length, HEAD), lambda i, j: (0, 0, 0))
    return pl.pallas_call(
        project_back_kernel,
        grid=(count, 3),
        in_specs=[
            pl.BlockSpec((length, cols), lambda i, j: (i, 0)),
            pair,
            pair,
            table,
            table,
            pl.BlockSpec((step, 3 * cols), lambda i, j: (j, 0)),
        ],
        out_specs=[
            pl.BlockSpec((length, 3 * cols), lambda i, j: (i, 0)),
            pl.BlockSpec((ranks, 1, length // ranks, step), lambda i, j: (0, i, 0, j)),
        ],
        out_shape=[
            jax.ShapeDtypeStruct((rows, 3 * cols), BF),
            jax.ShapeDtypeStruct((ranks, count, length // ranks, width), BF),
        ],
        compiler_params=pltpu.CompilerParams(vmem_limit_bytes=32 * MIB),
        cost_estimate=cost(
            flops=6 * rows * width * cols,
            bytes_accessed=6 * width * cols + 18 * rows * cols + 2 * rows * width,
            transcendentals=0,
        ),
        name="project_back",
    )(grad_query, grad_own, back, cosine, sine, weight)


def gelu_both(values):
    scale = (2.0 / jnp.pi) ** 0.5
    square = values * values
    tanh = jnp.tanh(scale * values * (1.0 + 0.044715 * square))
    half = 0.5 * (1.0 + tanh)
    slope = half + 0.5 * values * (1.0 - tanh * tanh) * scale * (1.0 + 3 * 0.044715 * square)
    return values * half, slope


def stack_units(first, own_ref, other_ref, which, into):
    ranks, _, blocks, sub, _ = own_ref.shape

    def fill(source):
        for block in range(blocks):
            for rank in range(ranks):
                row = (block * ranks + rank) * sub
                into[row : row + sub] = source[rank, which, block]

    @pl.when(first)
    def _():
        fill(own_ref)

    @pl.when(jnp.logical_not(first))
    def _():
        fill(other_ref)


def feed_kernel(count, place_ref, cot_ref, own_ref, other_ref, *refs):
    rows_in, refs = refs[: 5 * count], refs[5 * count :]
    grads_out, (rows_ref, down_ref, act_ref, pre_ref, up_ref, sum_ref) = (
        refs[: 5 * count],
        refs[5 * count :],
    )
    step = pl.program_id(0)
    half = up_ref.shape[0]
    shard_len = rows_ref.shape[1] // count
    part = shard_len // 2
    ctx, mine = place_ref[0], place_ref[2]

    for turn_of, at in ((0, 0), (1, LEVELS)):

        @pl.when(step == at)
        def _(turn_of=turn_of):
            stack_units(ctx == turn_of, own_ref, other_ref, 0, up_ref)
            stack_units(ctx == turn_of, own_ref, other_ref, 1, down_ref.at[0])

    for k in range(LEVELS):

        @pl.when((step < LEVELS) & (jnp.bitwise_xor(mine, k) == step))
        def _(k=k):
            for i in range(count):
                pieces = rows_in[5 * i : 5 * i + 5]
                rows = slice(i * shard_len, (i + 1) * shard_len)
                if k < LEVELS - 1:
                    rows_ref[0, rows] = pieces[k][...]
                else:
                    rows_ref[0, rows.start : rows.start + part] = pieces[3][...]
                    rows_ref[0, rows.start + part : rows.stop] = pieces[4][...]

    def run(used):
        upped = contract(rows_ref[0], up_ref[:used], 1, 1)
        activated, slope = gelu_both(upped)
        grad_act = contract(cot_ref[0], down_ref[0, :used], 1, 1)
        grad_upped = (grad_act * slope).astype(BF)
        act_ref[0, :, :used] = activated.astype(BF)
        pre_ref[0, :, :used] = grad_upped
        return contract(grad_upped, up_ref[:used], 1, 0)

    for one in range(LEVELS - 2):

        @pl.when(step == one)
        def _(one=one):
            sum_ref[...] = run(half // 2 ** (LEVELS - 2 - one))

    @pl.when(step >= LEVELS - 2)
    def _():
        result = run(half)

        @pl.when(step < LEVELS)
        def _():
            sum_ref[...] = result

        @pl.when(step == LEVELS)
        def _():
            sum_ref[...] += result

    level = jnp.minimum(step, LEVELS - 1)
    for k in range(LEVELS):

        @pl.when((step != LEVELS - 1) & (jnp.bitwise_xor(mine, k) == level))
        def _(k=k):
            for i in range(count):
                keep, keep_x, keep_y, send_x, send_y = grads_out[5 * i : 5 * i + 5]
                first = sum_ref[i * shard_len : i * shard_len + part].astype(BF)
                second = sum_ref[i * shard_len + part : (i + 1) * shard_len].astype(BF)
                if k == 0:
                    keep[:part] = first
                    keep[part:] = second
                elif k == 1:
                    send_x[0] = first
                    keep_x[...] = second
                elif k == 2:
                    keep_y[...] = first
                    send_y[0] = second
                else:
                    send_x[1] = first
                    send_y[1] = second


def feed(place, rows, cot, own, other):
    count = len(rows)
    _, length, width = cot.shape
    half = own.shape[0] * own.shape[2] * own.shape[3]
    shard_len = length // count
    part = shard_len // 2
    whole = lambda shape: pl.BlockSpec(
        shape, lambda s, p: (0,) * len(shape), pipeline_mode=pl.Buffered(1)
    )
    fixed = lambda shape: pl.BlockSpec(shape, lambda s, p: (0,) * len(shape))
    by_level = pl.BlockSpec((1, length, width), lambda s, p: (jnp.minimum(s, LEVELS - 1), 0, 0))
    by_half = pl.BlockSpec((1, half, width), lambda s, p: (s // LEVELS, 0, 0))
    by_step = pl.BlockSpec((1, length, half), lambda s, p: (s, 0, 0))
    pieces = [
        (shard_len, width),
        (part, width),
        (part, width),
        (2, part, width),
        (2, part, width),
    ]
    *grads, rows_all, down, activated, before = pl.pallas_call(
        functools.partial(feed_kernel, count),
        grid_spec=pltpu.PrefetchScalarGridSpec(
            num_scalar_prefetch=1,
            grid=(LEVELS + 1,),
            in_specs=[by_level, whole(own.shape), whole(own.shape)]
            + [whole(piece.shape) for one in rows for piece in one],
            out_specs=[fixed(shape) for shape in pieces] * count
            + [by_level, by_half, by_step, by_step],
            scratch_shapes=[pltpu.VMEM((half, width), BF), pltpu.VMEM((length, width), F32)],
        ),
        out_shape=[jax.ShapeDtypeStruct(shape, BF) for shape in pieces] * count
        + [
            jax.ShapeDtypeStruct(cot.shape, BF),
            jax.ShapeDtypeStruct((2, half, width), BF),
            jax.ShapeDtypeStruct((LEVELS + 1, length, half), BF),
            jax.ShapeDtypeStruct((LEVELS + 1, length, half), BF),
        ],
        compiler_params=pltpu.CompilerParams(vmem_limit_bytes=58 * MIB),
        cost_estimate=cost(
            flops=24 * length * width * half,
            bytes_accessed=24 * length * width + 8 * half * width + 20 * length * half,
            transcendentals=5 * length * half,
        ),
        name="feed",
    )(place, cot, own, other, *[piece for one in rows for piece in one])
    grads = [grads[5 * i : 5 * i + 5] for i in range(count)]
    return grads, rows_all, down, activated, before


def feed_weights_kernel(
    place_ref,
    rows_ref,
    cot_ref,
    act_ref,
    pre_ref,
    down_ref,
    keep_ref,
    send_ref,
    out_ref,
    up_sum,
    down_sum,
    out_sum,
    stage,
    sem,
):
    step = pl.program_id(0)
    half = down_ref.shape[1]
    ranks, _, blocks, sub, _ = stage.shape

    def add(used, fresh):
        up_part = contract(pre_ref[0, :, :used], rows_ref[0], 0, 0)
        down_part = contract(act_ref[0, :, :used], cot_ref[0], 0, 0)
        if fresh == used:
            up_sum[:used] = up_part
            down_sum[:used] = down_part
        else:
            up_sum[:fresh] += up_part[:fresh]
            down_sum[:fresh] += down_part[:fresh]
            if fresh < used:
                up_sum[fresh:used] = up_part[fresh:]
                down_sum[fresh:used] = down_part[fresh:]
        return contract(act_ref[0, :, :used], down_ref[0, :used], 1, 0)

    def store(which):
        for block in range(blocks):
            for rank in range(ranks):
                first = (block * ranks + rank) * sub
                stage[rank, 0, block] = up_sum[first : first + sub].astype(BF)
                stage[rank, 1, block] = down_sum[first : first + sub].astype(BF)

        @pl.when(place_ref[0] == which)
        def _():
            copy = pltpu.make_async_copy(stage, keep_ref, sem)
            copy.start()
            copy.wait()

        @pl.when(place_ref[0] != which)
        def _():
            copy = pltpu.make_async_copy(stage, send_ref, sem)
            copy.start()
            copy.wait()

    for one in range(LEVELS - 1):

        @pl.when(step == one)
        def _(one=one):
            used = half // 2 ** (LEVELS - 2 - one)
            out_ref[0] = add(used, used if one == 0 else used // 2).astype(BF)

    @pl.when(step == LEVELS - 1)
    def _():
        up_sum[...] += contract(pre_ref[0], rows_ref[0], 0, 0)
        down_sum[...] += contract(act_ref[0], cot_ref[0], 0, 0)
        out_sum[...] = contract(act_ref[0], down_ref[0], 1, 0)
        store(0)

    @pl.when(step == LEVELS)
    def _():
        out_ref[0] = (out_sum[...] + add(half, half)).astype(BF)
        store(1)


def feed_weights(place, rows, cot, activated, before, down, ranks, blocks):
    _, length, width = rows.shape
    half = down.shape[1]
    sub = half // (ranks * blocks)
    by_level = pl.BlockSpec((1, length, width), lambda s, p: (jnp.minimum(s, LEVELS - 1), 0, 0))
    by_half = pl.BlockSpec((1, half, width), lambda s, p: (s // LEVELS, 0, 0))
    by_step = pl.BlockSpec((1, length, half), lambda s, p: (s, 0, 0))
    shape = (ranks, 2, blocks, sub, width)
    return pl.pallas_call(
        feed_weights_kernel,
        grid_spec=pltpu.PrefetchScalarGridSpec(
            num_scalar_prefetch=1,
            grid=(LEVELS + 1,),
            in_specs=[by_level, by_level, by_step, by_step, by_half],
            out_specs=[
                pl.BlockSpec(memory_space=pl.ANY),
                pl.BlockSpec(memory_space=pl.ANY),
                by_level,
            ],
            scratch_shapes=[
                pltpu.VMEM((half, width), F32),
                pltpu.VMEM((half, width), F32),
                pltpu.VMEM((length, width), F32),
                pltpu.VMEM(shape, BF),
                pltpu.SemaphoreType.DMA(()),
            ],
        ),
        out_shape=[
            jax.ShapeDtypeStruct(shape, BF),
            jax.ShapeDtypeStruct(shape, BF),
            jax.ShapeDtypeStruct(rows.shape, BF),
        ],
        compiler_params=pltpu.CompilerParams(vmem_limit_bytes=56 * MIB),
        cost_estimate=cost(
            flops=24 * length * width * half,
            bytes_accessed=24 * length * width + 12 * half * width + 20 * length * half,
            transcendentals=0,
        ),
        name="feed_weights",
    )(place, rows, cot, activated, before, down)


def outer_kernel(count, *refs):
    lefts, rights, out_ref = refs[:count], refs[count : 2 * count], refs[-1]
    total = contract(lefts[0][...], rights[0][...], 0, 0)
    for left, right in zip(lefts[1:], rights[1:]):
        total = total + contract(left[...], right[...], 0, 0)
    out_ref[...] = total.astype(BF)


def outer(lefts, rights):
    rows, m = lefts[0].shape
    n = rights[0].shape[1]
    count = len(lefts)
    step = m // 4
    return pl.pallas_call(
        functools.partial(outer_kernel, count),
        grid=(4,),
        in_specs=[pl.BlockSpec((rows, step), lambda j: (0, j))] * count
        + [pl.BlockSpec((rows, n), lambda j: (0, 0))] * count,
        out_specs=pl.BlockSpec((step, n), lambda j: (j, 0)),
        out_shape=jax.ShapeDtypeStruct((m, n), BF),
        compiler_params=pltpu.CompilerParams(vmem_limit_bytes=32 * MIB),
        cost_estimate=cost(
            flops=2 * count * rows * m * n,
            bytes_accessed=2 * (count * rows * (m + n) + m * n),
            transcendentals=0,
        ),
        name="outer",
    )(*lefts, *rights)


def inverse_rms(values):
    return lax.rsqrt(jnp.mean(values * values, axis=-1, keepdims=True) + EPSILON)


def norm_back(values, inv_rms, weighted):
    return inv_rms * weighted - values * (inv_rms * inv_rms * inv_rms) * jnp.mean(
        weighted * values, axis=-1, keepdims=True
    )


def rotation(positions, head_size):
    half_size = head_size // 2
    frequency = 10000.0 ** (-jnp.arange(half_size, dtype=jnp.float32) / half_size)
    angles = positions.astype(jnp.float32)[:, None] * frequency[None, :]
    cosine, sine = jnp.cos(angles), jnp.sin(angles)
    cosine = jnp.concatenate([cosine, cosine], -1)
    sine = jnp.concatenate([-sine, sine], -1)
    return (
        jnp.stack([cosine, jnp.ones_like(cosine)]),
        jnp.stack([sine, jnp.zeros_like(sine)]),
    )


def product(equation, left, right):
    return jnp.einsum(equation, left, right, preferred_element_type=F32)


def local(inputs, w_query, w_key, w_value, w_out, w_up, w_down, gain_attn, gain_ffn, cotangent):
    count, shard_len, width = inputs.shape
    own_rows = count * shard_len
    ranks = lax.axis_size("mp")
    length_half = shard_len * ranks
    level = lax.axis_index("dp") % LEVELS
    ctx = lax.axis_index("ctx")
    rank = lax.axis_index("mp")
    part_rows, head_cols = w_query.shape
    place = jnp.stack([ctx, rank, level]).astype(jnp.int32)

    inputs_flat = inputs.reshape(own_rows, width)
    cot_flat = cotangent.reshape(own_rows, width)
    rows_all = lax.all_gather(inputs_flat, "mp", axis=0)
    out_found = [turn(w_out, "mp", k) for k in range(1, ranks)]

    gains = team_gather(level_gather_small(jnp.stack([gain_attn, gain_ffn]), level))
    gains = pair_gather(gains.reshape(-1, 2, part_rows), ctx, 1)
    gains = gains.transpose(2, 0, 1, 3).reshape(2, 1, width).astype(F32)
    gain_first, gain_second = gains[0], gains[1]

    qkv_full = model_gather(
        after(jnp.concatenate([w_query, w_key, w_value], axis=1), *out_found), level, ctx
    )
    blocks, unit_cols = w_up.shape[1:]
    sub = unit_cols // LEVELS
    half_blocks = blocks // 2
    up_turned = w_up.transpose(1, 2, 0)
    halves = [
        jnp.stack([up_turned[b : b + half_blocks], w_down[b : b + half_blocks]])
        for b in (0, half_blocks)
    ]
    own_part, sent_part = pair_split(halves[0], halves[1], ctx)
    pair = jnp.concatenate(
        [jnp.where(ctx == 0, own_part, sent_part), jnp.where(ctx == 0, sent_part, own_part)], -1
    )
    pair = pair.reshape(2, half_blocks, LEVELS, sub, 2 * part_rows).transpose(2, 0, 1, 3, 4)
    swapped = team_gather(level_swap(pair, level))
    swapped = side_by_side(swapped.reshape(-1, 2, half_blocks, sub, 2 * part_rows))
    cot_pieces = level_pieces(after(cot_flat, swapped))
    ranked = lax.all_gather(swapped, "mp", axis=0)
    positions = ctx * length_half + jnp.arange(length_half, dtype=jnp.int32)
    cosine, sine = rotation(positions, HEAD)
    qkv, normed = project(
        count, shard_len, rows_all, after(gain_first, *cot_pieces), qkv_full, cosine, sine
    )
    cot_rows = level_join(after(cot_pieces, qkv), level)
    out_parts = put(jnp.zeros((ranks,) + w_out.shape, BF), w_out, rank)
    for k in range(1, ranks):
        out_parts = put(out_parts, out_found[k - 1], (rank + ranks - k) % ranks)
    out_parts = after(out_parts.reshape(-1, part_rows).T, cot_pieces[3])
    out_full = model_gather(out_parts, level, ctx)
    early = lax.ppermute(qkv[1:], "ctx", [(0, 1)])
    parts, logs = attend(place, ranks, length_half, qkv, early)
    hidden, normed_two, mixed_own = finish_attention(
        place, inputs_flat, gain_second, out_full, rank_swap(parts)
    )

    ranked = after(ranked, hidden)
    (opened,), rows_second, down_mine, activated, before = feed(
        place, [level_pieces(normed_two)], cot_rows, ranked, flip(ranked, "ctx", 1)
    )
    own, by_x, by_y, got_x, got_y = opened
    got_x, got_y = flip(got_x, "dp", 1), flip(got_y, "dp", 2)

    grad_kept, grad_sent, results = feed_weights(
        place, rows_second, cot_rows, activated, before, down_mine, ranks, half_blocks
    )
    grad_sent = after(grad_sent, got_x, got_y)
    grad_ffn = (grad_kept.astype(F32) + flip(grad_sent, "ctx", 1).astype(F32)).astype(BF)
    grad_ffn_low = [grad_ffn[:, kind].reshape(-1, width) for kind in range(2)]
    grad_ffn = [
        lax.psum_scatter(one, "mp", scatter_dimension=0, tiled=True) for one in grad_ffn_low
    ]

    last_y, last_x = level_scatter_last(by_x, by_y, got_x, got_y)
    own = after(own, *grad_ffn_low)
    grad_hidden, grad_low, parts = begin_back(
        place, ranks, (own, got_x, last_y, got_y, last_x), hidden, cot_flat, gain_second, out_full
    )
    parts = rank_swap(parts)
    grad_query, grad_own, grad_early = attend_back(
        place, length_half, qkv, early, logs, parts, cosine, sine
    )
    grad_early = after(grad_early, grad_ffn[0])
    back = lax.ppermute(grad_early, "ctx", [(1, 0)])
    grad_qkv, grad_first = project_back(
        count, ranks, grad_query, grad_own, back, cosine, sine, qkv_full
    )
    grad_first = after(grad_first, grad_ffn[1])
    grad_ffn = after(grad_ffn, grad_first)
    grad_first = lax.psum_scatter(
        grad_first.reshape(-1, width), "mp", scatter_dimension=0, tiled=True
    )

    results_open = after(level_scatter_open(after(results, grad_low), level), grad_qkv)
    result = level_sum(results_open, level_scatter_last(*results_open[1:]))
    outputs = (hidden + result).astype(BF).reshape(inputs.shape)

    grad_ffn = jnp.stack(grad_ffn).reshape(2, half_blocks, sub, width)
    grad_ffn = jnp.stack(jnp.split(grad_ffn, width // (2 * part_rows), axis=-1))
    grad_ffn = team_scatter(grad_ffn.reshape((-1, LEVELS) + grad_ffn.shape[1:]))
    grad_ffn = level_swap(grad_ffn, level).transpose(1, 2, 0, 3, 4)
    grad_ffn = grad_ffn.reshape(2, half_blocks, unit_cols, 2 * part_rows)
    own_part, sent_part = pair_split(grad_ffn[..., :part_rows], grad_ffn[..., part_rows:], ctx)
    grad_ffn = jnp.concatenate(
        [jnp.where(ctx == 0, own_part, sent_part), jnp.where(ctx == 0, sent_part, own_part)], 1
    ).astype(F32)
    grad_up_out = grad_ffn[0].transpose(2, 0, 1)
    grad_down_out = grad_ffn[1]
    gain_ffn_part = jnp.sum(grad_up_out * w_up.astype(F32), axis=(1, 2)) / gain_ffn.astype(F32)

    grad_qkv_w = outer([normed], [grad_qkv])
    grad_qkv_w = model_scatter(grad_qkv_w, level, ctx, part_rows)
    originals = jnp.concatenate([w_query, w_key, w_value], axis=1).astype(F32)
    gain_attn_part = jnp.sum(grad_qkv_w * originals, axis=1) / gain_attn.astype(F32)
    gain_grads = jnp.stack([gain_attn_part, gain_ffn_part])
    gain_grads = gain_grads + sum([turn(gain_grads, "mp", k) for k in range(1, ranks)])

    grad_out_w = outer([after(grad_low, grad_qkv)], [mixed_own])
    grad_out_w = model_scatter(grad_out_w, level, ctx, part_rows).astype(BF)
    grad_out_w = jnp.stack(jnp.split(grad_out_w, ranks, axis=1))
    grad_out_out = take(grad_out_w, rank).astype(F32)
    for k in range(1, ranks):
        grad_out_out = grad_out_out + turn(take(grad_out_w, (rank + k) % ranks), "mp", k).astype(F32)
    grad_out_out = grad_out_out.T

    grad_first = after(grad_first, grad_out_out, gain_grads, outputs, grad_qkv_w, grad_up_out, grad_down_out)
    inputs_f = inputs.astype(F32)
    input_grads = grad_hidden.reshape(inputs.shape) + norm_back(
        inputs_f,
        inverse_rms(inputs_f),
        gain_first * grad_first.reshape(inputs.shape).astype(F32),
    )
    return (
        outputs,
        input_grads,
        grad_qkv_w[:, :head_cols],
        grad_qkv_w[:, head_cols : 2 * head_cols],
        grad_qkv_w[:, 2 * head_cols :],
        grad_out_out,
        grad_up_out,
        grad_down_out,
        gain_grads[0],
        gain_grads[1],
    )


def solution(mesh):
    in_specs = (
        P("dp", ("ctx", "mp"), None),
        P(("dp", "ctx"), "mp"),
        P(("dp", "ctx"), "mp"),
        P(("dp", "ctx"), "mp"),
        P("mp", ("dp", "ctx")),
        P(("dp", "ctx"), None, "mp"),
        P(None, "mp", ("dp", "ctx")),
        P(("dp", "ctx")),
        P(("dp", "ctx")),
        P("dp", ("ctx", "mp"), None),
    )
    out_specs = (
        P("dp", ("ctx", "mp"), None),
        P("dp", ("ctx", "mp"), None),
        P(("dp", "ctx"), "mp"),
        P(("dp", "ctx"), "mp"),
        P(("dp", "ctx"), "mp"),
        P("mp", ("dp", "ctx")),
        P(("dp", "ctx"), None, "mp"),
        P(None, "mp", ("dp", "ctx")),
        P(("dp", "ctx")),
        P(("dp", "ctx")),
    )
    return jax.shard_map(local, mesh=mesh, in_specs=in_specs, out_specs=out_specs, check_vma=False)
```
